512 devices in a mesh: ens: 16 (over x_lo, y), lat: 32 (over z, x_hi, core).
Axes of the slice: x: 4 (x_hi: 2, x_lo: 2; x = x_hi * 2 + x_lo), y: 8, z: 8, core: 2. Of those that a mesh axis runs over, the one named last changes fastest.
Arguments:
- latent_fields: bfloat16 [16, 96, 256, 128], P('ens', 'lat'), may hold values from -6 to 6
- target_fields: bfloat16 [96, 72, 128], P('lat'), may hold values from -9 to 9
- filters: bfloat16 [3, 256, 256], replicated, may hold values from -0.375 to 0.375
- decoder: bfloat16 [256, 72], replicated, may hold values from -0.375 to 0.375
- cycle_basis: float32 [96, 3, 10], replicated, may hold values from -1.8 to 1.8
- cycle_offsets: int32 [96, 10], replicated, may hold values from -8 to 8
Outputs:
- latent_grad: bfloat16 [16, 96, 256, 128], P('ens', 'lat')
- filter_grad: float32 [256, 3, 256], P('lat', None, 'ens')
The draws below stay inside these ranges and needn't reach their ends.
Inputs may be any that keep to these rules, and one draw needn't show every extreme that they name: `cycle_offsets`: a tap's longitude offset is the same for every longitude of its cycle.
All inputs are finite; a program needn't handle non-finite values.
Results may differ from the reference program's by a relative error of at most 0.022.
Values may be sent and summed in bfloat16 or wider, within the bound.
No kernel may reach another device: no remote copies, remote signals or barrier semaphores. Data moves between devices by JAX's collectives and lax.ppermute only.
A program may use at most 64 MiB of HBM per device.

```python
import jax
import jax.numpy as jnp
from jax import lax

C = 256
V = 72
K = 3
HALO = 2
SIDE = 2
LSPAN = 8
NLON = 128
TAPS = 10
MEMBERS = 16
NLAT = 96


def touch_ends(values, own_key, smallest, top_value):
    spot = [jax.random.randint(jax.random.fold_in(own_key, axis), (), 0, length) for axis, length in enumerate(values.shape)]
    main_axis = values.shape.index(max(values.shape))
    neighbour = spot[:main_axis] + [(spot[main_axis] + 1) % values.shape[main_axis]] + spot[main_axis + 1:]
    return values.at[tuple(spot)].set(smallest).at[tuple(neighbour)].set(top_value)


def block_levels(own_key, dims, shards, least, top_value):
    factor_of = 1.0
    for position, parts in shards:
        draws = jax.random.uniform(jax.random.fold_in(jax.random.fold_in(own_key, 6), position), (parts,), jnp.float32, least / len(shards), top_value / len(shards))
        factor_of = factor_of * jnp.repeat(jnp.exp(draws), dims[position] // parts).reshape((-1,) + (1,) * (len(dims) - 1 - position))
    return factor_of


def bell_draw(stream_key, extent, deviation, most, split=(), held_as=jnp.bfloat16):
    result = deviation * jax.random.normal(stream_key, extent, jnp.float32)
    if split:
        result = result * block_levels(stream_key, extent, split, -0.22, 0.18)
    return jnp.clip(result, -most, most).astype(held_as)


def setup_inputs(seed: int = 0) -> dict:
    key_list = jax.random.split(jax.random.key(seed), 7)
    latent_fields = bell_draw(key_list[0], (MEMBERS, NLAT, C, NLON), 1.0, 6.0, ((0, 16), (1, 32)))
    target_fields = bell_draw(key_list[1], (NLAT, V, NLON), 1.5, 9.0, ((0, 32),))
    filters = bell_draw(key_list[2], (K, C, C), C ** -0.5, 0.375)
    decoder = bell_draw(key_list[3], (C, V), C ** -0.5, 0.375)
    cycle_basis = bell_draw(key_list[4], (NLAT, K, TAPS), 0.3, 1.8, (), jnp.float32)
    cycle_offsets = touch_ends(jax.random.randint(key_list[5], (NLAT, TAPS), 0 - LSPAN, LSPAN + 1), jax.random.fold_in(key_list[5], 1), 0 - LSPAN, LSPAN).astype(jnp.int32)
    return dict(latent_fields=latent_fields, target_fields=target_fields, filters=filters, decoder=decoder, cycle_basis=cycle_basis, cycle_offsets=cycle_offsets)


DELTA = 0.25

def smooth_slope(differ):
    return differ / jnp.sqrt(differ * differ + DELTA * DELTA)

def reference(latent_fields, target_fields, filters, decoder, cycle_basis, cycle_offsets):
    longitude = jnp.arange(NLON, dtype=jnp.int32)
    filter_wide = filters.astype(jnp.float32)
    decoder_wide = decoder.astype(jnp.float32)
    basis_padded = jnp.pad(cycle_basis, ((HALO, HALO), (0, 0), (0, 0)))
    offsets_padded = jnp.pad(cycle_offsets, ((HALO, HALO), (0, 0)))

    def forward(member_field):
        projected = jnp.einsum('icj,kcd->ikdj', member_field.astype(jnp.float32), filter_wide).astype(jnp.bfloat16)
        padded = jnp.pad(projected, ((HALO, HALO), (0, 0), (0, 0), (0, 0)))
        conv_out = jnp.zeros((NLAT, C, NLON), jnp.float32)
        for tap_index in range(TAPS):
            row_step = tap_index // SIDE - HALO
            source = padded[HALO + row_step:HALO + row_step + NLAT]
            lookup = (longitude[None, :] + cycle_offsets[:, tap_index][:, None]) % NLON
            moved = jnp.take_along_axis(source, lookup[:, None, None, :], axis=3)
            conv_out = conv_out + lax.optimization_barrier(jnp.sum(cycle_basis[:, :, tap_index][:, :, None, None] * moved.astype(jnp.float32), axis=1))
        hidden = (member_field.astype(jnp.float32) + conv_out).astype(jnp.bfloat16)
        return jnp.einsum('icj,cv->ivj', hidden.astype(jnp.float32), decoder_wide)
    predicted = lax.map(forward, latent_fields)
    rounded = lax.optimization_barrier(predicted.astype(jnp.bfloat16)).astype(jnp.float32)

    def member_pairs(member_pred):
        return lax.optimization_barrier(jnp.sum(smooth_slope(member_pred[None] - rounded), axis=0))
    pair_sum = lax.map(member_pairs, rounded)
    latitude = jnp.pi * (jnp.arange(NLAT, dtype=jnp.float32) + 0.5) / NLAT - jnp.pi / 2
    area = jnp.cos(latitude)
    pred_grad = area[None, :, None, None] * (smooth_slope(predicted - target_fields.astype(jnp.float32)[None]) - pair_sum / (MEMBERS - 1))
    pred_grad = pred_grad.astype(jnp.bfloat16)

    def backward(running, inputs):
        member_field, member_grad = inputs
        grad_hidden = jnp.einsum('ivj,cv->icj', member_grad.astype(jnp.float32), decoder_wide).astype(jnp.bfloat16)
        padded = jnp.pad(grad_hidden, ((HALO, HALO), (0, 0), (0, 0)))
        adjoint = jnp.zeros((NLAT, K, C, NLON), jnp.float32)
        for tap_index in range(TAPS):
            row_step = tap_index // SIDE - HALO
            start = HALO - row_step
            source = padded[start:start + NLAT]
            weights = basis_padded[start:start + NLAT, :, tap_index]
            shifts = offsets_padded[start:start + NLAT, tap_index]
            lookup = (longitude[None, :] - shifts[:, None]) % NLON
            moved = jnp.take_along_axis(source, lookup[:, None, :], axis=2)
            adjoint = adjoint + weights[:, :, None, None] * moved.astype(jnp.float32)[:, None]
        adjoint = adjoint.astype(jnp.bfloat16)
        latent_grad = (grad_hidden.astype(jnp.float32) + jnp.einsum('ikdj,kcd->icj', adjoint.astype(jnp.float32), filter_wide)).astype(jnp.bfloat16)
        running = running + jnp.einsum('icj,ikdj->ckd', member_field.astype(jnp.float32), adjoint.astype(jnp.float32))
        return (running, latent_grad)
    total, latent_grad = lax.scan(backward, jnp.zeros((C, K, C), jnp.float32), (latent_fields, pred_grad))
    factor = 1.0 / jnp.sqrt(jnp.float32(MEMBERS * NLAT * NLON))
    return (latent_grad, total * factor)
```

```python
import functools
import math

import jax
import jax.numpy as jnp
import numpy as np
from jax import lax
from jax.experimental import pallas as pl
from jax.experimental.pallas import tpu as pltpu
from jax.sharding import PartitionSpec as P

HALO = 2
SIDE = 2
REACH = 2 * HALO + 1
DELTA = 0.25
BF = jnp.bfloat16
F32 = jnp.float32
VMEM = pl.BlockSpec(memory_space=pltpu.VMEM)
SMEM = pl.BlockSpec(memory_space=pltpu.SMEM)


def smooth_slope(differ):
    return differ * lax.rsqrt(differ * differ + DELTA * DELTA)


def dot_nn(a, b):
    return lax.dot_general(a, b, (((1,), (0,)), ((), ())), preferred_element_type=F32)


def dot_nt(a, b):
    return lax.dot_general(a, b, (((1,), (1,)), ((), ())), preferred_element_type=F32)


def call(kernel, out, specs, flops, moved):
    many = isinstance(out, (tuple, list))
    return pl.pallas_call(
        kernel,
        out_shape=out,
        in_specs=specs,
        out_specs=tuple([VMEM] * len(out)) if many else VMEM,
        compiler_params=pltpu.CompilerParams(vmem_limit_bytes=32 * 2**20),
        cost_estimate=pl.CostEstimate(flops=flops, bytes_accessed=moved, transcendentals=0),
    )


def prepare(rows, kernels, taps, lat_count, first, basis, offsets, filters, dec_t, dec_p, ahead, back, w_fwd, w_bwd):
    lon = ahead.shape[1] // REACH
    chan = filters.shape[1]
    base = first[0]
    lag = (lax.broadcasted_iota(jnp.int32, (lon, lon), 0) - lax.broadcasted_iota(jnp.int32, (lon, lon), 1)) & (lon - 1)

    def block(out, row, source, slot, step, sign):
        cycle = base + source
        inside = jnp.logical_and(cycle >= 0, cycle < lat_count)
        cycle = jnp.clip(cycle, 0, lat_count - 1)
        one, two = SIDE * step, SIDE * step + 1
        off_one, off_two = offsets[cycle, one], offsets[cycle, two]
        mask_one = lag == ((sign * off_one) & (lon - 1))
        mask_two = lag == ((sign * off_two) & (lon - 1))
        for k in range(kernels):
            weight_one = jnp.where(inside, basis[cycle, k * taps + one], 0.0)
            weight_two = jnp.where(inside, basis[cycle, k * taps + two], 0.0)
            weight_two = weight_two + jnp.where(off_one == off_two, weight_one, 0.0)
            value = jnp.where(mask_two, weight_two, jnp.where(mask_one, weight_one, 0.0))
            out[row, slot * lon : (slot + 1) * lon, k * lon : (k + 1) * lon] = value.astype(BF)

    for row in range(rows):
        for slot in range(REACH):
            block(ahead, row, row, slot, slot, 1)
            block(back, row, row + slot - HALO, slot, REACH - 1 - slot, -1)
    w_fwd[:, :chan] = dec_t[...]
    w_bwd[0] = dec_p[...]
    for k in range(kernels):
        w_fwd[:, (k + 1) * chan : (k + 2) * chan] = dot_nt(dec_t[...], filters[k]).astype(BF)
        w_bwd[k + 1] = dot_nn(filters[k], dec_p[...]).astype(BF)


def forward(rows, kernels, field, low, high, ahead, w_fwd, packed, predicted, mixed):
    lon = field.shape[2]
    chan = field.shape[1]
    wide = [low[0], low[1]] + [field[i] for i in range(rows)] + [high[0], high[1]]
    per = packed.shape[1]
    padded = predicted.shape[1]
    pieces = padded // per
    for i in range(rows):
        source = jnp.concatenate(wide[i : i + REACH], axis=1)
        taps = dot_nn(source, ahead[i]).astype(BF)
        for k in range(kernels):
            mixed[i, k * chan : (k + 1) * chan, :] = taps[:, k * lon : (k + 1) * lon]
        stack = jnp.concatenate([wide[i + HALO]] + [taps[:, k * lon : (k + 1) * lon] for k in range(kernels)], axis=0)
        pred = dot_nn(w_fwd[...], stack)
        predicted[i] = pred
        rounded = pred.astype(BF)
        for q in range(pieces):
            packed[i * pieces + q] = rounded[q * per : (q + 1) * per]
    for q in range(rows * pieces, packed.shape[0]):
        packed[q] = jnp.zeros(packed.shape[1:], BF)


def pairs(visitors, sums):
    members, height, _ = visitors.shape
    for start in range(0, height, 8):
        values = [visitors[m].astype(F32)[start : start + 8] for m in range(members)]
        totals = [None] * members
        for m in range(members):
            for n in range(m + 1, members):
                slope = smooth_slope(values[m] - values[n])
                totals[m] = slope if totals[m] is None else totals[m] + slope
                totals[n] = -slope if totals[n] is None else totals[n] - slope
        for m in range(members):
            sums[m, start : start + 8, :] = totals[m]


def gradient(rows, kernels, members, first, area, sums, predicted, target, mixed, pred_grad, partial):
    variables = target.shape[1]
    padded = predicted.shape[1]
    per = sums.shape[1]
    pieces = padded // per
    lon = predicted.shape[2]
    chan = mixed.shape[1] // kernels
    grads = []
    for i in range(rows):
        pair_sum = jnp.concatenate([sums[i * pieces + q] for q in range(pieces)], axis=0)
        aim = jnp.concatenate([target[i].astype(F32), jnp.zeros((padded - variables, lon), F32)], axis=0)
        grad = area[first[0] + i] * (smooth_slope(predicted[i] - aim) - pair_sum * (1.0 / (members - 1)))
        grad = grad.astype(BF)
        pred_grad[i] = grad
        grads.append(jnp.concatenate([grad, jnp.zeros((lon - padded, lon), BF)], axis=0))
    total = dot_nt(
        jnp.concatenate([mixed[i] for i in range(rows)], axis=1), jnp.concatenate(grads, axis=1)
    )
    owners = partial.shape[0]
    own = chan // owners
    for owner in range(owners):
        partial[owner] = jnp.concatenate(
            [total[k * chan + owner * own : k * chan + (owner + 1) * own] for k in range(kernels)], axis=0
        ).astype(BF)


def band_sum(factor, parts, dec_wide, spread):
    owners, height, lanes = parts.shape
    total = parts[0].astype(F32)
    for owner in range(1, owners):
        total = total + parts[owner].astype(F32)
    total = jnp.concatenate([total * factor, jnp.zeros((lanes - height, lanes), F32)], axis=0)
    upper = total.astype(BF)
    lower = (total - upper.astype(F32)).astype(BF)
    result = dot_nt(dec_wide[...], upper) + dot_nt(dec_wide[...], lower)
    per = spread.shape[1]
    for member in range(spread.shape[0]):
        spread[member] = result[member * per : (member + 1) * per]


def member_sum(parts, owned):
    own, kernels, width = owned.shape
    total = parts[0]
    for member in range(1, parts.shape[0]):
        total = total + parts[member]
    turned = total.T
    for k in range(kernels):
        owned[:, k, :] = turned[k * own : (k + 1) * own]


def adjoint(rows, kernels, pred_grad, low, high, back, w_bwd, result):
    lon = pred_grad.shape[2]
    wide = [low[0], low[1]] + [pred_grad[i] for i in range(rows)] + [high[0], high[1]]
    for i in range(rows):
        taps = dot_nn(jnp.concatenate(wide[i : i + REACH], axis=1), back[i]).astype(BF)
        total = dot_nn(w_bwd[0], wide[i + HALO])
        for k in range(kernels):
            total = total + dot_nn(w_bwd[k + 1], taps[:, k * lon : (k + 1) * lon])
        result[i] = total.astype(BF)


def halos(block, axis):
    count = lax.axis_size(axis)
    up = [(i, i + 1) for i in range(count - 1)]
    down = [(target, source) for source, target in up]
    return lax.ppermute(block[-HALO:], axis, up), lax.ppermute(block[:HALO], axis, down)


def body(latent_fields, target_fields, filters, decoder, cycle_basis, cycle_offsets):
    field = latent_fields[0]
    rows, chan, lon = field.shape
    lat_count, kernels, taps = cycle_basis.shape
    variables = decoder.shape[1]
    members, bands = lax.axis_size("ens"), lax.axis_size("lat")
    per = 16
    padded = -(-variables // per) * per
    first = (lax.axis_index("lat") * rows).astype(jnp.int32).reshape(1)
    area = jnp.asarray(np.cos(np.pi * (np.arange(lat_count) + 0.5) / lat_count - np.pi / 2), F32)
    dec_p = jnp.pad(decoder, ((0, 0), (0, padded - variables)))
    dec_wide = jnp.pad(decoder, ((0, 0), (0, lon - variables)))

    low, high = halos(field, "lat")
    ahead, back, w_fwd, w_bwd = call(
        functools.partial(prepare, rows, kernels, taps, lat_count),
        (
            jax.ShapeDtypeStruct((rows, REACH * lon, kernels * lon), BF),
            jax.ShapeDtypeStruct((rows, REACH * lon, kernels * lon), BF),
            jax.ShapeDtypeStruct((padded, (kernels + 1) * chan), BF),
            jax.ShapeDtypeStruct((kernels + 1, chan, padded), BF),
        ),
        [SMEM, SMEM, SMEM, VMEM, VMEM, VMEM],
        60_000_000,
        4_000_000,
    )(first, cycle_basis.reshape(lat_count, kernels * taps), cycle_offsets, filters, dec_p.T, dec_p)
    packed, predicted, mixed = call(
        functools.partial(forward, rows, kernels),
        (
            jax.ShapeDtypeStruct((members, per, lon), BF),
            jax.ShapeDtypeStruct((rows, padded, lon), F32),
            jax.ShapeDtypeStruct((rows, kernels * chan, lon), BF),
        ),
        [VMEM] * 5,
        450_000_000,
        3_000_000,
    )(field, low, high, ahead, w_fwd)
    visitors = lax.all_to_all(packed, "ens", 0, 0, tiled=True)
    sums = call(pairs, jax.ShapeDtypeStruct((members, per, lon), F32), [VMEM], 2_000_000, 200_000)(visitors)
    sums = lax.all_to_all(sums, "ens", 0, 0, tiled=True)
    own = chan // bands
    pred_grad, partial = call(
        functools.partial(gradient, rows, kernels, members),
        (
            jax.ShapeDtypeStruct((rows, padded, lon), BF),
            jax.ShapeDtypeStruct((bands, kernels * own, lon), BF),
        ),
        [SMEM, SMEM] + [VMEM] * 4,
        80_000_000,
        1_200_000,
    )(first, area, sums, predicted, target_fields, mixed)
    grad_low, grad_high = halos(pred_grad, "lat")
    parts = lax.all_to_all(partial, "lat", 0, 0, tiled=True)
    factor = 1.0 / math.sqrt(members * lat_count * lon)
    width = chan // members
    spread = call(
        functools.partial(band_sum, factor),
        jax.ShapeDtypeStruct((members, width, lon), F32),
        [VMEM] * 2,
        20_000_000,
        400_000,
    )(parts, dec_wide)
    spread = lax.all_to_all(spread, "ens", 0, 0, tiled=True)
    latent_grad = call(
        functools.partial(adjoint, rows, kernels),
        jax.ShapeDtypeStruct((rows, chan, lon), BF),
        [VMEM] * 5,
        200_000_000,
        2_000_000,
    )(pred_grad, grad_low, grad_high, back, w_bwd)
    owned = call(
        member_sum, jax.ShapeDtypeStruct((own, kernels, width), F32), [VMEM], 100_000, 150_000
    )(spread)
    return latent_grad[None], owned


def solution(mesh):
    placed = (P("ens", "lat", None, None), P("lat", None, None), P(), P(), P(), P())
    return jax.shard_map(
        body,
        mesh=mesh,
        in_specs=placed,
        out_specs=(P("ens", "lat", None, None), P("lat", None, "ens")),
        check_vma=False,
    )
```

```python
import functools
import math

import jax
import jax.numpy as jnp
import numpy as np
from jax import lax
from jax.experimental import pallas as pl
from jax.experimental.pallas import tpu as pltpu
from jax.sharding import PartitionSpec as P

HALO = 2
SIDE = 2
REACH = 2 * HALO + 1
DELTA = 0.25
BF = jnp.bfloat16
F32 = jnp.float32
VMEM = pl.BlockSpec(memory_space=pltpu.VMEM)
SMEM = pl.BlockSpec(memory_space=pltpu.SMEM)


def smooth_slope(differ):
    return differ * lax.rsqrt(differ * differ + DELTA * DELTA)


def dot_nn(a, b):
    return lax.dot_general(a, b, (((1,), (0,)), ((), ())), preferred_element_type=F32)


def dot_nt(a, b):
    return lax.dot_general(a, b, (((1,), (1,)), ((), ())), preferred_element_type=F32)


def call(kernel, out, specs, flops, moved, scratch=()):
    many = isinstance(out, (tuple, list))
    return pl.pallas_call(
        kernel,
        out_shape=out,
        in_specs=specs,
        out_specs=tuple([VMEM] * len(out)) if many else VMEM,
        scratch_shapes=list(scratch),
        compiler_params=pltpu.CompilerParams(vmem_limit_bytes=32 * 2**20),
        cost_estimate=pl.CostEstimate(flops=flops, bytes_accessed=moved, transcendentals=0),
    )


def tap_block(taps, lat_count, lag, base, basis, offsets, out, row, source, slot, step, sign):
    kernels, lon = basis.shape[1], lag.shape[0]
    cycle = base + source
    inside = jnp.logical_and(cycle >= 0, cycle < lat_count)
    cycle = jnp.clip(cycle, 0, lat_count - 1)
    one, two = SIDE * step, SIDE * step + 1
    off_one, off_two = offsets[one, cycle], offsets[two, cycle]
    mask_one = lag == ((sign * off_one) & (lon - 1))
    mask_two = lag == ((sign * off_two) & (lon - 1))
    for k in range(kernels):
        weight_one = jnp.where(inside, basis[one, k, cycle], 0.0)
        weight_two = jnp.where(inside, basis[two, k, cycle], 0.0)
        weight_two = weight_two + jnp.where(off_one == off_two, weight_one, 0.0)
        value = jnp.where(mask_two, weight_two, jnp.where(mask_one, weight_one, 0.0))
        out[row, slot * lon : (slot + 1) * lon, k * lon : (k + 1) * lon] = value.astype(BF)


def lags(lon):
    return (lax.broadcasted_iota(jnp.int32, (lon, lon), 0) - lax.broadcasted_iota(jnp.int32, (lon, lon), 1)) & (lon - 1)


def padded_rows(dec_t, padded):
    rows, chan = dec_t.shape
    return jnp.concatenate([dec_t[...].astype(F32), jnp.zeros((padded - rows, chan), F32)], axis=0).astype(BF)


def prepare_ahead(rows, taps, lat_count, first, basis, offsets, filters, dec_t, ahead, w_fwd, held, sem):
    fetch = pltpu.make_async_copy(filters, held, sem)
    fetch.start()
    lag = lags(ahead.shape[1] // REACH)
    for row in range(rows):
        for slot in range(REACH):
            tap_block(taps, lat_count, lag, first[0], basis, offsets, ahead, row, row, slot, slot, 1)
    kernels, chan = held.shape[:2]
    dec = padded_rows(dec_t, w_fwd.shape[0])
    w_fwd[:, :chan] = dec
    fetch.wait()
    for k in range(kernels):
        w_fwd[:, (k + 1) * chan : (k + 2) * chan] = dot_nt(dec, held[k]).astype(BF)


def prepare_back(rows, taps, lat_count, first, basis, offsets, filters, dec_t, back, w_bwd):
    lag = lags(back.shape[1] // REACH)
    for row in range(rows):
        for slot in range(REACH):
            step = REACH - 1 - slot
            tap_block(taps, lat_count, lag, first[0], basis, offsets, back, row, row + slot - HALO, slot, step, -1)
    kernels, chan = filters.shape[:2]
    dec = padded_rows(dec_t, w_bwd.shape[2])
    rank = (chan, chan)
    unit = lax.broadcasted_iota(jnp.int32, rank, 0) == lax.broadcasted_iota(jnp.int32, rank, 1)
    w_bwd[0] = dot_nt(jnp.where(unit, 1.0, 0.0).astype(BF), dec).astype(BF)
    for k in range(kernels):
        w_bwd[k + 1] = dot_nt(filters[k], dec).astype(BF)


def forward(rows, kernels, field, low, high, ahead, w_fwd, packed, predicted, mixed):
    lon = field.shape[2]
    chan = field.shape[1]
    wide = [low[0], low[1]] + [field[i] for i in range(rows)] + [high[0], high[1]]
    per = packed.shape[1]
    padded = predicted.shape[1]
    pieces = padded // per
    for i in range(rows):
        source = jnp.concatenate(wide[i : i + REACH], axis=1)
        taps = dot_nn(source, ahead[i]).astype(BF)
        for k in range(kernels):
            mixed[i, k * chan : (k + 1) * chan, :] = taps[:, k * lon : (k + 1) * lon]
        stack = jnp.concatenate([wide[i + HALO]] + [taps[:, k * lon : (k + 1) * lon] for k in range(kernels)], axis=0)
        pred = dot_nn(w_fwd[...], stack)
        predicted[i] = pred
        rounded = pred.astype(BF)
        for q in range(pieces):
            packed[i * pieces + q] = rounded[q * per : (q + 1) * per]
    for q in range(rows * pieces, packed.shape[0]):
        packed[q] = jnp.zeros(packed.shape[1:], BF)


def pairs(visitors, sums):
    members, height, _ = visitors.shape
    for start in range(0, height, 8):
        values = [visitors[m].astype(F32)[start : start + 8] for m in range(members)]
        totals = [None] * members
        for m in range(members):
            for n in range(m + 1, members):
                slope = smooth_slope(values[m] - values[n])
                totals[m] = slope if totals[m] is None else totals[m] + slope
                totals[n] = -slope if totals[n] is None else totals[n] - slope
        for m in range(members):
            sums[m, start : start + 8, :] = totals[m]


def gradient(rows, kernels, members, first, area, sums, predicted, target, mixed, pred_grad, partial):
    variables = target.shape[1]
    padded = predicted.shape[1]
    per = sums.shape[1]
    pieces = padded // per
    lon = predicted.shape[2]
    chan = mixed.shape[1] // kernels
    grads = []
    for i in range(rows):
        pair_sum = jnp.concatenate([sums[i * pieces + q] for q in range(pieces)], axis=0)
        aim = jnp.concatenate([target[i].astype(F32), jnp.zeros((padded - variables, lon), F32)], axis=0)
        grad = area[first[0] + i] * (smooth_slope(predicted[i] - aim) - pair_sum * (1.0 / (members - 1)))
        grad = grad.astype(BF)
        pred_grad[i] = grad
        grads.append(jnp.concatenate([grad, jnp.zeros((lon - padded, lon), BF)], axis=0))
    total = dot_nt(
        jnp.concatenate([mixed[i] for i in range(rows)], axis=1), jnp.concatenate(grads, axis=1)
    )
    owners = partial.shape[0]
    own = chan // owners
    for owner in range(owners):
        partial[owner] = jnp.concatenate(
            [total[k * chan + owner * own : k * chan + (owner + 1) * own] for k in range(kernels)], axis=0
        ).astype(BF)


def band_sum(factor, parts, w_bwd, spread):
    owners, height, lanes = parts.shape
    total = parts[0].astype(F32)
    for owner in range(1, owners):
        total = total + parts[owner].astype(F32)
    total = jnp.concatenate([total * factor, jnp.zeros((lanes - height, lanes), F32)], axis=0)
    upper = total.astype(BF)
    lower = (total - upper.astype(F32)).astype(BF)
    dec = w_bwd[0]
    padded = dec.shape[1]
    result = dot_nt(dec, upper[:, :padded]) + dot_nt(dec, lower[:, :padded])
    per = spread.shape[1]
    for member in range(spread.shape[0]):
        spread[member] = result[member * per : (member + 1) * per]


def member_sum(parts, owned):
    kernels, own, width = owned.shape
    total = parts[0]
    for member in range(1, parts.shape[0]):
        total = total + parts[member]
    turned = total.T
    for k in range(kernels):
        owned[k] = turned[k * own : (k + 1) * own, :width]


def adjoint(rows, kernels, pred_grad, low, high, back, w_bwd, result):
    lon = pred_grad.shape[2]
    wide = [low[0], low[1]] + [pred_grad[i] for i in range(rows)] + [high[0], high[1]]
    for i in range(rows):
        taps = dot_nn(jnp.concatenate(wide[i : i + REACH], axis=1), back[i]).astype(BF)
        total = dot_nn(w_bwd[0], wide[i + HALO])
        for k in range(kernels):
            total = total + dot_nn(w_bwd[k + 1], taps[:, k * lon : (k + 1) * lon])
        result[i] = total.astype(BF)


def halos(block, axis):
    count = lax.axis_size(axis)
    up = [(i, i + 1) for i in range(count - 1)]
    down = [(target, source) for source, target in up]
    return lax.ppermute(block[-HALO:], axis, up), lax.ppermute(block[:HALO], axis, down)


def body(latent_fields, target_fields, filters, decoder, cycle_basis, cycle_offsets):
    field = latent_fields[0]
    rows, chan, lon = field.shape
    lat_count, kernels, taps = cycle_basis.shape
    variables = decoder.shape[1]
    members, bands = lax.axis_size("ens"), lax.axis_size("lat")
    per = 16
    padded = -(-variables // per) * per
    first = (lax.axis_index("lat") * rows).astype(jnp.int32).reshape(1)
    area = jnp.asarray(np.cos(np.pi * (np.arange(lat_count) + 0.5) / lat_count - np.pi / 2), F32)
    dec_t = decoder.T
    basis = cycle_basis.transpose(2, 1, 0)
    offsets = cycle_offsets.T

    low, high = halos(field, "lat")
    ahead, w_fwd = call(
        functools.partial(prepare_ahead, rows, taps, lat_count),
        (
            jax.ShapeDtypeStruct((rows, REACH * lon, kernels * lon), BF),
            jax.ShapeDtypeStruct((padded, (kernels + 1) * chan), BF),
        ),
        [SMEM, SMEM, SMEM, pl.BlockSpec(memory_space=pltpu.HBM), VMEM],
        30_000_000,
        2_000_000,
        [pltpu.VMEM(filters.shape, BF), pltpu.SemaphoreType.DMA],
    )(first, basis, offsets, filters, dec_t)
    back, w_bwd = call(
        functools.partial(prepare_back, rows, taps, lat_count),
        (
            jax.ShapeDtypeStruct((rows, REACH * lon, kernels * lon), BF),
            jax.ShapeDtypeStruct((kernels + 1, chan, padded), BF),
        ),
        [SMEM, SMEM, SMEM, VMEM, VMEM],
        50_000_000,
        2_000_000,
    )(first, basis, offsets, filters, dec_t)
    packed, predicted, mixed = call(
        functools.partial(forward, rows, kernels),
        (
            jax.ShapeDtypeStruct((members, per, lon), BF),
            jax.ShapeDtypeStruct((rows, padded, lon), F32),
            jax.ShapeDtypeStruct((rows, kernels * chan, lon), BF),
        ),
        [VMEM] * 5,
        450_000_000,
        3_000_000,
    )(field, low, high, ahead, w_fwd)
    visitors = lax.all_to_all(packed, "ens", 0, 0, tiled=True)
    sums = call(pairs, jax.ShapeDtypeStruct((members, per, lon), F32), [VMEM], 2_000_000, 200_000)(visitors)
    sums = lax.all_to_all(sums, "ens", 0, 0, tiled=True)
    own = chan // bands
    pred_grad, partial = call(
        functools.partial(gradient, rows, kernels, members),
        (
            jax.ShapeDtypeStruct((rows, padded, lon), BF),
            jax.ShapeDtypeStruct((bands, kernels * own, lon), BF),
        ),
        [SMEM, SMEM] + [VMEM] * 4,
        80_000_000,
        1_200_000,
    )(first, area, sums, predicted, target_fields, mixed)
    parts = lax.all_to_all(partial, "lat", 0, 0, tiled=True)
    grad_low, grad_high = halos(pred_grad, "lat")
    latent_grad = call(
        functools.partial(adjoint, rows, kernels),
        jax.ShapeDtypeStruct((rows, chan, lon), BF),
        [VMEM] * 5,
        200_000_000,
        2_000_000,
    )(pred_grad, grad_low, grad_high, back, w_bwd)
    parts, latent_grad = lax.optimization_barrier((parts, latent_grad))
    factor = 1.0 / math.sqrt(members * lat_count * lon)
    width = chan // members
    spread = call(
        functools.partial(band_sum, factor),
        jax.ShapeDtypeStruct((members, width, lon), F32),
        [VMEM] * 2,
        20_000_000,
        400_000,
    )(parts, w_bwd)
    spread = lax.all_to_all(spread, "ens", 0, 0, tiled=True)
    owned = call(
        member_sum, jax.ShapeDtypeStruct((kernels, own, width), F32), [VMEM], 100_000, 150_000
    )(spread)
    return latent_grad[None], owned.transpose(1, 0, 2)


def solution(mesh):
    placed = (P("ens", "lat", None, None), P("lat", None, None), P(), P(), P(), P())
    return jax.shard_map(
        body,
        mesh=mesh,
        in_specs=placed,
        out_specs=(P("ens", "lat", None, None), P("lat", None, "ens")),
        check_vma=False,
    )
```

```python
import functools
import math

import jax
import jax.numpy as jnp
import numpy as np
from jax import lax
from jax.experimental import pallas as pl
from jax.experimental.pallas import tpu as pltpu
from jax.sharding import PartitionSpec as P

HALO = 2
SIDE = 2
REACH = 2 * HALO + 1
DELTA = 0.25
BF = jnp.bfloat16
F32 = jnp.float32
VMEM = pl.BlockSpec(memory_space=pltpu.VMEM)
SMEM = pl.BlockSpec(memory_space=pltpu.SMEM)


def smooth_slope(differ):
    return differ * lax.rsqrt(differ * differ + DELTA * DELTA)


def dot_nn(a, b):
    return lax.dot_general(a, b, (((1,), (0,)), ((), ())), preferred_element_type=F32)


def dot_nt(a, b):
    return lax.dot_general(a, b, (((1,), (1,)), ((), ())), preferred_element_type=F32)


def call(kernel, out, specs, flops, moved, scratch=()):
    many = isinstance(out, (tuple, list))
    return pl.pallas_call(
        kernel,
        out_shape=out,
        in_specs=specs,
        out_specs=tuple([VMEM] * len(out)) if many else VMEM,
        scratch_shapes=list(scratch),
        compiler_params=pltpu.CompilerParams(vmem_limit_bytes=32 * 2**20),
        cost_estimate=pl.CostEstimate(flops=flops, bytes_accessed=moved, transcendentals=0),
    )


def tap_block(taps, lat_count, lag, base, basis, offsets, out, row, source, slot, step, sign):
    kernels, lon = basis.shape[1], lag.shape[0]
    cycle = base + source
    inside = jnp.logical_and(cycle >= 0, cycle < lat_count)
    cycle = jnp.clip(cycle, 0, lat_count - 1)
    one, two = SIDE * step, SIDE * step + 1
    off_one, off_two = offsets[one, cycle], offsets[two, cycle]
    mask_one = lag == ((sign * off_one) & (lon - 1))
    mask_two = lag == ((sign * off_two) & (lon - 1))
    for k in range(kernels):
        weight_one = jnp.where(inside, basis[one, k, cycle], 0.0)
        weight_two = jnp.where(inside, basis[two, k, cycle], 0.0)
        weight_two = weight_two + jnp.where(off_one == off_two, weight_one, 0.0)
        value = jnp.where(mask_two, weight_two, jnp.where(mask_one, weight_one, 0.0))
        out[row, slot * lon : (slot + 1) * lon, k * lon : (k + 1) * lon] = value.astype(BF)


def lags(lon):
    return (lax.broadcasted_iota(jnp.int32, (lon, lon), 0) - lax.broadcasted_iota(jnp.int32, (lon, lon), 1)) & (lon - 1)


def padded_rows(dec_t, padded):
    rows, chan = dec_t.shape
    return jnp.concatenate([dec_t[...].astype(F32), jnp.zeros((padded - rows, chan), F32)], axis=0).astype(BF)


def prepare_ahead(
    rows, taps, lat_count, first, basis, offsets, filters, dec_in, field, ahead, w_fwd, held, near, dec_t, sems
):
    moves = ((filters, held), (dec_in, dec_t), (field, near))
    moves = [pltpu.make_async_copy(source, target, sems.at[n]) for n, (source, target) in enumerate(moves)]
    for move in moves:
        move.start()
    lag = lags(ahead.shape[1] // REACH)
    for row in range(rows):
        for slot in range(REACH):
            tap_block(taps, lat_count, lag, first[0], basis, offsets, ahead, row, row, slot, slot, 1)
    kernels, chan = held.shape[:2]
    for move in moves:
        move.wait()
    dec = padded_rows(dec_t, w_fwd.shape[0])
    w_fwd[:, :chan] = dec
    for k in range(kernels):
        w_fwd[:, (k + 1) * chan : (k + 2) * chan] = dot_nt(dec, held[k]).astype(BF)


def prepare_back(rows, taps, lat_count, first, basis, offsets, filters, dec_t, back, w_bwd):
    lag = lags(back.shape[1] // REACH)
    for row in range(rows):
        for slot in range(REACH):
            step = REACH - 1 - slot
            tap_block(taps, lat_count, lag, first[0], basis, offsets, back, row, row + slot - HALO, slot, step, -1)
    kernels, chan = filters.shape[:2]
    dec = padded_rows(dec_t, w_bwd.shape[2])
    rank = (chan, chan)
    unit = lax.broadcasted_iota(jnp.int32, rank, 0) == lax.broadcasted_iota(jnp.int32, rank, 1)
    w_bwd[0] = dot_nt(jnp.where(unit, 1.0, 0.0).astype(BF), dec).astype(BF)
    for k in range(kernels):
        w_bwd[k + 1] = dot_nt(filters[k], dec).astype(BF)


def forward(rows, kernels, field, low, high, ahead, w_fwd, packed, predicted, mixed):
    lon = field.shape[2]
    chan = field.shape[1]
    wide = [low[0], low[1]] + [field[i] for i in range(rows)] + [high[0], high[1]]
    per = packed.shape[1]
    padded = predicted.shape[1]
    pieces = padded // per
    for i in range(rows):
        source = jnp.concatenate(wide[i : i + REACH], axis=1)
        taps = dot_nn(source, ahead[i]).astype(BF)
        for k in range(kernels):
            mixed[i, k * chan : (k + 1) * chan, :] = taps[:, k * lon : (k + 1) * lon]
        stack = jnp.concatenate([wide[i + HALO]] + [taps[:, k * lon : (k + 1) * lon] for k in range(kernels)], axis=0)
        pred = dot_nn(w_fwd[...], stack)
        predicted[i] = pred
        rounded = pred.astype(BF)
        for q in range(pieces):
            packed[i * pieces + q] = rounded[q * per : (q + 1) * per]
    for q in range(rows * pieces, packed.shape[0]):
        packed[q] = jnp.zeros(packed.shape[1:], BF)


def pairs(visitors, sums):
    members, height, _ = visitors.shape
    for start in range(0, height, 8):
        values = [visitors[m].astype(F32)[start : start + 8] for m in range(members)]
        totals = [None] * members
        for m in range(members):
            for n in range(m + 1, members):
                slope = smooth_slope(values[m] - values[n])
                totals[m] = slope if totals[m] is None else totals[m] + slope
                totals[n] = -slope if totals[n] is None else totals[n] - slope
        for m in range(members):
            sums[m, start : start + 8, :] = totals[m]


def gradient(rows, kernels, members, first, area, sums, predicted, target, mixed, pred_grad, partial):
    variables = target.shape[1]
    padded = predicted.shape[1]
    per = sums.shape[1]
    pieces = padded // per
    lon = predicted.shape[2]
    chan = mixed.shape[1] // kernels
    grads = []
    for i in range(rows):
        pair_sum = jnp.concatenate([sums[i * pieces + q] for q in range(pieces)], axis=0)
        aim = jnp.concatenate([target[i].astype(F32), jnp.zeros((padded - variables, lon), F32)], axis=0)
        grad = area[first[0] + i] * (smooth_slope(predicted[i] - aim) - pair_sum * (1.0 / (members - 1)))
        grad = grad.astype(BF)
        pred_grad[i] = grad
        grads.append(jnp.concatenate([grad, jnp.zeros((lon - padded, lon), BF)], axis=0))
    total = dot_nt(
        jnp.concatenate([mixed[i] for i in range(rows)], axis=1), jnp.concatenate(grads, axis=1)
    )
    owners = partial.shape[0]
    own = chan // owners
    for owner in range(owners):
        partial[owner] = jnp.concatenate(
            [total[k * chan + owner * own : k * chan + (owner + 1) * own] for k in range(kernels)], axis=0
        ).astype(BF)


def band_sum(factor, parts, w_bwd, spread):
    owners, height, lanes = parts.shape
    total = parts[0].astype(F32)
    for owner in range(1, owners):
        total = total + parts[owner].astype(F32)
    total = jnp.concatenate([total * factor, jnp.zeros((lanes - height, lanes), F32)], axis=0)
    upper = total.astype(BF)
    lower = (total - upper.astype(F32)).astype(BF)
    dec = w_bwd[0]
    padded = dec.shape[1]
    result = dot_nt(dec, upper[:, :padded]) + dot_nt(dec, lower[:, :padded])
    per = spread.shape[1]
    for member in range(spread.shape[0]):
        spread[member] = result[member * per : (member + 1) * per]


def member_sum(parts, owned):
    kernels, own, width = owned.shape
    total = parts[0]
    for member in range(1, parts.shape[0]):
        total = total + parts[member]
    turned = total.T
    for k in range(kernels):
        owned[k] = turned[k * own : (k + 1) * own, :width]


def adjoint(rows, kernels, pred_grad, low, high, back, w_bwd, result):
    lon = pred_grad.shape[2]
    wide = [low[0], low[1]] + [pred_grad[i] for i in range(rows)] + [high[0], high[1]]
    for i in range(rows):
        taps = dot_nn(jnp.concatenate(wide[i : i + REACH], axis=1), back[i]).astype(BF)
        total = dot_nn(w_bwd[0], wide[i + HALO])
        for k in range(kernels):
            total = total + dot_nn(w_bwd[k + 1], taps[:, k * lon : (k + 1) * lon])
        result[i] = total.astype(BF)


def halos(block, axis):
    count = lax.axis_size(axis)
    up = [(i, i + 1) for i in range(count - 1)]
    down = [(target, source) for source, target in up]
    return lax.ppermute(block[-HALO:], axis, up), lax.ppermute(block[:HALO], axis, down)


def body(latent_fields, target_fields, filters, decoder, cycle_basis, cycle_offsets):
    field = latent_fields[0]
    rows, chan, lon = field.shape
    lat_count, kernels, taps = cycle_basis.shape
    variables = decoder.shape[1]
    members, bands = lax.axis_size("ens"), lax.axis_size("lat")
    per = 16
    padded = -(-variables // per) * per
    first = (lax.axis_index("lat") * rows).astype(jnp.int32).reshape(1)
    area = jnp.asarray(np.cos(np.pi * (np.arange(lat_count) + 0.5) / lat_count - np.pi / 2), F32)
    dec_t = decoder.T
    basis = cycle_basis.transpose(2, 1, 0)
    offsets = cycle_offsets.T

    low, high = halos(field, "lat")
    stay = functools.partial(pltpu.with_memory_space_constraint, memory_space=pltpu.HBM)
    hbm = pl.BlockSpec(memory_space=pltpu.HBM)
    ahead, w_fwd, held, near, dec_near = call(
        functools.partial(prepare_ahead, rows, taps, lat_count),
        (
            jax.ShapeDtypeStruct((rows, REACH * lon, kernels * lon), BF),
            jax.ShapeDtypeStruct((padded, (kernels + 1) * chan), BF),
            jax.ShapeDtypeStruct(filters.shape, BF),
            jax.ShapeDtypeStruct(field.shape, BF),
            jax.ShapeDtypeStruct(dec_t.shape, BF),
        ),
        [SMEM, SMEM, SMEM, hbm, hbm, hbm],
        30_000_000,
        2_000_000,
        [pltpu.SemaphoreType.DMA((3,))],
    )(first, stay(basis), stay(offsets), stay(filters), stay(dec_t), stay(field))
    back, w_bwd = call(
        functools.partial(prepare_back, rows, taps, lat_count),
        (
            jax.ShapeDtypeStruct((rows, REACH * lon, kernels * lon), BF),
            jax.ShapeDtypeStruct((kernels + 1, chan, padded), BF),
        ),
        [SMEM, SMEM, SMEM, VMEM, VMEM],
        50_000_000,
        2_000_000,
    )(first, stay(basis), stay(offsets), held, dec_near)
    packed, predicted, mixed = call(
        functools.partial(forward, rows, kernels),
        (
            jax.ShapeDtypeStruct((members, per, lon), BF),
            jax.ShapeDtypeStruct((rows, padded, lon), F32),
            jax.ShapeDtypeStruct((rows, kernels * chan, lon), BF),
        ),
        [VMEM] * 5,
        450_000_000,
        3_000_000,
    )(near, low, high, ahead, w_fwd)
    visitors = lax.all_to_all(packed, "ens", 0, 0, tiled=True)
    visitors, back, w_bwd = lax.optimization_barrier((visitors, back, w_bwd))
    sums = call(pairs, jax.ShapeDtypeStruct((members, per, lon), F32), [VMEM], 2_000_000, 200_000)(visitors)
    sums = lax.all_to_all(sums, "ens", 0, 0, tiled=True)
    own = chan // bands
    pred_grad, partial = call(
        functools.partial(gradient, rows, kernels, members),
        (
            jax.ShapeDtypeStruct((rows, padded, lon), BF),
            jax.ShapeDtypeStruct((bands, kernels * own, lon), BF),
        ),
        [SMEM, SMEM] + [VMEM] * 4,
        80_000_000,
        1_200_000,
    )(first, area, sums, predicted, target_fields, mixed)
    parts = lax.all_to_all(partial, "lat", 0, 0, tiled=True)
    grad_low, grad_high = halos(pred_grad, "lat")
    latent_grad = call(
        functools.partial(adjoint, rows, kernels),
        jax.ShapeDtypeStruct((rows, chan, lon), BF),
        [VMEM] * 5,
        200_000_000,
        2_000_000,
    )(pred_grad, grad_low, grad_high, back, w_bwd)
    parts, latent_grad = lax.optimization_barrier((parts, latent_grad))
    factor = 1.0 / math.sqrt(members * lat_count * lon)
    width = chan // members
    spread = call(
        functools.partial(band_sum, factor),
        jax.ShapeDtypeStruct((members, width, lon), F32),
        [VMEM] * 2,
        20_000_000,
        400_000,
    )(parts, w_bwd)
    spread = lax.all_to_all(spread, "ens", 0, 0, tiled=True)
    owned = call(
        member_sum, jax.ShapeDtypeStruct((kernels, own, width), F32), [VMEM], 100_000, 150_000
    )(spread)
    return latent_grad[None], owned.transpose(1, 0, 2)


def solution(mesh):
    placed = (P("ens", "lat", None, None), P("lat", None, None), P(), P(), P(), P())
    return jax.shard_map(
        body,
        mesh=mesh,
        in_specs=placed,
        out_specs=(P("ens", "lat", None, None), P("lat", None, "ens")),
        check_vma=False,
    )
```

```python
import functools
import math

import jax
import jax.numpy as jnp
import numpy as np
from jax import lax
from jax.experimental import pallas as pl
from jax.experimental.pallas import tpu as pltpu
from jax.sharding import PartitionSpec as P

HALO = 2
SIDE = 2
REACH = 2 * HALO + 1
DELTA = 0.25
BF = jnp.bfloat16
F32 = jnp.float32
VMEM = pl.BlockSpec(memory_space=pltpu.VMEM)
SMEM = pl.BlockSpec(memory_space=pltpu.SMEM)


def smooth_slope(differ):
    return differ * lax.rsqrt(differ * differ + DELTA * DELTA)


def dot_nn(a, b):
    return lax.dot_general(a, b, (((1,), (0,)), ((), ())), preferred_element_type=F32)


def dot_nt(a, b):
    return lax.dot_general(a, b, (((1,), (1,)), ((), ())), preferred_element_type=F32)


def call(kernel, out, specs, flops, moved, scratch=()):
    many = isinstance(out, (tuple, list))
    return pl.pallas_call(
        kernel,
        out_shape=out,
        in_specs=specs,
        out_specs=tuple([VMEM] * len(out)) if many else VMEM,
        scratch_shapes=list(scratch),
        compiler_params=pltpu.CompilerParams(vmem_limit_bytes=32 * 2**20),
        cost_estimate=pl.CostEstimate(flops=flops, bytes_accessed=moved, transcendentals=0),
    )


def tap_block(taps, lat_count, lag, base, basis, offsets, out, row, source, slot, step, sign):
    kernels, lon = basis.shape[1], lag.shape[0]
    cycle = base + source
    inside = jnp.logical_and(cycle >= 0, cycle < lat_count)
    cycle = jnp.clip(cycle, 0, lat_count - 1)
    one, two = SIDE * step, SIDE * step + 1
    off_one, off_two = offsets[one, cycle], offsets[two, cycle]
    mask_one = lag == ((sign * off_one) & (lon - 1))
    mask_two = lag == ((sign * off_two) & (lon - 1))
    for k in range(kernels):
        weight_one = jnp.where(inside, basis[one, k, cycle], 0.0)
        weight_two = jnp.where(inside, basis[two, k, cycle], 0.0)
        weight_two = weight_two + jnp.where(off_one == off_two, weight_one, 0.0)
        value = jnp.where(mask_two, weight_two, jnp.where(mask_one, weight_one, 0.0))
        out[row, slot * lon : (slot + 1) * lon, k * lon : (k + 1) * lon] = value.astype(BF)


def lags(lon):
    return (lax.broadcasted_iota(jnp.int32, (lon, lon), 0) - lax.broadcasted_iota(jnp.int32, (lon, lon), 1)) & (lon - 1)


def padded_rows(dec_t, padded):
    rows, chan = dec_t.shape
    return jnp.concatenate([dec_t[...].astype(F32), jnp.zeros((padded - rows, chan), F32)], axis=0).astype(BF)


def prepare_ahead(
    rows, taps, lat_count, place, basis, offsets, filters, dec_in, field, ahead, w_fwd, held, near, dec_t, sems
):
    moves = ((filters, held), (dec_in, dec_t), (field, near))
    moves = [pltpu.make_async_copy(source, target, sems.at[n]) for n, (source, target) in enumerate(moves)]
    for move in moves:
        move.start()
    lag = lags(ahead.shape[1] // REACH)
    for row in range(rows):
        for slot in range(REACH):
            tap_block(taps, lat_count, lag, place[0] * rows, basis, offsets, ahead, row, row, slot, slot, 1)
    kernels, chan = held.shape[:2]
    for move in moves:
        move.wait()
    dec = padded_rows(dec_t, w_fwd.shape[0])
    w_fwd[:, :chan] = dec
    for k in range(kernels):
        w_fwd[:, (k + 1) * chan : (k + 2) * chan] = dot_nt(dec, held[k]).astype(BF)


def prepare_back(rows, taps, lat_count, place, basis, offsets, filters, dec_t, back, w_bwd):
    lag = lags(back.shape[1] // REACH)
    for row in range(rows):
        for slot in range(REACH):
            step = REACH - 1 - slot
            tap_block(taps, lat_count, lag, place[0] * rows, basis, offsets, back, row, row + slot - HALO, slot, step, -1)
    kernels, chan = filters.shape[:2]
    dec = padded_rows(dec_t, w_bwd.shape[2])
    rank = (chan, chan)
    unit = lax.broadcasted_iota(jnp.int32, rank, 0) == lax.broadcasted_iota(jnp.int32, rank, 1)
    w_bwd[0] = dot_nt(jnp.where(unit, 1.0, 0.0).astype(BF), dec).astype(BF)
    for k in range(kernels):
        w_bwd[k + 1] = dot_nt(filters[k], dec).astype(BF)


def forward(rows, kernels, place, field, cross, chip, ahead, w_fwd, packed, predicted, mixed):
    lon = field.shape[2]
    chan = field.shape[1]
    low, high = sides((place[0] & 1) == 1, cross, chip)
    wide = low + [field[i] for i in range(rows)] + high
    per = packed.shape[1]
    padded = predicted.shape[1]
    pieces = padded // per
    for i in range(rows):
        source = jnp.concatenate(wide[i : i + REACH], axis=1)
        taps = dot_nn(source, ahead[i]).astype(BF)
        for k in range(kernels):
            mixed[i, k * chan : (k + 1) * chan, :] = taps[:, k * lon : (k + 1) * lon]
        stack = jnp.concatenate([wide[i + HALO]] + [taps[:, k * lon : (k + 1) * lon] for k in range(kernels)], axis=0)
        pred = dot_nn(w_fwd[...], stack)
        predicted[i] = pred
        rounded = pred.astype(BF)
        for q in range(pieces):
            packed[i * pieces + q] = rounded[q * per : (q + 1) * per]
    for q in range(rows * pieces, packed.shape[0]):
        packed[q] = jnp.zeros(packed.shape[1:], BF)


def pairs(visitors, sums):
    members, height, _ = visitors.shape
    for start in range(0, height, 8):
        values = [visitors[m].astype(F32)[start : start + 8] for m in range(members)]
        totals = [None] * members
        for m in range(members):
            for n in range(m + 1, members):
                slope = smooth_slope(values[m] - values[n])
                totals[m] = slope if totals[m] is None else totals[m] + slope
                totals[n] = -slope if totals[n] is None else totals[n] - slope
        for m in range(members):
            sums[m, start : start + 8, :] = totals[m]


def gradient(rows, kernels, members, place, area, sums, predicted, target, mixed, pred_grad, cross, chip, partial):
    variables = target.shape[1]
    padded = predicted.shape[1]
    per = sums.shape[1]
    pieces = padded // per
    lon = predicted.shape[2]
    chan = mixed.shape[1] // kernels
    grads, edges = [], []
    odd = (place[0] & 1) == 1
    for i in range(rows):
        pair_sum = jnp.concatenate([sums[i * pieces + q] for q in range(pieces)], axis=0)
        aim = jnp.concatenate([target[i].astype(F32), jnp.zeros((padded - variables, lon), F32)], axis=0)
        grad = area[place[0] * rows + i] * (smooth_slope(predicted[i] - aim) - pair_sum * (1.0 / (members - 1)))
        grad = grad.astype(BF)
        pred_grad[i] = grad
        edges.append(grad)
        grads.append(jnp.concatenate([grad, jnp.zeros((lon - padded, lon), BF)], axis=0))
    for n in range(HALO):
        top, bottom = edges[rows - HALO + n], edges[n]
        cross[n] = jnp.where(odd, top, bottom)
        chip[n] = jnp.where(odd, bottom, top)
    total = dot_nt(
        jnp.concatenate([mixed[i] for i in range(rows)], axis=1), jnp.concatenate(grads, axis=1)
    )
    owners = partial.shape[0]
    own = chan // owners
    for owner in range(owners):
        partial[owner] = jnp.concatenate(
            [total[k * chan + owner * own : k * chan + (owner + 1) * own] for k in range(kernels)], axis=0
        ).astype(BF)


def band_sum(factor, parts, w_bwd, spread):
    owners, height, lanes = parts.shape
    total = parts[0].astype(F32)
    for owner in range(1, owners):
        total = total + parts[owner].astype(F32)
    total = jnp.concatenate([total * factor, jnp.zeros((lanes - height, lanes), F32)], axis=0)
    upper = total.astype(BF)
    lower = (total - upper.astype(F32)).astype(BF)
    dec = w_bwd[0]
    padded = dec.shape[1]
    result = dot_nt(dec, upper[:, :padded]) + dot_nt(dec, lower[:, :padded])
    per = spread.shape[1]
    for member in range(spread.shape[0]):
        spread[member] = result[member * per : (member + 1) * per]


def member_sum(parts, owned):
    kernels, own, width = owned.shape
    total = parts[0]
    for member in range(1, parts.shape[0]):
        total = total + parts[member]
    turned = total.T
    for k in range(kernels):
        owned[k] = turned[k * own : (k + 1) * own, :width]


def adjoint(rows, kernels, place, pred_grad, cross, chip, back, w_bwd, result):
    lon = pred_grad.shape[2]
    low, high = sides((place[0] & 1) == 1, cross, chip)
    wide = low + [pred_grad[i] for i in range(rows)] + high
    for i in range(rows):
        taps = dot_nn(jnp.concatenate(wide[i : i + REACH], axis=1), back[i]).astype(BF)
        total = dot_nn(w_bwd[0], wide[i + HALO])
        for k in range(kernels):
            total = total + dot_nn(w_bwd[k + 1], taps[:, k * lon : (k + 1) * lon])
        result[i] = total.astype(BF)


def cut(place, field, cross, chip, sems):
    rows = field.shape[0]
    odd = (place[0] & 1)
    far = (rows - HALO) * odd
    moves = [
        pltpu.make_async_copy(field.at[pl.ds(far, HALO)], cross, sems.at[0]),
        pltpu.make_async_copy(field.at[pl.ds(rows - HALO - far, HALO)], chip, sems.at[1]),
    ]
    for move in moves:
        move.start()
    for move in moves:
        move.wait()


def sides(odd, cross, chip):
    low = [jnp.where(odd, chip[n], cross[n]) for n in range(HALO)]
    high = [jnp.where(odd, cross[n], chip[n]) for n in range(HALO)]
    return low, high


def exchange(cross, chip, axis):
    count = lax.axis_size(axis)
    far = [(i, i + 1) for i in range(1, count - 1, 2)]
    near = [(i, i + 1) for i in range(0, count - 1, 2)]
    cross = lax.ppermute(cross, axis, far + [(b, a) for a, b in far])
    chip = lax.ppermute(chip, axis, near + [(b, a) for a, b in near])
    return cross, chip


def body(latent_fields, target_fields, filters, decoder, cycle_basis, cycle_offsets):
    field = latent_fields[0]
    rows, chan, lon = field.shape
    lat_count, kernels, taps = cycle_basis.shape
    variables = decoder.shape[1]
    members, bands = lax.axis_size("ens"), lax.axis_size("lat")
    per = 16
    padded = -(-variables // per) * per
    band = lax.axis_index("lat").astype(jnp.int32)
    place = band.reshape(1)
    area = jnp.asarray(np.cos(np.pi * (np.arange(lat_count) + 0.5) / lat_count - np.pi / 2), F32)
    dec_t = decoder.T
    basis = cycle_basis.transpose(2, 1, 0)
    offsets = cycle_offsets.T

    stay = functools.partial(pltpu.with_memory_space_constraint, memory_space=pltpu.HBM)
    hbm = pl.BlockSpec(memory_space=pltpu.HBM)
    edge = jax.ShapeDtypeStruct((HALO, chan, lon), BF)
    pair = pltpu.SemaphoreType.DMA((2,))
    cross, chip = call(cut, (edge, edge), [SMEM, hbm], 0, 500_000, [pair])(place, stay(field))
    cross, chip = exchange(cross, chip, "lat")
    ahead, w_fwd, held, near, dec_near = call(
        functools.partial(prepare_ahead, rows, taps, lat_count),
        (
            jax.ShapeDtypeStruct((rows, REACH * lon, kernels * lon), BF),
            jax.ShapeDtypeStruct((padded, (kernels + 1) * chan), BF),
            jax.ShapeDtypeStruct(filters.shape, BF),
            jax.ShapeDtypeStruct(field.shape, BF),
            jax.ShapeDtypeStruct(dec_t.shape, BF),
        ),
        [SMEM, SMEM, SMEM, hbm, hbm, hbm],
        30_000_000,
        2_000_000,
        [pltpu.SemaphoreType.DMA((3,))],
    )(place, stay(basis), stay(offsets), stay(filters), stay(dec_t), stay(field))
    back, w_bwd = call(
        functools.partial(prepare_back, rows, taps, lat_count),
        (
            jax.ShapeDtypeStruct((rows, REACH * lon, kernels * lon), BF),
            jax.ShapeDtypeStruct((kernels + 1, chan, padded), BF),
        ),
        [SMEM, SMEM, SMEM, VMEM, VMEM],
        50_000_000,
        2_000_000,
    )(place, stay(basis), stay(offsets), held, dec_near)
    packed, predicted, mixed = call(
        functools.partial(forward, rows, kernels),
        (
            jax.ShapeDtypeStruct((members, per, lon), BF),
            jax.ShapeDtypeStruct((rows, padded, lon), F32),
            jax.ShapeDtypeStruct((rows, kernels * chan, lon), BF),
        ),
        [SMEM] + [VMEM] * 5,
        450_000_000,
        3_000_000,
    )(place, near, cross, chip, ahead, w_fwd)
    visitors = lax.all_to_all(packed, "ens", 0, 0, tiled=True)
    visitors, back, w_bwd = lax.optimization_barrier((visitors, back, w_bwd))
    sums = call(pairs, jax.ShapeDtypeStruct((members, per, lon), F32), [VMEM], 2_000_000, 200_000)(visitors)
    sums = lax.all_to_all(sums, "ens", 0, 0, tiled=True)
    own = chan // bands
    edge = jax.ShapeDtypeStruct((HALO, padded, lon), BF)
    pred_grad, cross, chip, partial = call(
        functools.partial(gradient, rows, kernels, members),
        (
            jax.ShapeDtypeStruct((rows, padded, lon), BF),
            edge,
            edge,
            jax.ShapeDtypeStruct((bands, kernels * own, lon), BF),
        ),
        [SMEM, SMEM] + [VMEM] * 4,
        80_000_000,
        1_200_000,
    )(place, area, sums, predicted, target_fields, mixed)
    parts = lax.all_to_all(partial, "lat", 0, 0, tiled=True)
    cross, chip = exchange(cross, chip, "lat")
    parts, cross, chip = lax.optimization_barrier((parts, cross, chip))
    latent_grad = call(
        functools.partial(adjoint, rows, kernels),
        jax.ShapeDtypeStruct((rows, chan, lon), BF),
        [SMEM] + [VMEM] * 5,
        200_000_000,
        2_000_000,
    )(place, pred_grad, cross, chip, back, w_bwd)
    factor = 1.0 / math.sqrt(members * lat_count * lon)
    width = chan // members
    spread = call(
        functools.partial(band_sum, factor),
        jax.ShapeDtypeStruct((members, width, lon), F32),
        [VMEM] * 2,
        20_000_000,
        400_000,
    )(parts, w_bwd)
    spread = lax.all_to_all(spread, "ens", 0, 0, tiled=True)
    spread, latent_grad = lax.optimization_barrier((spread, latent_grad))
    owned = call(
        member_sum, jax.ShapeDtypeStruct((kernels, own, width), F32), [VMEM], 100_000, 150_000
    )(spread)
    return latent_grad[None], owned.transpose(1, 0, 2)


def solution(mesh):
    placed = (P("ens", "lat", None, None), P("lat", None, None), P(), P(), P(), P())
    return jax.shard_map(
        body,
        mesh=mesh,
        in_specs=placed,
        out_specs=(P("ens", "lat", None, None), P("lat", None, "ens")),
        check_vma=False,
    )
```

```python
import functools
import math

import jax
import jax.numpy as jnp
import numpy as np
from jax import lax
from jax.experimental import pallas as pl
from jax.experimental.pallas import tpu as pltpu
from jax.sharding import PartitionSpec as P

HALO = 2
SIDE = 2
REACH = 2 * HALO + 1
DELTA = 0.25
BF = jnp.bfloat16
F32 = jnp.float32
VMEM = pl.BlockSpec(memory_space=pltpu.VMEM)
SMEM = pl.BlockSpec(memory_space=pltpu.SMEM)


def smooth_slope(differ):
    return differ * lax.rsqrt(differ * differ + DELTA * DELTA)


def dot_nn(a, b):
    return lax.dot_general(a, b, (((1,), (0,)), ((), ())), preferred_element_type=F32)


def dot_nt(a, b):
    return lax.dot_general(a, b, (((1,), (1,)), ((), ())), preferred_element_type=F32)


def call(kernel, out, specs, flops, moved, scratch=()):
    many = isinstance(out, (tuple, list))
    return pl.pallas_call(
        kernel,
        out_shape=out,
        in_specs=specs,
        out_specs=tuple([VMEM] * len(out)) if many else VMEM,
        scratch_shapes=list(scratch),
        compiler_params=pltpu.CompilerParams(vmem_limit_bytes=32 * 2**20),
        cost_estimate=pl.CostEstimate(flops=flops, bytes_accessed=moved, transcendentals=0),
    )


def tap_block(taps, lat_count, lag, base, basis, offsets, out, row, source, slot, step, sign):
    kernels, lon = basis.shape[1], lag.shape[0]
    cycle = base + source
    inside = jnp.logical_and(cycle >= 0, cycle < lat_count)
    cycle = jnp.clip(cycle, 0, lat_count - 1)
    one, two = SIDE * step, SIDE * step + 1
    off_one, off_two = offsets[one, cycle], offsets[two, cycle]
    mask_one = lag == ((sign * off_one) & (lon - 1))
    mask_two = lag == ((sign * off_two) & (lon - 1))
    for k in range(kernels):
        weight_one = jnp.where(inside, basis[one, k, cycle], 0.0)
        weight_two = jnp.where(inside, basis[two, k, cycle], 0.0)
        weight_two = weight_two + jnp.where(off_one == off_two, weight_one, 0.0)
        value = jnp.where(mask_two, weight_two, jnp.where(mask_one, weight_one, 0.0))
        out[row, slot * lon : (slot + 1) * lon, k * lon : (k + 1) * lon] = value.astype(BF)


def lags(lon):
    return (lax.broadcasted_iota(jnp.int32, (lon, lon), 0) - lax.broadcasted_iota(jnp.int32, (lon, lon), 1)) & (lon - 1)


def padded_rows(dec_t, padded):
    rows, chan = dec_t.shape
    return jnp.concatenate([dec_t[...].astype(F32), jnp.zeros((padded - rows, chan), F32)], axis=0).astype(BF)


def prepare_ahead(
    rows, taps, lat_count, place, basis, offsets, filters, dec_in, field, ahead, w_fwd, held, near, dec_t, sems
):
    moves = ((filters, held), (dec_in, dec_t), (field, near))
    moves = [pltpu.make_async_copy(source, target, sems.at[n]) for n, (source, target) in enumerate(moves)]
    for move in moves:
        move.start()
    lag = lags(ahead.shape[1] // REACH)
    for row in range(rows):
        for slot in range(REACH):
            tap_block(taps, lat_count, lag, place[0] * rows, basis, offsets, ahead, row, row, slot, slot, 1)
    kernels, chan = held.shape[:2]
    for move in moves:
        move.wait()
    dec = padded_rows(dec_t, w_fwd.shape[0])
    w_fwd[:, :chan] = dec
    for k in range(kernels):
        w_fwd[:, (k + 1) * chan : (k + 2) * chan] = dot_nt(dec, held[k]).astype(BF)


def prepare_back(rows, taps, lat_count, place, basis, offsets, filters, dec_t, back, w_bwd):
    lag = lags(back.shape[1] // REACH)
    for row in range(rows):
        for slot in range(REACH):
            step = REACH - 1 - slot
            tap_block(taps, lat_count, lag, place[0] * rows, basis, offsets, back, row, row + slot - HALO, slot, step, -1)
    kernels, chan = filters.shape[:2]
    dec = padded_rows(dec_t, w_bwd.shape[2])
    rank = (chan, chan)
    unit = lax.broadcasted_iota(jnp.int32, rank, 0) == lax.broadcasted_iota(jnp.int32, rank, 1)
    w_bwd[0] = dot_nt(jnp.where(unit, 1.0, 0.0).astype(BF), dec).astype(BF)
    for k in range(kernels):
        w_bwd[k + 1] = dot_nt(filters[k], dec).astype(BF)


def forward(rows, kernels, place, field, cross, chip, ahead, w_fwd, packed, predicted, mixed):
    lon = field.shape[2]
    chan = field.shape[1]
    low, high = sides((place[0] & 1) == 1, cross, chip)
    wide = low + [field[i] for i in range(rows)] + high
    per = packed.shape[1]
    padded = predicted.shape[1]
    pieces = padded // per
    for i in range(rows):
        source = jnp.concatenate(wide[i : i + REACH], axis=1)
        taps = dot_nn(source, ahead[i]).astype(BF)
        for k in range(kernels):
            mixed[i, k * chan : (k + 1) * chan, :] = taps[:, k * lon : (k + 1) * lon]
        stack = jnp.concatenate([wide[i + HALO]] + [taps[:, k * lon : (k + 1) * lon] for k in range(kernels)], axis=0)
        pred = dot_nn(w_fwd[...], stack)
        predicted[i] = pred
        rounded = pred.astype(BF)
        for q in range(pieces):
            packed[i * pieces + q] = rounded[q * per : (q + 1) * per]
    for q in range(rows * pieces, packed.shape[0]):
        packed[q] = jnp.zeros(packed.shape[1:], BF)


def pairs(visitors, sums):
    members, height, _ = visitors.shape
    pieces = []
    for start in range(0, height, 8):
        values = [visitors[m].astype(F32)[start : start + 8] for m in range(members)]
        totals = [None] * members
        for m in range(members):
            for n in range(m + 1, members):
                slope = smooth_slope(values[m] - values[n])
                totals[m] = slope if totals[m] is None else totals[m] + slope
                totals[n] = -slope if totals[n] is None else totals[n] - slope
        pieces.append(totals)
    for m in range(members):
        sums[m] = jnp.concatenate([totals[m] for totals in pieces], axis=0).astype(BF)


def gradient(rows, kernels, members, place, area, sums, predicted, target, mixed, pred_grad, cross, chip, partial):
    variables = target.shape[1]
    padded = predicted.shape[1]
    per = sums.shape[1]
    pieces = padded // per
    lon = predicted.shape[2]
    chan = mixed.shape[1] // kernels
    grads, edges = [], []
    odd = (place[0] & 1) == 1
    for i in range(rows):
        pair_sum = jnp.concatenate([sums[i * pieces + q].astype(F32) for q in range(pieces)], axis=0)
        aim = jnp.concatenate([target[i].astype(F32), jnp.zeros((padded - variables, lon), F32)], axis=0)
        grad = area[place[0] * rows + i] * (smooth_slope(predicted[i] - aim) - pair_sum * (1.0 / (members - 1)))
        grad = grad.astype(BF)
        pred_grad[i] = grad
        edges.append(grad)
        grads.append(jnp.concatenate([grad, jnp.zeros((lon - padded, lon), BF)], axis=0))
    for n in range(HALO):
        top, bottom = edges[rows - HALO + n], edges[n]
        cross[n] = jnp.where(odd, top, bottom)
        chip[n] = jnp.where(odd, bottom, top)
    total = dot_nt(
        jnp.concatenate([mixed[i] for i in range(rows)], axis=1), jnp.concatenate(grads, axis=1)
    )
    owners = partial.shape[0]
    own = chan // owners
    for owner in range(owners):
        partial[owner] = jnp.concatenate(
            [total[k * chan + owner * own : k * chan + (owner + 1) * own] for k in range(kernels)], axis=0
        ).astype(BF)


def band_sum(factor, parts, w_bwd, spread):
    owners, height, lanes = parts.shape
    total = parts[0].astype(F32)
    for owner in range(1, owners):
        total = total + parts[owner].astype(F32)
    total = jnp.concatenate([total * factor, jnp.zeros((lanes - height, lanes), F32)], axis=0)
    upper = total.astype(BF)
    lower = (total - upper.astype(F32)).astype(BF)
    dec = w_bwd[0]
    padded = dec.shape[1]
    result = dot_nt(dec, upper[:, :padded]) + dot_nt(dec, lower[:, :padded])
    per = spread.shape[1]
    for member in range(spread.shape[0]):
        spread[member] = result[member * per : (member + 1) * per].astype(BF)


def member_sum(parts, owned):
    kernels, own, width = owned.shape
    total = parts[0].astype(F32)
    for member in range(1, parts.shape[0]):
        total = total + parts[member].astype(F32)
    turned = total.T
    for k in range(kernels):
        owned[k] = turned[k * own : (k + 1) * own, :width]


def adjoint(rows, kernels, place, pred_grad, cross, chip, back, w_bwd, result):
    lon = pred_grad.shape[2]
    low, high = sides((place[0] & 1) == 1, cross, chip)
    wide = low + [pred_grad[i] for i in range(rows)] + high
    for i in range(rows):
        taps = dot_nn(jnp.concatenate(wide[i : i + REACH], axis=1), back[i]).astype(BF)
        total = dot_nn(w_bwd[0], wide[i + HALO])
        for k in range(kernels):
            total = total + dot_nn(w_bwd[k + 1], taps[:, k * lon : (k + 1) * lon])
        result[i] = total.astype(BF)


def cut(place, field, cross, chip, sems):
    rows = field.shape[0]
    odd = (place[0] & 1)
    far = (rows - HALO) * odd
    moves = [
        pltpu.make_async_copy(field.at[pl.ds(far, HALO)], cross, sems.at[0]),
        pltpu.make_async_copy(field.at[pl.ds(rows - HALO - far, HALO)], chip, sems.at[1]),
    ]
    for move in moves:
        move.start()
    for move in moves:
        move.wait()


def sides(odd, cross, chip):
    low = [jnp.where(odd, chip[n], cross[n]) for n in range(HALO)]
    high = [jnp.where(odd, cross[n], chip[n]) for n in range(HALO)]
    return low, high


def exchange(cross, chip, axis):
    count = lax.axis_size(axis)
    far = [(i, i + 1) for i in range(1, count - 1, 2)]
    near = [(i, i + 1) for i in range(0, count - 1, 2)]
    cross = lax.ppermute(cross, axis, far + [(b, a) for a, b in far])
    chip = lax.ppermute(chip, axis, near + [(b, a) for a, b in near])
    return cross, chip


def body(latent_fields, target_fields, filters, decoder, cycle_basis, cycle_offsets):
    field = latent_fields[0]
    rows, chan, lon = field.shape
    lat_count, kernels, taps = cycle_basis.shape
    variables = decoder.shape[1]
    members, bands = lax.axis_size("ens"), lax.axis_size("lat")
    per = 16
    padded = -(-variables // per) * per
    band = lax.axis_index("lat").astype(jnp.int32)
    place = band.reshape(1)
    area = jnp.asarray(np.cos(np.pi * (np.arange(lat_count) + 0.5) / lat_count - np.pi / 2), F32)
    dec_t = decoder.T
    basis = cycle_basis.transpose(2, 1, 0)
    offsets = cycle_offsets.T

    stay = functools.partial(pltpu.with_memory_space_constraint, memory_space=pltpu.HBM)
    hbm = pl.BlockSpec(memory_space=pltpu.HBM)
    edge = jax.ShapeDtypeStruct((HALO, chan, lon), BF)
    pair = pltpu.SemaphoreType.DMA((2,))
    cross, chip = call(cut, (edge, edge), [SMEM, hbm], 0, 500_000, [pair])(place, stay(field))
    cross, chip = exchange(cross, chip, "lat")
    ahead, w_fwd, held, near, dec_near = call(
        functools.partial(prepare_ahead, rows, taps, lat_count),
        (
            jax.ShapeDtypeStruct((rows, REACH * lon, kernels * lon), BF),
            jax.ShapeDtypeStruct((padded, (kernels + 1) * chan), BF),
            jax.ShapeDtypeStruct(filters.shape, BF),
            jax.ShapeDtypeStruct(field.shape, BF),
            jax.ShapeDtypeStruct(dec_t.shape, BF),
        ),
        [SMEM, SMEM, SMEM, hbm, hbm, hbm],
        30_000_000,
        2_000_000,
        [pltpu.SemaphoreType.DMA((3,))],
    )(place, stay(basis), stay(offsets), stay(filters), stay(dec_t), stay(field))
    back, w_bwd = call(
        functools.partial(prepare_back, rows, taps, lat_count),
        (
            jax.ShapeDtypeStruct((rows, REACH * lon, kernels * lon), BF),
            jax.ShapeDtypeStruct((kernels + 1, chan, padded), BF),
        ),
        [SMEM, SMEM, SMEM, VMEM, VMEM],
        50_000_000,
        2_000_000,
    )(place, stay(basis), stay(offsets), held, dec_near)
    packed, predicted, mixed = call(
        functools.partial(forward, rows, kernels),
        (
            jax.ShapeDtypeStruct((members, per, lon), BF),
            jax.ShapeDtypeStruct((rows, padded, lon), F32),
            jax.ShapeDtypeStruct((rows, kernels * chan, lon), BF),
        ),
        [SMEM] + [VMEM] * 5,
        450_000_000,
        3_000_000,
    )(place, near, cross, chip, ahead, w_fwd)
    visitors = lax.all_to_all(packed, "ens", 0, 0, tiled=True)
    sums = call(pairs, jax.ShapeDtypeStruct((members, per, lon), BF), [VMEM], 2_000_000, 200_000)(visitors)
    sums = lax.all_to_all(sums, "ens", 0, 0, tiled=True)
    own = chan // bands
    edge = jax.ShapeDtypeStruct((HALO, padded, lon), BF)
    pred_grad, cross, chip, partial = call(
        functools.partial(gradient, rows, kernels, members),
        (
            jax.ShapeDtypeStruct((rows, padded, lon), BF),
            edge,
            edge,
            jax.ShapeDtypeStruct((bands, kernels * own, lon), BF),
        ),
        [SMEM, SMEM] + [VMEM] * 4,
        80_000_000,
        1_200_000,
    )(place, area, sums, predicted, target_fields, mixed)
    parts = lax.all_to_all(partial, "lat", 0, 0, tiled=True)
    cross, chip = exchange(cross, chip, "lat")
    latent_grad = call(
        functools.partial(adjoint, rows, kernels),
        jax.ShapeDtypeStruct((rows, chan, lon), BF),
        [SMEM] + [VMEM] * 5,
        200_000_000,
        2_000_000,
    )(place, pred_grad, cross, chip, back, w_bwd)
    parts, latent_grad = lax.optimization_barrier((parts, latent_grad))
    factor = 1.0 / math.sqrt(members * lat_count * lon)
    width = chan // members
    spread = call(
        functools.partial(band_sum, factor),
        jax.ShapeDtypeStruct((members, width, lon), BF),
        [VMEM] * 2,
        20_000_000,
        400_000,
    )(parts, w_bwd)
    spread = lax.all_to_all(spread, "ens", 0, 0, tiled=True)
    owned = call(
        member_sum, jax.ShapeDtypeStruct((kernels, own, width), F32), [VMEM], 100_000, 150_000
    )(spread)
    return latent_grad[None], owned.transpose(1, 0, 2)


def solution(mesh):
    placed = (P("ens", "lat", None, None), P("lat", None, None), P(), P(), P(), P())
    return jax.shard_map(
        body,
        mesh=mesh,
        in_specs=placed,
        out_specs=(P("ens", "lat", None, None), P("lat", None, "ens")),
        check_vma=False,
    )
```

```python
import functools
import math

import jax
import jax.numpy as jnp
import numpy as np
from jax import lax
from jax.experimental import pallas as pl
from jax.experimental.pallas import tpu as pltpu
from jax.sharding import PartitionSpec as P

HALO = 2
SIDE = 2
REACH = 2 * HALO + 1
DELTA = 0.25
BF = jnp.bfloat16
F32 = jnp.float32
VMEM = pl.BlockSpec(memory_space=pltpu.VMEM)
SMEM = pl.BlockSpec(memory_space=pltpu.SMEM)


def smooth_slope(differ):
    return differ * lax.rsqrt(differ * differ + DELTA * DELTA)


def dot_nn(a, b):
    return lax.dot_general(a, b, (((1,), (0,)), ((), ())), preferred_element_type=F32)


def dot_nt(a, b):
    return lax.dot_general(a, b, (((1,), (1,)), ((), ())), preferred_element_type=F32)


def dot_tn(a, b):
    return lax.dot_general(a, b, (((0,), (0,)), ((), ())), preferred_element_type=F32)


def dot_tt(a, b):
    return lax.dot_general(a, b, (((0,), (1,)), ((), ())), preferred_element_type=F32)


def call(kernel, out, specs, flops, moved, scratch=()):
    many = isinstance(out, (tuple, list))
    return pl.pallas_call(
        kernel,
        out_shape=out,
        in_specs=specs,
        out_specs=tuple([VMEM] * len(out)) if many else VMEM,
        scratch_shapes=list(scratch),
        compiler_params=pltpu.CompilerParams(vmem_limit_bytes=32 * 2**20),
        cost_estimate=pl.CostEstimate(flops=flops, bytes_accessed=moved, transcendentals=0),
    )


def tap_block(lat_count, lag, place, rows, basis, offsets, source, step, store):
    kernels, lon = basis.shape[1], lag.shape[0]
    cycle = place[0] * rows + source
    inside = jnp.logical_and(cycle >= 0, cycle < lat_count)
    cycle = jnp.clip(cycle, 0, lat_count - 1)
    one, two = SIDE * step, SIDE * step + 1
    off_one, off_two = offsets[one, cycle], offsets[two, cycle]
    mask_one = lag == (off_one & (lon - 1))
    mask_two = lag == (off_two & (lon - 1))
    for k in range(kernels):
        weight_one = jnp.where(inside, basis[one, k, cycle], 0.0)
        weight_two = jnp.where(inside, basis[two, k, cycle], 0.0)
        weight_two = weight_two + jnp.where(off_one == off_two, weight_one, 0.0)
        value = jnp.where(mask_two, weight_two, jnp.where(mask_one, weight_one, 0.0))
        store[:, k * lon : (k + 1) * lon] = value.astype(BF)


def edge_taps(rows):
    outside = list(range(-HALO, 0)) + list(range(rows, rows + HALO))
    return [(at, step) for at in outside for step in range(REACH) if 0 <= at + step - HALO < rows]


def lags(lon):
    return (lax.broadcasted_iota(jnp.int32, (lon, lon), 0) - lax.broadcasted_iota(jnp.int32, (lon, lon), 1)) & (lon - 1)


def padded_rows(dec_t, padded):
    rows, chan = dec_t.shape
    return jnp.concatenate([dec_t[...].astype(F32), jnp.zeros((padded - rows, chan), F32)], axis=0).astype(BF)


def prepare(
    rows, lat_count, place, basis, offsets, filters, dec_in, field, ahead, edge, w_fwd, near, held, dec_t, sems
):
    moves = ((filters, held), (dec_in, dec_t), (field, near))
    moves = [pltpu.make_async_copy(source, target, sems.at[n]) for n, (source, target) in enumerate(moves)]
    for move in moves:
        move.start()
    lon = ahead.shape[1] // REACH
    lag = lags(lon)
    for row in range(rows):
        for step in range(REACH):
            tap_block(lat_count, lag, place, rows, basis, offsets, row, step, ahead.at[row, step * lon : (step + 1) * lon])
    for n, (at, step) in enumerate(edge_taps(rows)):
        tap_block(lat_count, lag, place, rows, basis, offsets, at, step, edge.at[n])
    kernels, chan = held.shape[:2]
    for move in moves:
        move.wait()
    dec = padded_rows(dec_t, w_fwd.shape[0])
    w_fwd[:, :chan] = dec
    for k in range(kernels):
        w_fwd[:, (k + 1) * chan : (k + 2) * chan] = dot_nt(dec, held[k]).astype(BF)


def forward(rows, kernels, place, field, cross, chip, ahead, w_fwd, packed, predicted, mixed):
    lon = field.shape[2]
    chan = field.shape[1]
    low, high = sides((place[0] & 1) == 1, cross, chip)
    wide = low + [field[i] for i in range(rows)] + high
    per = packed.shape[1]
    padded = predicted.shape[1]
    pieces = padded // per
    for i in range(rows):
        source = jnp.concatenate(wide[i : i + REACH], axis=1)
        taps = dot_nn(source, ahead[i]).astype(BF)
        for k in range(kernels):
            mixed[i, k * chan : (k + 1) * chan, :] = taps[:, k * lon : (k + 1) * lon]
        stack = jnp.concatenate([wide[i + HALO]] + [taps[:, k * lon : (k + 1) * lon] for k in range(kernels)], axis=0)
        pred = dot_nn(w_fwd[...], stack)
        predicted[i] = pred
        rounded = pred.astype(BF)
        for q in range(pieces):
            packed[i * pieces + q] = rounded[q * per : (q + 1) * per]
    for q in range(rows * pieces, packed.shape[0]):
        packed[q] = jnp.zeros(packed.shape[1:], BF)


def pairs(visitors, sums):
    members, height, _ = visitors.shape
    pieces = []
    for start in range(0, height, 8):
        values = [visitors[m].astype(F32)[start : start + 8] for m in range(members)]
        totals = [None] * members
        for m in range(members):
            for n in range(m + 1, members):
                slope = smooth_slope(values[m] - values[n])
                totals[m] = slope if totals[m] is None else totals[m] + slope
                totals[n] = -slope if totals[n] is None else totals[n] - slope
        pieces.append(totals)
    for m in range(members):
        sums[m] = jnp.concatenate([totals[m] for totals in pieces], axis=0).astype(BF)


def gradient(rows, kernels, members, place, area, sums, predicted, target, mixed, pred_grad, cross, chip, partial):
    variables = target.shape[1]
    padded = predicted.shape[1]
    per = sums.shape[1]
    pieces = padded // per
    lon = predicted.shape[2]
    chan = mixed.shape[1] // kernels
    grads, edges = [], []
    odd = (place[0] & 1) == 1
    for i in range(rows):
        pair_sum = jnp.concatenate([sums[i * pieces + q].astype(F32) for q in range(pieces)], axis=0)
        aim = jnp.concatenate([target[i].astype(F32), jnp.zeros((padded - variables, lon), F32)], axis=0)
        grad = area[place[0] * rows + i] * (smooth_slope(predicted[i] - aim) - pair_sum * (1.0 / (members - 1)))
        grad = grad.astype(BF)
        pred_grad[i] = grad
        edges.append(grad)
        grads.append(jnp.concatenate([grad, jnp.zeros((lon - padded, lon), BF)], axis=0))
    for n in range(HALO):
        top, bottom = edges[rows - HALO + n], edges[n]
        cross[n] = jnp.where(odd, top, bottom)
        chip[n] = jnp.where(odd, bottom, top)
    total = dot_nt(
        jnp.concatenate([mixed[i] for i in range(rows)], axis=1), jnp.concatenate(grads, axis=1)
    )
    owners = partial.shape[0]
    own = chan // owners
    for owner in range(owners):
        partial[owner] = jnp.concatenate(
            [total[k * chan + owner * own : k * chan + (owner + 1) * own] for k in range(kernels)], axis=0
        ).astype(BF)


def band_sum(factor, parts, w_fwd, spread):
    owners, height, lanes = parts.shape
    total = parts[0].astype(F32)
    for owner in range(1, owners):
        total = total + parts[owner].astype(F32)
    total = jnp.concatenate([total * factor, jnp.zeros((lanes - height, lanes), F32)], axis=0)
    upper = total.astype(BF)
    lower = (total - upper.astype(F32)).astype(BF)
    per = spread.shape[1]
    padded = w_fwd.shape[0]
    dec = w_fwd[:, : per * spread.shape[0]]
    result = dot_tt(dec, upper[:, :padded]) + dot_tt(dec, lower[:, :padded])
    for member in range(spread.shape[0]):
        spread[member] = result[member * per : (member + 1) * per].astype(BF)


def member_sum(parts, owned):
    kernels, own, width = owned.shape
    total = parts[0].astype(F32)
    for member in range(1, parts.shape[0]):
        total = total + parts[member].astype(F32)
    turned = total.T
    for k in range(kernels):
        owned[k] = turned[k * own : (k + 1) * own, :width]


def adjoint_own(rows, kernels, pred_grad, ahead, turned):
    lon = pred_grad.shape[2]
    for k in range(kernels):
        sums = [None] * rows
        for at in range(rows):
            least = HALO - at
            taps = ahead[at, least * lon : (least + rows) * lon, k * lon : (k + 1) * lon]
            found = dot_nt(pred_grad[at], taps)
            for row in range(rows):
                piece = found[:, row * lon : (row + 1) * lon]
                sums[row] = piece if sums[row] is None else sums[row] + piece
        for row in range(rows):
            turned[k, :, row * lon : (row + 1) * lon] = sums[row]


def adjoint_rest(rows, kernels, place, pred_grad, cross, chip, turned, edge, w_fwd, result):
    lon = pred_grad.shape[2]
    chan = result.shape[1]
    low, high = sides((place[0] & 1) == 1, cross, chip)
    outer = dict(enumerate(low, -HALO)) | dict(enumerate(high, rows))
    total = dot_tn(w_fwd[:, :chan], jnp.concatenate([pred_grad[i] for i in range(rows)], axis=1))
    for k in range(kernels):
        sums = [turned[k, :, row * lon : (row + 1) * lon] for row in range(rows)]
        for n, (at, step) in enumerate(edge_taps(rows)):
            row = at + step - HALO
            sums[row] = sums[row] + dot_nt(outer[at], edge[n, :, k * lon : (k + 1) * lon])
        taps = jnp.concatenate(sums, axis=1).astype(BF)
        total = total + dot_tn(w_fwd[:, (k + 1) * chan : (k + 2) * chan], taps)
    for i in range(rows):
        result[i] = total[:, i * lon : (i + 1) * lon].astype(BF)


def cut(place, field, cross, chip, sems):
    rows = field.shape[0]
    odd = (place[0] & 1)
    far = (rows - HALO) * odd
    moves = [
        pltpu.make_async_copy(field.at[pl.ds(far, HALO)], cross, sems.at[0]),
        pltpu.make_async_copy(field.at[pl.ds(rows - HALO - far, HALO)], chip, sems.at[1]),
    ]
    for move in moves:
        move.start()
    for move in moves:
        move.wait()


def sides(odd, cross, chip):
    low = [jnp.where(odd, chip[n], cross[n]) for n in range(HALO)]
    high = [jnp.where(odd, cross[n], chip[n]) for n in range(HALO)]
    return low, high


def exchange(cross, chip, axis):
    count = lax.axis_size(axis)
    far = [(i, i + 1) for i in range(1, count - 1, 2)]
    near = [(i, i + 1) for i in range(0, count - 1, 2)]
    cross = lax.ppermute(cross, axis, far + [(b, a) for a, b in far])
    chip = lax.ppermute(chip, axis, near + [(b, a) for a, b in near])
    return cross, chip


def body(latent_fields, target_fields, filters, decoder, cycle_basis, cycle_offsets):
    field = latent_fields[0]
    rows, chan, lon = field.shape
    lat_count, kernels, taps = cycle_basis.shape
    variables = decoder.shape[1]
    members, bands = lax.axis_size("ens"), lax.axis_size("lat")
    per = 16
    padded = -(-variables // per) * per
    band = lax.axis_index("lat").astype(jnp.int32)
    place = band.reshape(1)
    area = jnp.asarray(np.cos(np.pi * (np.arange(lat_count) + 0.5) / lat_count - np.pi / 2), F32)
    dec_t = decoder.T
    basis = cycle_basis.transpose(2, 1, 0)
    offsets = cycle_offsets.T

    stay = functools.partial(pltpu.with_memory_space_constraint, memory_space=pltpu.HBM)
    hbm = pl.BlockSpec(memory_space=pltpu.HBM)
    edge = jax.ShapeDtypeStruct((HALO, chan, lon), BF)
    pair = pltpu.SemaphoreType.DMA((2,))
    cross, chip = call(cut, (edge, edge), [SMEM, hbm], 0, 500_000, [pair])(place, stay(field))
    cross, chip = exchange(cross, chip, "lat")
    ahead, tap_edge, w_fwd, near = call(
        functools.partial(prepare, rows, lat_count),
        (
            jax.ShapeDtypeStruct((rows, REACH * lon, kernels * lon), BF),
            jax.ShapeDtypeStruct((len(edge_taps(rows)), lon, kernels * lon), BF),
            jax.ShapeDtypeStruct((padded, (kernels + 1) * chan), BF),
            jax.ShapeDtypeStruct(field.shape, BF),
        ),
        [SMEM, SMEM, SMEM, hbm, hbm, hbm],
        30_000_000,
        2_000_000,
        [pltpu.VMEM(filters.shape, BF), pltpu.VMEM(dec_t.shape, BF), pltpu.SemaphoreType.DMA((3,))],
    )(place, stay(basis), stay(offsets), stay(filters), stay(dec_t), stay(field))
    packed, predicted, mixed = call(
        functools.partial(forward, rows, kernels),
        (
            jax.ShapeDtypeStruct((members, per, lon), BF),
            jax.ShapeDtypeStruct((rows, padded, lon), F32),
            jax.ShapeDtypeStruct((rows, kernels * chan, lon), BF),
        ),
        [SMEM] + [VMEM] * 5,
        450_000_000,
        3_000_000,
    )(place, near, cross, chip, ahead, w_fwd)
    visitors = lax.all_to_all(packed, "ens", 0, 0, tiled=True)
    sums = call(pairs, jax.ShapeDtypeStruct((members, per, lon), BF), [VMEM], 2_000_000, 200_000)(visitors)
    sums = lax.all_to_all(sums, "ens", 0, 0, tiled=True)
    own = chan // bands
    edge = jax.ShapeDtypeStruct((HALO, padded, lon), BF)
    pred_grad, cross, chip, partial = call(
        functools.partial(gradient, rows, kernels, members),
        (
            jax.ShapeDtypeStruct((rows, padded, lon), BF),
            edge,
            edge,
            jax.ShapeDtypeStruct((bands, kernels * own, lon), BF),
        ),
        [SMEM, SMEM] + [VMEM] * 4,
        80_000_000,
        1_200_000,
    )(place, area, sums, predicted, target_fields, mixed)
    parts = lax.all_to_all(partial, "lat", 0, 0, tiled=True)
    cross, chip = exchange(cross, chip, "lat")
    turned = call(
        functools.partial(adjoint_own, rows, kernels),
        jax.ShapeDtypeStruct((kernels, padded, rows * lon), F32),
        [VMEM] * 2,
        80_000_000,
        1_500_000,
    )(pred_grad, ahead)
    latent_grad = call(
        functools.partial(adjoint_rest, rows, kernels),
        jax.ShapeDtypeStruct((rows, chan, lon), BF),
        [SMEM] + [VMEM] * 6,
        150_000_000,
        1_500_000,
    )(place, pred_grad, cross, chip, turned, tap_edge, w_fwd)
    parts, latent_grad = lax.optimization_barrier((parts, latent_grad))
    factor = 1.0 / math.sqrt(members * lat_count * lon)
    width = chan // members
    spread = call(
        functools.partial(band_sum, factor),
        jax.ShapeDtypeStruct((members, width, lon), BF),
        [VMEM] * 2,
        20_000_000,
        400_000,
    )(parts, w_fwd)
    spread = lax.all_to_all(spread, "ens", 0, 0, tiled=True)
    owned = call(
        member_sum, jax.ShapeDtypeStruct((kernels, own, width), F32), [VMEM], 100_000, 150_000
    )(spread)
    return latent_grad[None], owned.transpose(1, 0, 2)


def solution(mesh):
    placed = (P("ens", "lat", None, None), P("lat", None, None), P(), P(), P(), P())
    return jax.shard_map(
        body,
        mesh=mesh,
        in_specs=placed,
        out_specs=(P("ens", "lat", None, None), P("lat", None, "ens")),
        check_vma=False,
    )
```

```python
import functools
import math

import jax
import jax.numpy as jnp
import numpy as np
from jax import lax
from jax.experimental import pallas as pl
from jax.experimental.pallas import tpu as pltpu
from jax.sharding import PartitionSpec as P

HALO = 2
SIDE = 2
REACH = 2 * HALO + 1
DELTA = 0.25
BF = jnp.bfloat16
F32 = jnp.float32
VMEM = pl.BlockSpec(memory_space=pltpu.VMEM)
SMEM = pl.BlockSpec(memory_space=pltpu.SMEM)


def smooth_slope(differ):
    return differ * lax.rsqrt(differ * differ + DELTA * DELTA)


def dot_nn(a, b):
    return lax.dot_general(a, b, (((1,), (0,)), ((), ())), preferred_element_type=F32)


def dot_nt(a, b):
    return lax.dot_general(a, b, (((1,), (1,)), ((), ())), preferred_element_type=F32)


def call(kernel, out, specs, flops, moved, scratch=()):
    many = isinstance(out, (tuple, list))
    return pl.pallas_call(
        kernel,
        out_shape=out,
        in_specs=specs,
        out_specs=tuple([VMEM] * len(out)) if many else VMEM,
        scratch_shapes=list(scratch),
        compiler_params=pltpu.CompilerParams(vmem_limit_bytes=32 * 2**20),
        cost_estimate=pl.CostEstimate(flops=flops, bytes_accessed=moved, transcendentals=0),
    )


def tap_block(lat_count, lag, place, rows, basis, offsets, source, step, store):
    kernels, lon = basis.shape[1], lag.shape[0]
    cycle = place[0] * rows + source
    inside = jnp.logical_and(cycle >= 0, cycle < lat_count)
    cycle = jnp.clip(cycle, 0, lat_count - 1)
    one, two = SIDE * step, SIDE * step + 1
    off_one, off_two = offsets[one, cycle], offsets[two, cycle]
    mask_one = lag == (off_one & (lon - 1))
    mask_two = lag == (off_two & (lon - 1))
    for k in range(kernels):
        weight_one = jnp.where(inside, basis[one, k, cycle], 0.0)
        weight_two = jnp.where(inside, basis[two, k, cycle], 0.0)
        weight_two = weight_two + jnp.where(off_one == off_two, weight_one, 0.0)
        value = jnp.where(mask_two, weight_two, jnp.where(mask_one, weight_one, 0.0))
        store[:, k * lon : (k + 1) * lon] = value.astype(BF)


def edge_taps(rows):
    outside = list(range(-HALO, 0)) + list(range(rows, rows + HALO))
    return [(at, step) for at in outside for step in range(REACH) if 0 <= at + step - HALO < rows]


def lags(lon):
    return (lax.broadcasted_iota(jnp.int32, (lon, lon), 0) - lax.broadcasted_iota(jnp.int32, (lon, lon), 1)) & (lon - 1)


def padded_rows(dec_t, padded):
    rows, chan = dec_t.shape
    return jnp.concatenate([dec_t[...].astype(F32), jnp.zeros((padded - rows, chan), F32)], axis=0).astype(BF)


def prepare(
    rows, lat_count, place, basis, offsets, filters, dec_in, field, ahead, edge, w_fwd, w_bwd, near, held, dec_t, sems
):
    moves = ((filters, held), (dec_in, dec_t), (field, near))
    moves = [pltpu.make_async_copy(source, target, sems.at[n]) for n, (source, target) in enumerate(moves)]
    for move in moves:
        move.start()
    lon = ahead.shape[1] // REACH
    lag = lags(lon)
    for row in range(rows):
        for step in range(REACH):
            tap_block(lat_count, lag, place, rows, basis, offsets, row, step, ahead.at[row, step * lon : (step + 1) * lon])
    for n, (at, step) in enumerate(edge_taps(rows)):
        tap_block(lat_count, lag, place, rows, basis, offsets, at, step, edge.at[n])
    kernels, chan = held.shape[:2]
    for move in moves:
        move.wait()
    dec = padded_rows(dec_t, w_fwd.shape[0])
    w_fwd[:, :chan] = dec
    for k in range(kernels):
        w_fwd[:, (k + 1) * chan : (k + 2) * chan] = dot_nt(dec, held[k]).astype(BF)
        w_bwd[k + 1] = dot_nt(held[k], dec).astype(BF)
    square = (chan, chan)
    unit = lax.broadcasted_iota(jnp.int32, square, 0) == lax.broadcasted_iota(jnp.int32, square, 1)
    w_bwd[0] = dot_nt(jnp.where(unit, 1.0, 0.0).astype(BF), dec).astype(BF)


def forward(rows, kernels, place, field, cross, chip, ahead, w_fwd, packed, predicted, mixed):
    lon = field.shape[2]
    chan = field.shape[1]
    low, high = sides((place[0] & 1) == 1, cross, chip)
    wide = low + [field[i] for i in range(rows)] + high
    per = packed.shape[1]
    padded = predicted.shape[1]
    pieces = padded // per
    for i in range(rows):
        source = jnp.concatenate(wide[i : i + REACH], axis=1)
        taps = dot_nn(source, ahead[i]).astype(BF)
        for k in range(kernels):
            mixed[i, k * chan : (k + 1) * chan, :] = taps[:, k * lon : (k + 1) * lon]
        stack = jnp.concatenate([wide[i + HALO]] + [taps[:, k * lon : (k + 1) * lon] for k in range(kernels)], axis=0)
        pred = dot_nn(w_fwd[...], stack)
        predicted[i] = pred
        rounded = pred.astype(BF)
        for q in range(pieces):
            packed[i * pieces + q] = rounded[q * per : (q + 1) * per]
    for q in range(rows * pieces, packed.shape[0]):
        packed[q] = jnp.zeros(packed.shape[1:], BF)


def pairs(visitors, sums):
    members, height, _ = visitors.shape
    pieces = []
    for start in range(0, height, 8):
        values = [visitors[m].astype(F32)[start : start + 8] for m in range(members)]
        totals = [None] * members
        for m in range(members):
            for n in range(m + 1, members):
                slope = smooth_slope(values[m] - values[n])
                totals[m] = slope if totals[m] is None else totals[m] + slope
                totals[n] = -slope if totals[n] is None else totals[n] - slope
        pieces.append(totals)
    for m in range(members):
        sums[m] = jnp.concatenate([totals[m] for totals in pieces], axis=0).astype(BF)


def gradient(rows, kernels, members, place, area, sums, predicted, target, mixed, pred_grad, cross, chip, partial):
    variables = target.shape[1]
    padded = predicted.shape[1]
    per = sums.shape[1]
    pieces = padded // per
    lon = predicted.shape[2]
    chan = mixed.shape[1] // kernels
    grads, edges = [], []
    odd = (place[0] & 1) == 1
    for i in range(rows):
        pair_sum = jnp.concatenate([sums[i * pieces + q].astype(F32) for q in range(pieces)], axis=0)
        aim = jnp.concatenate([target[i].astype(F32), jnp.zeros((padded - variables, lon), F32)], axis=0)
        grad = area[place[0] * rows + i] * (smooth_slope(predicted[i] - aim) - pair_sum * (1.0 / (members - 1)))
        grad = grad.astype(BF)
        pred_grad[i] = grad
        edges.append(grad)
        grads.append(jnp.concatenate([grad, jnp.zeros((lon - padded, lon), BF)], axis=0))
    for n in range(HALO):
        top, bottom = edges[rows - HALO + n], edges[n]
        cross[n] = jnp.where(odd, top, bottom)
        chip[n] = jnp.where(odd, bottom, top)
    total = dot_nt(
        jnp.concatenate([mixed[i] for i in range(rows)], axis=1), jnp.concatenate(grads, axis=1)
    )
    first, second, third = [total[k * chan : (k + 1) * chan] for k in range(kernels)]
    lane = lax.broadcasted_iota(jnp.int32, first.shape, 1)
    spare = lon - variables
    upper = jnp.where(lane < variables, first, pltpu.roll(third, variables, 1))
    tail = jnp.where(lane < 2 * variables - spare, pltpu.roll(third, variables - spare, 1), 0.0)
    lower = jnp.where(lane < variables, second, tail)
    owners = partial.shape[0]
    own = chan // owners
    for owner in range(owners):
        mine = slice(owner * own, (owner + 1) * own)
        partial[owner] = jnp.concatenate([upper[mine], lower[mine]], axis=0).astype(BF)


def band_sum(factor, variables, parts, w_bwd, spread):
    owners, height, lon = parts.shape
    total = parts[0].astype(F32)
    for owner in range(1, owners):
        total = total + parts[owner].astype(F32)
    total = total * factor
    own = height // 2
    spare = lon - variables
    lane = lax.broadcasted_iota(jnp.int32, (own, lon), 1)
    front = pltpu.roll(total[:own], lon - variables, 1)
    rest = pltpu.roll(total[own:], lon + spare - variables, 1)
    third = jnp.where(lane < spare, front, jnp.where(lane < variables, rest, 0.0))
    wide = lax.broadcasted_iota(jnp.int32, total.shape, 1)
    total = jnp.where(wide < variables, total, 0.0)
    total = jnp.concatenate([total, third, jnp.zeros((lon - height - own, lon), F32)], axis=0)
    upper = total.astype(BF)
    lower = (total - upper.astype(F32)).astype(BF)
    dec = w_bwd[0]
    padded = dec.shape[1]
    result = dot_nt(dec, upper[:, :padded]) + dot_nt(dec, lower[:, :padded])
    per = spread.shape[1]
    for member in range(spread.shape[0]):
        spread[member] = result[member * per : (member + 1) * per].astype(BF)


def member_sum(parts, owned):
    kernels, own, width = owned.shape
    total = parts[0].astype(F32)
    for member in range(1, parts.shape[0]):
        total = total + parts[member].astype(F32)
    turned = total.T
    for k in range(kernels):
        owned[k] = turned[k * own : (k + 1) * own, :width]


def adjoint_own(rows, kernels, pred_grad, ahead, turned):
    lon = pred_grad.shape[2]
    for k in range(kernels):
        sums = [None] * rows
        for at in range(rows):
            least = HALO - at
            taps = ahead[at, least * lon : (least + rows) * lon, k * lon : (k + 1) * lon]
            found = dot_nt(pred_grad[at], taps)
            for row in range(rows):
                piece = found[:, row * lon : (row + 1) * lon]
                sums[row] = piece if sums[row] is None else sums[row] + piece
        for row in range(rows):
            turned[k, :, row * lon : (row + 1) * lon] = sums[row]


def adjoint_rest(rows, kernels, place, pred_grad, cross, chip, turned, edge, w_bwd, result):
    lon = pred_grad.shape[2]
    low, high = sides((place[0] & 1) == 1, cross, chip)
    outer = dict(enumerate(low, -HALO)) | dict(enumerate(high, rows))
    total = dot_nn(w_bwd[0], jnp.concatenate([pred_grad[i] for i in range(rows)], axis=1))
    for k in range(kernels):
        sums = [turned[k, :, row * lon : (row + 1) * lon] for row in range(rows)]
        for n, (at, step) in enumerate(edge_taps(rows)):
            row = at + step - HALO
            sums[row] = sums[row] + dot_nt(outer[at], edge[n, :, k * lon : (k + 1) * lon])
        taps = jnp.concatenate(sums, axis=1).astype(BF)
        total = total + dot_nn(w_bwd[k + 1], taps)
    for i in range(rows):
        result[i] = total[:, i * lon : (i + 1) * lon].astype(BF)


def cut(place, field, cross, chip, sems):
    rows = field.shape[0]
    odd = (place[0] & 1)
    far = (rows - HALO) * odd
    moves = [
        pltpu.make_async_copy(field.at[pl.ds(far, HALO)], cross, sems.at[0]),
        pltpu.make_async_copy(field.at[pl.ds(rows - HALO - far, HALO)], chip, sems.at[1]),
    ]
    for move in moves:
        move.start()
    for move in moves:
        move.wait()


def sides(odd, cross, chip):
    low = [jnp.where(odd, chip[n], cross[n]) for n in range(HALO)]
    high = [jnp.where(odd, cross[n], chip[n]) for n in range(HALO)]
    return low, high


def exchange(cross, chip, axis):
    count = lax.axis_size(axis)
    far = [(i, i + 1) for i in range(1, count - 1, 2)]
    near = [(i, i + 1) for i in range(0, count - 1, 2)]
    cross = lax.ppermute(cross, axis, far + [(b, a) for a, b in far])
    chip = lax.ppermute(chip, axis, near + [(b, a) for a, b in near])
    return cross, chip


def body(latent_fields, target_fields, filters, decoder, cycle_basis, cycle_offsets):
    field = latent_fields[0]
    rows, chan, lon = field.shape
    lat_count, kernels, taps = cycle_basis.shape
    variables = decoder.shape[1]
    members, bands = lax.axis_size("ens"), lax.axis_size("lat")
    per = 16
    padded = -(-variables // per) * per
    band = lax.axis_index("lat").astype(jnp.int32)
    place = band.reshape(1)
    area = jnp.asarray(np.cos(np.pi * (np.arange(lat_count) + 0.5) / lat_count - np.pi / 2), F32)
    dec_t = decoder.T
    basis = cycle_basis.transpose(2, 1, 0)
    offsets = cycle_offsets.T

    stay = functools.partial(pltpu.with_memory_space_constraint, memory_space=pltpu.HBM)
    hbm = pl.BlockSpec(memory_space=pltpu.HBM)
    edge = jax.ShapeDtypeStruct((HALO, chan, lon), BF)
    pair = pltpu.SemaphoreType.DMA((2,))
    cross, chip = call(cut, (edge, edge), [SMEM, hbm], 0, 500_000, [pair])(place, stay(field))
    cross, chip = exchange(cross, chip, "lat")
    ahead, tap_edge, w_fwd, w_bwd, near = call(
        functools.partial(prepare, rows, lat_count),
        (
            jax.ShapeDtypeStruct((rows, REACH * lon, kernels * lon), BF),
            jax.ShapeDtypeStruct((len(edge_taps(rows)), lon, kernels * lon), BF),
            jax.ShapeDtypeStruct((padded, (kernels + 1) * chan), BF),
            jax.ShapeDtypeStruct((kernels + 1, chan, padded), BF),
            jax.ShapeDtypeStruct(field.shape, BF),
        ),
        [SMEM, SMEM, SMEM, hbm, hbm, hbm],
        30_000_000,
        2_000_000,
        [pltpu.VMEM(filters.shape, BF), pltpu.VMEM(dec_t.shape, BF), pltpu.SemaphoreType.DMA((3,))],
    )(place, stay(basis), stay(offsets), stay(filters), stay(dec_t), stay(field))
    packed, predicted, mixed = call(
        functools.partial(forward, rows, kernels),
        (
            jax.ShapeDtypeStruct((members, per, lon), BF),
            jax.ShapeDtypeStruct((rows, padded, lon), F32),
            jax.ShapeDtypeStruct((rows, kernels * chan, lon), BF),
        ),
        [SMEM] + [VMEM] * 5,
        450_000_000,
        3_000_000,
    )(place, near, cross, chip, ahead, w_fwd)
    visitors = lax.all_to_all(packed, "ens", 0, 0, tiled=True)
    sums = call(pairs, jax.ShapeDtypeStruct((members, per, lon), BF), [VMEM], 2_000_000, 200_000)(visitors)
    sums = lax.all_to_all(sums, "ens", 0, 0, tiled=True)
    own = chan // bands
    edge = jax.ShapeDtypeStruct((HALO, padded, lon), BF)
    pred_grad, cross, chip, partial = call(
        functools.partial(gradient, rows, kernels, members),
        (
            jax.ShapeDtypeStruct((rows, padded, lon), BF),
            edge,
            edge,
            jax.ShapeDtypeStruct((bands, 2 * own, lon), BF),
        ),
        [SMEM, SMEM] + [VMEM] * 4,
        80_000_000,
        1_200_000,
    )(place, area, sums, predicted, target_fields, mixed)
    parts = lax.all_to_all(partial, "lat", 0, 0, tiled=True)
    cross, chip = exchange(cross, chip, "lat")
    turned = call(
        functools.partial(adjoint_own, rows, kernels),
        jax.ShapeDtypeStruct((kernels, padded, rows * lon), F32),
        [VMEM] * 2,
        80_000_000,
        1_500_000,
    )(pred_grad, ahead)
    latent_grad = call(
        functools.partial(adjoint_rest, rows, kernels),
        jax.ShapeDtypeStruct((rows, chan, lon), BF),
        [SMEM] + [VMEM] * 6,
        150_000_000,
        1_500_000,
    )(place, pred_grad, cross, chip, turned, tap_edge, w_bwd)
    parts, latent_grad = lax.optimization_barrier((parts, latent_grad))
    factor = 1.0 / math.sqrt(members * lat_count * lon)
    width = chan // members
    spread = call(
        functools.partial(band_sum, factor, variables),
        jax.ShapeDtypeStruct((members, width, lon), BF),
        [VMEM] * 2,
        20_000_000,
        400_000,
    )(parts, w_bwd)
    spread = lax.all_to_all(spread, "ens", 0, 0, tiled=True)
    owned = call(
        member_sum, jax.ShapeDtypeStruct((kernels, own, width), F32), [VMEM], 100_000, 150_000
    )(spread)
    return latent_grad[None], owned.transpose(1, 0, 2)


def solution(mesh):
    placed = (P("ens", "lat", None, None), P("lat", None, None), P(), P(), P(), P())
    return jax.shard_map(
        body,
        mesh=mesh,
        in_specs=placed,
        out_specs=(P("ens", "lat", None, None), P("lat", None, "ens")),
        check_vma=False,
    )
```

```python
import functools
import math

import jax
import jax.numpy as jnp
import numpy as np
from jax import lax
from jax.experimental import pallas as pl
from jax.experimental.pallas import tpu as pltpu
from jax.sharding import Mesh, PartitionSpec as P

HALO = 2
SIDE = 2
REACH = 2 * HALO + 1
DELTA = 0.25
LAT = ("pair", "core")
BF = jnp.bfloat16
F32 = jnp.float32
VMEM = pl.BlockSpec(memory_space=pltpu.VMEM)
SMEM = pl.BlockSpec(memory_space=pltpu.SMEM)


def smooth_slope(differ):
    return differ * lax.rsqrt(differ * differ + DELTA * DELTA)


def dot_nn(a, b):
    return lax.dot_general(a, b, (((1,), (0,)), ((), ())), preferred_element_type=F32)


def dot_nt(a, b):
    return lax.dot_general(a, b, (((1,), (1,)), ((), ())), preferred_element_type=F32)


def call(kernel, out, specs, flops, moved, scratch=(), home=VMEM):
    many = isinstance(out, (tuple, list))
    return pl.pallas_call(
        kernel,
        out_shape=out,
        in_specs=specs,
        out_specs=tuple([home] * len(out)) if many else home,
        scratch_shapes=list(scratch),
        compiler_params=pltpu.CompilerParams(vmem_limit_bytes=32 * 2**20),
        cost_estimate=pl.CostEstimate(flops=flops, bytes_accessed=moved, transcendentals=0),
    )


def tap_block(lat_count, lag, band, rows, basis, offsets, source, step, put):
    kernels, lon = basis.shape[1], lag.shape[0]
    cycle = band * rows + source
    inside = jnp.logical_and(cycle >= 0, cycle < lat_count)
    cycle = jnp.clip(cycle, 0, lat_count - 1)
    one, two = SIDE * step, SIDE * step + 1
    off_one, off_two = offsets[one, cycle], offsets[two, cycle]
    mask_one = lag == (off_one & (lon - 1))
    mask_two = lag == (off_two & (lon - 1))
    for k in range(kernels):
        weight_one = jnp.where(inside, basis[one, k, cycle], 0.0)
        weight_two = jnp.where(inside, basis[two, k, cycle], 0.0)
        weight_two = weight_two + jnp.where(off_one == off_two, weight_one, 0.0)
        value = jnp.where(mask_two, weight_two, jnp.where(mask_one, weight_one, 0.0))
        put(k, value.astype(BF))


def edge_taps(rows, row):
    outside = list(range(-HALO, 0)) + list(range(rows, rows + HALO))
    return [(at, row - at + HALO) for at in outside if 0 <= row - at + HALO < REACH]


def lags(lon):
    return (lax.broadcasted_iota(jnp.int32, (lon, lon), 0) - lax.broadcasted_iota(jnp.int32, (lon, lon), 1)) & (lon - 1)


def padded_rows(dec_t, padded):
    rows, chan = dec_t.shape
    return jnp.concatenate([dec_t[...].astype(F32), jnp.zeros((padded - rows, chan), F32)], axis=0).astype(BF)


def prepare(
    rows, lat_count, place, basis, offsets, filters, dec_in, field, ahead, edge, w_fwd, w_bwd, near, held, dec_t, sems
):
    moves = ((filters, held), (dec_in, dec_t), (field, near))
    moves = [pltpu.make_async_copy(source, target, sems.at[n]) for n, (source, target) in enumerate(moves)]
    for move in moves:
        move.start()
    lon = ahead.shape[1] // REACH
    lag = lags(lon)
    def block(source, step, put):
        tap_block(lat_count, lag, place[0], rows, basis, offsets, source, step, put)

    def ahead_put(row, step):
        def put(k, value):
            ahead[row, step * lon : (step + 1) * lon, k * lon : (k + 1) * lon] = value

        return put

    def edge_put(row, slot):
        def put(k, value):
            edge[row, k * lon : (k + 1) * lon, slot * lon : (slot + 1) * lon] = value

        return put

    for row in range(rows):
        for step in range(REACH):
            block(row, step, ahead_put(row, step))
        for slot, (at, step) in enumerate(edge_taps(rows, row)):
            block(at, step, edge_put(row, slot))
    kernels, chan = held.shape[:2]
    padded = w_fwd.shape[0]
    for move in moves:
        move.wait()
    dec = padded_rows(dec_t, padded)

    def placed(k):
        above, below = jnp.zeros((k * padded, chan), BF), jnp.zeros(((kernels - k) * padded, chan), BF)
        return jnp.concatenate([part for part in (above, dec, below) if part.shape[0]], axis=0)

    square = (chan, chan)
    unit = lax.broadcasted_iota(jnp.int32, square, 0) == lax.broadcasted_iota(jnp.int32, square, 1)
    columns = dot_nt(jnp.where(unit, 1.0, 0.0).astype(BF), placed(0))
    w_fwd[:, :chan] = dec
    for k in range(kernels):
        w_fwd[:, (k + 1) * chan : (k + 2) * chan] = dot_nt(dec, held[k]).astype(BF)
        columns = columns + dot_nt(held[k], placed(k + 1))
    w_bwd[...] = columns.astype(BF)


def forward(rows, kernels, place, field, cross, chip, ahead, w_fwd, packed, predicted, mixed):
    lon = field.shape[2]
    chan = field.shape[1]
    low, high = sides((place[0] & 1) == 1, cross, chip)
    wide = low + [field[i] for i in range(rows)] + high
    per = packed.shape[1]
    padded = predicted.shape[1]
    pieces = padded // per
    for i in range(rows):
        source = jnp.concatenate(wide[i : i + REACH], axis=1)
        taps = dot_nn(source, ahead[i]).astype(BF)
        for k in range(kernels):
            mixed[i, k * chan : (k + 1) * chan, :] = taps[:, k * lon : (k + 1) * lon]
        stack = jnp.concatenate([wide[i + HALO]] + [taps[:, k * lon : (k + 1) * lon] for k in range(kernels)], axis=0)
        pred = dot_nn(w_fwd[...], stack)
        predicted[i] = pred
        rounded = pred.astype(BF)
        for q in range(pieces):
            packed[i * pieces + q] = rounded[q * per : (q + 1) * per]
    for q in range(rows * pieces, packed.shape[0]):
        packed[q] = jnp.zeros(packed.shape[1:], BF)


def pairs(visitors, sums):
    members, height, _ = visitors.shape
    pieces = []
    for start in range(0, height, 8):
        values = [visitors[m].astype(F32)[start : start + 8] for m in range(members)]
        totals = [None] * members
        for m in range(members):
            for n in range(m + 1, members):
                slope = smooth_slope(values[m] - values[n])
                totals[m] = slope if totals[m] is None else totals[m] + slope
                totals[n] = -slope if totals[n] is None else totals[n] - slope
        pieces.append(totals)
    for m in range(members):
        sums[m] = jnp.concatenate([totals[m] for totals in pieces], axis=0).astype(BF)


def gradient(rows, kernels, members, place, area, sums, predicted, target, mixed, pred_grad, cross, give, keep):
    variables = target.shape[1]
    padded = predicted.shape[1]
    per = sums.shape[1]
    pieces = padded // per
    lon = predicted.shape[2]
    chan = mixed.shape[1] // kernels
    grads, edges = [], []
    odd = (place[0] & 1) == 1
    for i in range(rows):
        pair_sum = jnp.concatenate([sums[i * pieces + q].astype(F32) for q in range(pieces)], axis=0)
        aim = jnp.concatenate([target[i].astype(F32), jnp.zeros((padded - variables, lon), F32)], axis=0)
        grad = area[place[0] * rows + i] * (smooth_slope(predicted[i] - aim) - pair_sum * (1.0 / (members - 1)))
        grad = grad.astype(BF)
        pred_grad[i] = grad
        edges.append(grad)
        grads.append(jnp.concatenate([grad, jnp.zeros((lon - padded, lon), BF)], axis=0))
    for n in range(HALO):
        top, bottom = edges[rows - HALO + n], edges[n]
        cross[n] = jnp.where(odd, top, bottom)
        near = jnp.where(odd, bottom, top)
        for q in range(pieces):
            give[n * pieces + q] = near[q * per : (q + 1) * per]
    total = dot_nt(
        jnp.concatenate([mixed[i] for i in range(rows)], axis=1), jnp.concatenate(grads, axis=1)
    )
    first, second, third = [total[k * chan : (k + 1) * chan] for k in range(kernels)]
    lane = lax.broadcasted_iota(jnp.int32, first.shape, 1)
    spare = lon - variables
    upper = jnp.where(lane < variables, first, pltpu.roll(third, variables, 1))
    tail = jnp.where(lane < 2 * variables - spare, pltpu.roll(third, variables - spare, 1), 0.0)
    lower = jnp.where(lane < variables, second, tail)
    owners = keep.shape[0]
    own = chan // (2 * owners)

    def chunk(owner):
        mine = slice(owner * own, (owner + 1) * own)
        return jnp.concatenate([upper[mine], lower[mine]], axis=0)

    for owner in range(owners):
        even, uneven = chunk(2 * owner), chunk(2 * owner + 1)
        keep[owner] = jnp.where(odd, uneven, even)
        give[HALO * pieces + owner] = jnp.where(odd, even, uneven).astype(BF)


def fold(got, keep, merged):
    owners = keep.shape[0]
    skip = got.shape[0] - owners
    for owner in range(owners):
        merged[owner] = (keep[owner] + got[skip + owner].astype(F32)).astype(BF)


def band_sum(factor, variables, padded, parts, w_bwd, spread):
    owners, height, lon = parts.shape
    total = parts[0].astype(F32)
    for owner in range(1, owners):
        total = total + parts[owner].astype(F32)
    total = total * factor
    own = height // 2
    spare = lon - variables
    lane = lax.broadcasted_iota(jnp.int32, (own, lon), 1)
    front = pltpu.roll(total[:own], lon - variables, 1)
    rest = pltpu.roll(total[own:], lon + spare - variables, 1)
    third = jnp.where(lane < spare, front, jnp.where(lane < variables, rest, 0.0))
    wide = lax.broadcasted_iota(jnp.int32, total.shape, 1)
    total = jnp.where(wide < variables, total, 0.0)
    total = jnp.concatenate([total, third, jnp.zeros((lon - height - own, lon), F32)], axis=0)
    upper = total.astype(BF)
    lower = (total - upper.astype(F32)).astype(BF)
    dec = w_bwd[:, :padded]
    result = dot_nt(dec, upper[:, :padded]) + dot_nt(dec, lower[:, :padded])
    per = spread.shape[1]
    for member in range(spread.shape[0]):
        spread[member] = result[member * per : (member + 1) * per].astype(BF)


def member_sum(parts, owned):
    kernels, own, width = owned.shape
    total = parts[0].astype(F32)
    for member in range(1, parts.shape[0]):
        total = total + parts[member].astype(F32)
    turned = total.T
    for k in range(kernels):
        owned[k] = turned[k * own : (k + 1) * own, :width]


def adjoint_own(rows, kernels, pred_grad, ahead, turned):
    lon = pred_grad.shape[2]
    for k in range(kernels):
        sums = [None] * rows
        for at in range(rows):
            least = HALO - at
            taps = ahead[at, least * lon : (least + rows) * lon, k * lon : (k + 1) * lon]
            found = dot_nt(pred_grad[at], taps)
            for row in range(rows):
                piece = found[:, row * lon : (row + 1) * lon]
                sums[row] = piece if sums[row] is None else sums[row] + piece
        for row in range(rows):
            turned[row, :, k * lon : (k + 1) * lon] = sums[row]


def adjoint_rest(rows, kernels, place, pred_grad, cross, got, turned, edge, w_bwd, result, buffer, sems):
    padded, lon = pred_grad.shape[1:]
    pieces = padded // got.shape[1]
    chip = [jnp.concatenate([got[n * pieces + q] for q in range(pieces)], axis=0) for n in range(HALO)]
    low, high = sides((place[0] & 1) == 1, cross, chip)
    outer = dict(enumerate(low, -HALO)) | dict(enumerate(high, rows))
    moves = []
    for row in range(rows):
        sources = jnp.concatenate([outer[at] for at, _ in edge_taps(rows, row)], axis=1)
        taps = (turned[row] + dot_nt(sources, edge[row])).astype(BF)
        stack = [pred_grad[row]] + [taps[:, k * lon : (k + 1) * lon] for k in range(kernels)]
        buffer[row] = dot_nn(w_bwd[...], jnp.concatenate(stack, axis=0)).astype(BF)
        moves.append(pltpu.make_async_copy(buffer.at[row], result.at[row], sems.at[row]))
        moves[-1].start()
    for move in moves:
        move.wait()


def cut(place, field, cross, chip, sems):
    rows = field.shape[0]
    odd = (place[0] & 1)
    far = (rows - HALO) * odd
    moves = [
        pltpu.make_async_copy(field.at[pl.ds(far, HALO)], cross, sems.at[0]),
        pltpu.make_async_copy(field.at[pl.ds(rows - HALO - far, HALO)], chip, sems.at[1]),
    ]
    for move in moves:
        move.start()
    for move in moves:
        move.wait()


def sides(odd, cross, chip):
    low = [jnp.where(odd, chip[n], cross[n]) for n in range(HALO)]
    high = [jnp.where(odd, cross[n], chip[n]) for n in range(HALO)]
    return low, high


def across(block, axes, start):
    count = lax.axis_size(axes)
    pairs_up = [(i, i + 1) for i in range(start, count - 1, 2)]
    return lax.ppermute(block, axes, pairs_up + [(b, a) for a, b in pairs_up])


def body(latent_fields, target_fields, filters, decoder, cycle_basis, cycle_offsets):
    field = latent_fields[0]
    rows, chan, lon = field.shape
    lat_count, kernels, taps = cycle_basis.shape
    variables = decoder.shape[1]
    members, bands = lax.axis_size("ens"), lax.axis_size(LAT)
    per = 16
    padded = -(-variables // per) * per
    band = lax.axis_index(LAT).astype(jnp.int32)
    place = band.reshape(1)
    area = jnp.asarray(np.cos(np.pi * (np.arange(lat_count) + 0.5) / lat_count - np.pi / 2), F32)
    dec_t = decoder.T
    basis = cycle_basis.transpose(2, 1, 0)
    offsets = cycle_offsets.T

    stay = functools.partial(pltpu.with_memory_space_constraint, memory_space=pltpu.HBM)
    hbm = pl.BlockSpec(memory_space=pltpu.HBM)
    edge = jax.ShapeDtypeStruct((HALO, chan, lon), BF)
    pair = pltpu.SemaphoreType.DMA((2,))
    cross, chip = call(cut, (edge, edge), [SMEM, hbm], 0, 500_000, [pair])(place, stay(field))
    cross, chip = across(cross, LAT, 1), across(chip, LAT, 0)
    ahead, tap_edge, w_fwd, w_bwd, near = call(
        functools.partial(prepare, rows, lat_count),
        (
            jax.ShapeDtypeStruct((rows, REACH * lon, kernels * lon), BF),
            jax.ShapeDtypeStruct((rows, kernels * lon, (REACH - rows) * lon), BF),
            jax.ShapeDtypeStruct((padded, (kernels + 1) * chan), BF),
            jax.ShapeDtypeStruct((chan, (kernels + 1) * padded), BF),
            jax.ShapeDtypeStruct(field.shape, BF),
        ),
        [SMEM, SMEM, SMEM, hbm, hbm, hbm],
        30_000_000,
        2_000_000,
        [pltpu.VMEM(filters.shape, BF), pltpu.VMEM(dec_t.shape, BF), pltpu.SemaphoreType.DMA((3,))],
    )(place, stay(basis), stay(offsets), stay(filters), stay(dec_t), stay(field))
    packed, predicted, mixed = call(
        functools.partial(forward, rows, kernels),
        (
            jax.ShapeDtypeStruct((members, per, lon), BF),
            jax.ShapeDtypeStruct((rows, padded, lon), F32),
            jax.ShapeDtypeStruct((rows, kernels * chan, lon), BF),
        ),
        [SMEM] + [VMEM] * 5,
        450_000_000,
        3_000_000,
    )(place, near, cross, chip, ahead, w_fwd)
    visitors = lax.all_to_all(packed, "ens", 0, 0, tiled=True)
    sums = call(pairs, jax.ShapeDtypeStruct((members, per, lon), BF), [VMEM], 2_000_000, 200_000)(visitors)
    sums = lax.all_to_all(sums, "ens", 0, 0, tiled=True)
    own = chan // bands
    pieces = padded // per
    owners = bands // 2
    pred_grad, cross, give, keep = call(
        functools.partial(gradient, rows, kernels, members),
        (
            jax.ShapeDtypeStruct((rows, padded, lon), BF),
            jax.ShapeDtypeStruct((HALO, padded, lon), BF),
            jax.ShapeDtypeStruct((HALO * pieces + owners, per, lon), BF),
            jax.ShapeDtypeStruct((owners, 2 * own, lon), F32),
        ),
        [SMEM, SMEM] + [VMEM] * 4,
        80_000_000,
        1_200_000,
    )(place, area, sums, predicted, target_fields, mixed)
    got = across(give, LAT, 0)
    turned = call(
        functools.partial(adjoint_own, rows, kernels),
        jax.ShapeDtypeStruct((rows, padded, kernels * lon), F32),
        [VMEM] * 2,
        80_000_000,
        1_500_000,
    )(pred_grad, ahead)
    got, turned = lax.optimization_barrier((got, turned))
    merged = call(fold, jax.ShapeDtypeStruct((owners, 2 * own, lon), BF), [VMEM] * 2, 100_000, 300_000)(got, keep)
    cross, merged = lax.optimization_barrier((cross, merged))
    parts = lax.all_to_all(merged, "pair", 0, 0, tiled=True)
    cross = across(cross, LAT, 1)
    latent_grad = call(
        functools.partial(adjoint_rest, rows, kernels),
        jax.ShapeDtypeStruct((rows, chan, lon), BF),
        [SMEM] + [VMEM] * 6,
        150_000_000,
        1_500_000,
        [pltpu.VMEM((rows, chan, lon), BF), pltpu.SemaphoreType.DMA((rows,))],
        hbm,
    )(place, pred_grad, cross, got, turned, tap_edge, w_bwd)
    parts, latent_grad = lax.optimization_barrier((parts, latent_grad))
    factor = 1.0 / math.sqrt(members * lat_count * lon)
    width = chan // members
    spread = call(
        functools.partial(band_sum, factor, variables, padded),
        jax.ShapeDtypeStruct((members, width, lon), BF),
        [VMEM] * 2,
        20_000_000,
        400_000,
    )(parts, w_bwd)
    spread = lax.all_to_all(spread, "ens", 0, 0, tiled=True)
    owned = call(
        member_sum, jax.ShapeDtypeStruct((kernels, own, width), F32), [VMEM], 100_000, 150_000
    )(spread)
    return latent_grad[None], owned.transpose(1, 0, 2)


def solution(mesh):
    members, bands = mesh.devices.shape
    split = Mesh(mesh.devices.reshape(members, bands // 2, 2), ("ens", "pair", "core"))
    placed = (P("ens", LAT, None, None), P(LAT, None, None), P(), P(), P(), P())
    return jax.shard_map(
        body,
        mesh=split,
        in_specs=placed,
        out_specs=(P("ens", LAT, None, None), P(LAT, None, "ens")),
        check_vma=False,
    )
```

```python
import functools
import math

import jax
import jax.numpy as jnp
import numpy as np
from jax import lax
from jax.experimental import pallas as pl
from jax.experimental.pallas import tpu as pltpu
from jax.sharding import Mesh, PartitionSpec as P

HALO = 2
SIDE = 2
REACH = 2 * HALO + 1
DELTA = 0.25
LAT = ("pair", "core")
BF = jnp.bfloat16
F32 = jnp.float32
VMEM = pl.BlockSpec(memory_space=pltpu.VMEM)
SMEM = pl.BlockSpec(memory_space=pltpu.SMEM)


def smooth_slope(differ):
    return differ * lax.rsqrt(differ * differ + DELTA * DELTA)


def dot_nn(a, b):
    return lax.dot_general(a, b, (((1,), (0,)), ((), ())), preferred_element_type=F32)


def dot_nt(a, b):
    return lax.dot_general(a, b, (((1,), (1,)), ((), ())), preferred_element_type=F32)


def call(kernel, out, specs, flops, moved, scratch=(), home=VMEM):
    many = isinstance(out, (tuple, list))
    return pl.pallas_call(
        kernel,
        out_shape=out,
        in_specs=specs,
        out_specs=tuple([home] * len(out)) if many else home,
        scratch_shapes=list(scratch),
        compiler_params=pltpu.CompilerParams(vmem_limit_bytes=32 * 2**20),
        cost_estimate=pl.CostEstimate(flops=flops, bytes_accessed=moved, transcendentals=0),
    )


def tap_block(lat_count, lag, band, rows, basis, offsets, source, step, put):
    kernels, lon = basis.shape[1], lag.shape[0]
    cycle = band * rows + source
    inside = jnp.logical_and(cycle >= 0, cycle < lat_count)
    cycle = jnp.clip(cycle, 0, lat_count - 1)
    one, two = SIDE * step, SIDE * step + 1
    off_one, off_two = offsets[one, cycle], offsets[two, cycle]
    mask_one = lag == (off_one & (lon - 1))
    mask_two = lag == (off_two & (lon - 1))
    for k in range(kernels):
        weight_one = jnp.where(inside, basis[one, k, cycle], 0.0)
        weight_two = jnp.where(inside, basis[two, k, cycle], 0.0)
        weight_two = weight_two + jnp.where(off_one == off_two, weight_one, 0.0)
        value = jnp.where(mask_two, weight_two, jnp.where(mask_one, weight_one, 0.0))
        put(k, value.astype(BF))


def edge_taps(rows, row):
    outside = list(range(-HALO, 0)) + list(range(rows, rows + HALO))
    return [(at, row - at + HALO) for at in outside if 0 <= row - at + HALO < REACH]


def lags(lon):
    return (lax.broadcasted_iota(jnp.int32, (lon, lon), 0) - lax.broadcasted_iota(jnp.int32, (lon, lon), 1)) & (lon - 1)


def padded_rows(dec_t, padded):
    rows, chan = dec_t.shape
    return jnp.concatenate([dec_t[...].astype(F32), jnp.zeros((padded - rows, chan), F32)], axis=0).astype(BF)


def prepare(
    rows, lat_count, place, basis, offsets, filters, dec_in, field, ahead, edge, w_fwd, w_bwd, near, held, dec_t, sems
):
    moves = ((filters, held), (dec_in, dec_t), (field, near))
    moves = [pltpu.make_async_copy(source, target, sems.at[n]) for n, (source, target) in enumerate(moves)]
    for move in moves:
        move.start()
    lon = ahead.shape[1] // REACH
    lag = lags(lon)
    def block(source, step, put):
        tap_block(lat_count, lag, place[0], rows, basis, offsets, source, step, put)

    def ahead_put(row, step):
        def put(k, value):
            ahead[row, step * lon : (step + 1) * lon, k * lon : (k + 1) * lon] = value

        return put

    def edge_put(row, slot):
        def put(k, value):
            edge[row, k * lon : (k + 1) * lon, slot * lon : (slot + 1) * lon] = value

        return put

    for row in range(rows):
        for step in range(REACH):
            block(row, step, ahead_put(row, step))
        for slot, (at, step) in enumerate(edge_taps(rows, row)):
            block(at, step, edge_put(row, slot))
    kernels, chan = held.shape[:2]
    padded = w_fwd.shape[0]
    for move in moves:
        move.wait()
    dec = padded_rows(dec_t, padded)

    def placed(k):
        above, below = jnp.zeros((k * padded, chan), BF), jnp.zeros(((kernels - k) * padded, chan), BF)
        return jnp.concatenate([part for part in (above, dec, below) if part.shape[0]], axis=0)

    square = (chan, chan)
    unit = lax.broadcasted_iota(jnp.int32, square, 0) == lax.broadcasted_iota(jnp.int32, square, 1)
    columns = dot_nt(jnp.where(unit, 1.0, 0.0).astype(BF), placed(0))
    w_fwd[:, :chan] = dec
    for k in range(kernels):
        w_fwd[:, (k + 1) * chan : (k + 2) * chan] = dot_nt(dec, held[k]).astype(BF)
        columns = columns + dot_nt(held[k], placed(k + 1))
    w_bwd[...] = columns.astype(BF)


def forward(rows, kernels, place, field, cross, chip, ahead, w_fwd, packed, predicted, mixed):
    lon = field.shape[2]
    chan = field.shape[1]
    low, high = sides((place[0] & 1) == 1, cross, chip)
    wide = low + [field[i] for i in range(rows)] + high
    per = packed.shape[1]
    padded = predicted.shape[1]
    pieces = padded // per
    for i in range(rows):
        source = jnp.concatenate(wide[i : i + REACH], axis=1)
        taps = dot_nn(source, ahead[i]).astype(BF)
        for k in range(kernels):
            mixed[i, k * chan : (k + 1) * chan, :] = taps[:, k * lon : (k + 1) * lon]
        stack = jnp.concatenate([wide[i + HALO]] + [taps[:, k * lon : (k + 1) * lon] for k in range(kernels)], axis=0)
        pred = dot_nn(w_fwd[...], stack)
        predicted[i] = pred
        rounded = pred.astype(BF)
        for q in range(pieces):
            packed[i * pieces + q] = rounded[q * per : (q + 1) * per]
    for q in range(rows * pieces, packed.shape[0]):
        packed[q] = jnp.zeros(packed.shape[1:], BF)


def pairs(visitors, sums):
    members, height, _ = visitors.shape
    pieces = []
    for start in range(0, height, 8):
        values = [visitors[m].astype(F32)[start : start + 8] for m in range(members)]
        totals = [None] * members
        for m in range(members):
            for n in range(m + 1, members):
                slope = smooth_slope(values[m] - values[n])
                totals[m] = slope if totals[m] is None else totals[m] + slope
                totals[n] = -slope if totals[n] is None else totals[n] - slope
        pieces.append(totals)
    for m in range(members):
        sums[m] = jnp.concatenate([totals[m] for totals in pieces], axis=0).astype(BF)


def gradient(rows, kernels, members, place, area, sums, predicted, target, mixed, pred_grad, cross, give, keep):
    variables = target.shape[1]
    padded = predicted.shape[1]
    per = sums.shape[1]
    pieces = padded // per
    lon = predicted.shape[2]
    chan = mixed.shape[1] // kernels
    grads, edges = [], []
    odd = (place[0] & 1) == 1
    for i in range(rows):
        pair_sum = jnp.concatenate([sums[i * pieces + q].astype(F32) for q in range(pieces)], axis=0)
        aim = jnp.concatenate([target[i].astype(F32), jnp.zeros((padded - variables, lon), F32)], axis=0)
        grad = area[place[0] * rows + i] * (smooth_slope(predicted[i] - aim) - pair_sum * (1.0 / (members - 1)))
        grad = grad.astype(BF)
        pred_grad[i] = grad
        edges.append(grad)
        grads.append(jnp.concatenate([grad, jnp.zeros((lon - padded, lon), BF)], axis=0))
    for n in range(HALO):
        top, bottom = edges[rows - HALO + n], edges[n]
        cross[n] = jnp.where(odd, top, bottom)
        near = jnp.where(odd, bottom, top)
        for q in range(pieces):
            give[n * pieces + q] = near[q * per : (q + 1) * per]
    total = dot_nt(
        jnp.concatenate([mixed[i] for i in range(rows)], axis=1), jnp.concatenate(grads, axis=1)
    )
    first, second, third = [total[k * chan : (k + 1) * chan] for k in range(kernels)]
    lane = lax.broadcasted_iota(jnp.int32, first.shape, 1)
    spare = lon - variables
    upper = jnp.where(lane < variables, first, pltpu.roll(third, variables, 1))
    tail = jnp.where(lane < 2 * variables - spare, pltpu.roll(third, variables - spare, 1), 0.0)
    lower = jnp.where(lane < variables, second, tail)
    owners = keep.shape[0]
    own = chan // (2 * owners)

    def chunk(owner):
        mine = slice(owner * own, (owner + 1) * own)
        return jnp.concatenate([upper[mine], lower[mine]], axis=0)

    for owner in range(owners):
        even, uneven = chunk(2 * owner), chunk(2 * owner + 1)
        keep[owner] = jnp.where(odd, uneven, even)
        give[HALO * pieces + owner] = jnp.where(odd, even, uneven).astype(BF)


def fold(got, keep, merged):
    owners = keep.shape[0]
    skip = got.shape[0] - owners
    for owner in range(owners):
        merged[owner] = (keep[owner] + got[skip + owner].astype(F32)).astype(BF)


def band_sum(factor, variables, padded, parts, w_bwd, spread):
    owners, height, lon = parts.shape
    total = parts[0].astype(F32)
    for owner in range(1, owners):
        total = total + parts[owner].astype(F32)
    total = total * factor
    own = height // 2
    spare = lon - variables
    lane = lax.broadcasted_iota(jnp.int32, (own, lon), 1)
    front = pltpu.roll(total[:own], lon - variables, 1)
    rest = pltpu.roll(total[own:], lon + spare - variables, 1)
    third = jnp.where(lane < spare, front, jnp.where(lane < variables, rest, 0.0))
    wide = lax.broadcasted_iota(jnp.int32, total.shape, 1)
    total = jnp.where(wide < variables, total, 0.0)
    total = jnp.concatenate([total, third, jnp.zeros((lon - height - own, lon), F32)], axis=0)
    upper = total.astype(BF)
    lower = (total - upper.astype(F32)).astype(BF)
    dec = w_bwd[:, :padded]
    result = dot_nt(dec, upper[:, :padded]) + dot_nt(dec, lower[:, :padded])
    per = spread.shape[1]
    for member in range(spread.shape[0]):
        spread[member] = result[member * per : (member + 1) * per].astype(BF)


def member_sum(parts, owned):
    kernels, own, width = owned.shape
    total = parts[0].astype(F32)
    for member in range(1, parts.shape[0]):
        total = total + parts[member].astype(F32)
    turned = total.T
    for k in range(kernels):
        owned[k] = turned[k * own : (k + 1) * own, :width]


def adjoint_own(rows, kernels, pred_grad, ahead, turned):
    lon = pred_grad.shape[2]
    for k in range(kernels):
        sums = [None] * rows
        for at in range(rows):
            least = HALO - at
            taps = ahead[at, least * lon : (least + rows) * lon, k * lon : (k + 1) * lon]
            found = dot_nt(pred_grad[at], taps)
            for row in range(rows):
                piece = found[:, row * lon : (row + 1) * lon]
                sums[row] = piece if sums[row] is None else sums[row] + piece
        for row in range(rows):
            turned[row, :, k * lon : (k + 1) * lon] = sums[row]


def adjoint_rest(rows, kernels, place, pred_grad, cross, got, turned, edge, w_bwd, result, buffer, sems):
    padded, lon = pred_grad.shape[1:]
    pieces = padded // got.shape[1]
    chip = [jnp.concatenate([got[n * pieces + q] for q in range(pieces)], axis=0) for n in range(HALO)]
    low, high = sides((place[0] & 1) == 1, cross, chip)
    outer = dict(enumerate(low, -HALO)) | dict(enumerate(high, rows))
    moves = []
    for row in range(rows):
        sources = jnp.concatenate([outer[at] for at, _ in edge_taps(rows, row)], axis=1)
        taps = (turned[row] + dot_nt(sources, edge[row])).astype(BF)
        stack = [pred_grad[row]] + [taps[:, k * lon : (k + 1) * lon] for k in range(kernels)]
        buffer[row] = dot_nn(w_bwd[...], jnp.concatenate(stack, axis=0)).astype(BF)
        moves.append(pltpu.make_async_copy(buffer.at[row], result.at[row], sems.at[row]))
        moves[-1].start()
    for move in moves:
        move.wait()


def cut(place, field, cross, chip, sems):
    rows = field.shape[0]
    odd = (place[0] & 1)
    far = (rows - HALO) * odd
    moves = [
        pltpu.make_async_copy(field.at[pl.ds(far, HALO)], cross, sems.at[0]),
        pltpu.make_async_copy(field.at[pl.ds(rows - HALO - far, HALO)], chip, sems.at[1]),
    ]
    for move in moves:
        move.start()
    for move in moves:
        move.wait()


def sides(odd, cross, chip):
    low = [jnp.where(odd, chip[n], cross[n]) for n in range(HALO)]
    high = [jnp.where(odd, cross[n], chip[n]) for n in range(HALO)]
    return low, high


def across(block, axes, start):
    count = lax.axis_size(axes)
    pairs_up = [(i, i + 1) for i in range(start, count - 1, 2)]
    return lax.ppermute(block, axes, pairs_up + [(b, a) for a, b in pairs_up])


def body(latent_fields, target_fields, filters, decoder, cycle_basis, cycle_offsets):
    field = latent_fields[0]
    rows, chan, lon = field.shape
    lat_count, kernels, taps = cycle_basis.shape
    variables = decoder.shape[1]
    members, bands = lax.axis_size("ens"), lax.axis_size(LAT)
    per = 16
    padded = -(-variables // per) * per
    band = lax.axis_index(LAT).astype(jnp.int32)
    place = band.reshape(1)
    area = jnp.asarray(np.cos(np.pi * (np.arange(lat_count) + 0.5) / lat_count - np.pi / 2), F32)
    dec_t = decoder.T
    basis = cycle_basis.transpose(2, 1, 0)
    offsets = cycle_offsets.T

    stay = functools.partial(pltpu.with_memory_space_constraint, memory_space=pltpu.HBM)
    hbm = pl.BlockSpec(memory_space=pltpu.HBM)
    edge = jax.ShapeDtypeStruct((HALO, chan, lon), BF)
    pair = pltpu.SemaphoreType.DMA((2,))
    cross, chip = call(cut, (edge, edge), [SMEM, hbm], 0, 500_000, [pair])(place, stay(field))
    cross, chip = across(cross, LAT, 1), across(chip, LAT, 0)
    ahead, tap_edge, w_fwd, w_bwd, near = call(
        functools.partial(prepare, rows, lat_count),
        (
            jax.ShapeDtypeStruct((rows, REACH * lon, kernels * lon), BF),
            jax.ShapeDtypeStruct((rows, kernels * lon, (REACH - rows) * lon), BF),
            jax.ShapeDtypeStruct((padded, (kernels + 1) * chan), BF),
            jax.ShapeDtypeStruct((chan, (kernels + 1) * padded), BF),
            jax.ShapeDtypeStruct(field.shape, BF),
        ),
        [SMEM, SMEM, SMEM, hbm, hbm, hbm],
        30_000_000,
        2_000_000,
        [pltpu.VMEM(filters.shape, BF), pltpu.VMEM(dec_t.shape, BF), pltpu.SemaphoreType.DMA((3,))],
    )(place, stay(basis), stay(offsets), stay(filters), stay(dec_t), stay(field))
    packed, predicted, mixed = call(
        functools.partial(forward, rows, kernels),
        (
            jax.ShapeDtypeStruct((members, per, lon), BF),
            jax.ShapeDtypeStruct((rows, padded, lon), F32),
            jax.ShapeDtypeStruct((rows, kernels * chan, lon), BF),
        ),
        [SMEM] + [VMEM] * 5,
        450_000_000,
        3_000_000,
    )(place, near, cross, chip, ahead, w_fwd)
    visitors = lax.all_to_all(packed, "ens", 0, 0, tiled=True)
    sums = call(pairs, jax.ShapeDtypeStruct((members, per, lon), BF), [VMEM], 2_000_000, 200_000)(visitors)
    sums = lax.all_to_all(sums, "ens", 0, 0, tiled=True)
    own = chan // bands
    pieces = padded // per
    owners = bands // 2
    pred_grad, cross, give, keep = call(
        functools.partial(gradient, rows, kernels, members),
        (
            jax.ShapeDtypeStruct((rows, padded, lon), BF),
            jax.ShapeDtypeStruct((HALO, padded, lon), BF),
            jax.ShapeDtypeStruct((HALO * pieces + owners, per, lon), BF),
            jax.ShapeDtypeStruct((owners, 2 * own, lon), F32),
        ),
        [SMEM, SMEM] + [VMEM] * 4,
        80_000_000,
        1_200_000,
    )(place, area, sums, predicted, target_fields, mixed)
    got = across(give, LAT, 0)
    turned = call(
        functools.partial(adjoint_own, rows, kernels),
        jax.ShapeDtypeStruct((rows, padded, kernels * lon), F32),
        [VMEM] * 2,
        80_000_000,
        1_500_000,
    )(pred_grad, ahead)
    got, turned = lax.optimization_barrier((got, turned))
    merged = call(fold, jax.ShapeDtypeStruct((owners, 2 * own, lon), BF), [VMEM] * 2, 100_000, 300_000)(got, keep)
    parts = lax.all_to_all(merged, "pair", 0, 0, tiled=True)
    factor = 1.0 / math.sqrt(members * lat_count * lon)
    width = chan // members
    spread = call(
        functools.partial(band_sum, factor, variables, padded),
        jax.ShapeDtypeStruct((members, width, lon), BF),
        [VMEM] * 2,
        20_000_000,
        400_000,
    )(parts, w_bwd)
    cross, spread = lax.optimization_barrier((cross, spread))
    spread = lax.all_to_all(spread, "ens", 0, 0, tiled=True)
    cross = across(cross, LAT, 1)
    latent_grad = call(
        functools.partial(adjoint_rest, rows, kernels),
        jax.ShapeDtypeStruct((rows, chan, lon), BF),
        [SMEM] + [VMEM] * 6,
        150_000_000,
        1_500_000,
        [pltpu.VMEM((rows, chan, lon), BF), pltpu.SemaphoreType.DMA((rows,))],
        hbm,
    )(place, pred_grad, cross, got, turned, tap_edge, w_bwd)
    spread, latent_grad = lax.optimization_barrier((spread, latent_grad))
    owned = call(
        member_sum, jax.ShapeDtypeStruct((kernels, own, width), F32), [VMEM], 100_000, 150_000
    )(spread)
    return latent_grad[None], owned.transpose(1, 0, 2)


def solution(mesh):
    members, bands = mesh.devices.shape
    split = Mesh(mesh.devices.reshape(members, bands // 2, 2), ("ens", "pair", "core"))
    placed = (P("ens", LAT, None, None), P(LAT, None, None), P(), P(), P(), P())
    return jax.shard_map(
        body,
        mesh=split,
        in_specs=placed,
        out_specs=(P("ens", LAT, None, None), P(LAT, None, "ens")),
        check_vma=False,
    )
```

```python
import functools
import math

import jax
import jax.numpy as jnp
import numpy as np
from jax import lax
from jax.experimental import pallas as pl
from jax.experimental.pallas import tpu as pltpu
from jax.sharding import PartitionSpec as P

HALO = 2
SIDE = 2
REACH = 2 * HALO + 1
DELTA = 0.25
BF = jnp.bfloat16
F32 = jnp.float32
VMEM = pl.BlockSpec(memory_space=pltpu.VMEM)


def smooth_slope(differ):
    return differ * lax.rsqrt(differ * differ + DELTA * DELTA)


def dot_nn(a, b):
    return lax.dot_general(a, b, (((1,), (0,)), ((), ())), preferred_element_type=F32)


def dot_nt(a, b):
    return lax.dot_general(a, b, (((1,), (1,)), ((), ())), preferred_element_type=F32)


def call(kernel, out, specs, flops, moved, scratch=(), home=VMEM):
    many = isinstance(out, (tuple, list))
    return pl.pallas_call(
        kernel,
        out_shape=out,
        in_specs=specs,
        out_specs=tuple([home] * len(out)) if many else home,
        scratch_shapes=list(scratch),
        compiler_params=pltpu.CompilerParams(vmem_limit_bytes=32 * 2**20),
        cost_estimate=pl.CostEstimate(flops=flops, bytes_accessed=moved, transcendentals=0),
    )


def odd_band():
    return (lax.axis_index("lat") & 1) == 1


def tap_block(lat_count, lag, band, rows, basis, offsets, source, step, put):
    kernels, lon = basis.shape[1], lag.shape[0]
    cycle = band * rows + source
    inside = jnp.logical_and(cycle >= 0, cycle < lat_count)
    cycle = jnp.clip(cycle, 0, lat_count - 1)
    one, two = SIDE * step, SIDE * step + 1
    off_one, off_two = offsets[one, cycle], offsets[two, cycle]
    mask_one = lag == (off_one & (lon - 1))
    mask_two = lag == (off_two & (lon - 1))
    for k in range(kernels):
        weight_one = jnp.where(inside, basis[one, k, cycle], 0.0)
        weight_two = jnp.where(inside, basis[two, k, cycle], 0.0)
        weight_two = weight_two + jnp.where(off_one == off_two, weight_one, 0.0)
        value = jnp.where(mask_two, weight_two, jnp.where(mask_one, weight_one, 0.0))
        put(k, value.astype(BF))


def edge_taps(rows, row):
    outside = list(range(-HALO, 0)) + list(range(rows, rows + HALO))
    return [(at, row - at + HALO) for at in outside if 0 <= row - at + HALO < REACH]


def lags(lon):
    return (lax.broadcasted_iota(jnp.int32, (lon, lon), 0) - lax.broadcasted_iota(jnp.int32, (lon, lon), 1)) & (lon - 1)


def padded_rows(dec_t, padded):
    rows, chan = dec_t.shape
    return jnp.concatenate([dec_t[...].astype(F32), jnp.zeros((padded - rows, chan), F32)], axis=0).astype(BF)


def prepare(
    rows, lat_count, basis_in, offsets_in, filters, dec_in, field,
    ahead, edge, w_fwd, w_bwd, near, held, dec_t, basis, offsets, sems,
):
    moves = ((offsets_in, offsets), (basis_in, basis), (dec_in, dec_t), (filters, held), (field, near))
    moves = [pltpu.make_async_copy(source, target, sems.at[n]) for n, (source, target) in enumerate(moves)]
    for move in moves:
        move.start()
    lon = ahead.shape[1] // REACH
    lag = lags(lon)
    band = lax.axis_index("lat")

    def block(source, step, put):
        tap_block(lat_count, lag, band, rows, basis, offsets, source, step, put)

    def ahead_put(row, step):
        def put(k, value):
            ahead[row, step * lon : (step + 1) * lon, k * lon : (k + 1) * lon] = value

        return put

    def edge_put(row, slot):
        def put(k, value):
            edge[row, k * lon : (k + 1) * lon, slot * lon : (slot + 1) * lon] = value

        return put

    for move in moves[:2]:
        move.wait()
    for row in range(rows):
        for step in range(REACH):
            block(row, step, ahead_put(row, step))
        for slot, (at, step) in enumerate(edge_taps(rows, row)):
            block(at, step, edge_put(row, slot))
    kernels, chan = held.shape[:2]
    padded = w_fwd.shape[0]
    for move in moves[2:]:
        move.wait()
    dec = padded_rows(dec_t, padded)

    square = (chan, chan)
    unit = lax.broadcasted_iota(jnp.int32, square, 0) == lax.broadcasted_iota(jnp.int32, square, 1)
    columns = [dot_nt(jnp.where(unit, 1.0, 0.0).astype(BF), dec)]
    w_fwd[:, :chan] = dec
    for k in range(kernels):
        w_fwd[:, (k + 1) * chan : (k + 2) * chan] = dot_nt(dec, held[k]).astype(BF)
        columns.append(dot_nt(held[k], dec))
    w_bwd[...] = jnp.concatenate(columns, axis=1).astype(BF)


def forward(rows, kernels, field, cross, chip, ahead, w_fwd, packed, predicted, mixed):
    lon = field.shape[2]
    chan = field.shape[1]
    low, high = sides(odd_band(), cross, chip)
    wide = low + [field[i] for i in range(rows)] + high
    per = packed.shape[1]
    padded = predicted.shape[1]
    pieces = padded // per
    for i in range(rows):
        source = jnp.concatenate(wide[i : i + REACH], axis=1)
        taps = dot_nn(source, ahead[i]).astype(BF)
        for k in range(kernels):
            mixed[i, k * chan : (k + 1) * chan, :] = taps[:, k * lon : (k + 1) * lon]
        stack = jnp.concatenate([wide[i + HALO]] + [taps[:, k * lon : (k + 1) * lon] for k in range(kernels)], axis=0)
        pred = dot_nn(w_fwd[...], stack)
        predicted[i] = pred
        rounded = pred.astype(BF)
        for q in range(pieces):
            packed[i * pieces + q] = rounded[q * per : (q + 1) * per]
    for q in range(rows * pieces, packed.shape[0]):
        packed[q] = jnp.zeros(packed.shape[1:], BF)


def pairs(visitors, sums):
    members, height, _ = visitors.shape
    pieces = []
    for start in range(0, height, 8):
        values = [visitors[m].astype(F32)[start : start + 8] for m in range(members)]
        totals = [None] * members
        for m in range(members):
            for n in range(m + 1, members):
                slope = smooth_slope(values[m] - values[n])
                totals[m] = slope if totals[m] is None else totals[m] + slope
                totals[n] = -slope if totals[n] is None else totals[n] - slope
        pieces.append(totals)
    for m in range(members):
        sums[m] = jnp.concatenate([totals[m] for totals in pieces], axis=0).astype(BF)


def gradient(rows, kernels, members, area, sums, predicted, target, mixed, pred_grad, cross, chip, partial):
    variables = target.shape[1]
    padded = predicted.shape[1]
    per = sums.shape[1]
    pieces = padded // per
    lon = predicted.shape[2]
    chan = mixed.shape[1] // kernels
    grads, edges = [], []
    odd = odd_band()
    band = lax.axis_index("lat")
    for i in range(rows):
        pair_sum = jnp.concatenate([sums[i * pieces + q].astype(F32) for q in range(pieces)], axis=0)
        aim = jnp.concatenate([target[i].astype(F32), jnp.zeros((padded - variables, lon), F32)], axis=0)
        grad = area[pl.ds(band * rows + i, 1), :] * (smooth_slope(predicted[i] - aim) - pair_sum * (1.0 / (members - 1)))
        grad = grad.astype(BF)
        pred_grad[i] = grad
        edges.append(grad)
        grads.append(jnp.concatenate([grad, jnp.zeros((lon - padded, lon), BF)], axis=0))
    for n in range(HALO):
        top, bottom = edges[rows - HALO + n], edges[n]
        cross[n] = jnp.where(odd, top, bottom)
        chip[n] = jnp.where(odd, bottom, top)
    total = dot_nt(
        jnp.concatenate([mixed[i] for i in range(rows)], axis=1), jnp.concatenate(grads, axis=1)
    )
    first, second, third = [total[k * chan : (k + 1) * chan] for k in range(kernels)]
    lane = lax.broadcasted_iota(jnp.int32, first.shape, 1)
    spare = lon - variables
    upper = jnp.where(lane < variables, first, pltpu.roll(third, variables, 1))
    tail = jnp.where(lane < 2 * variables - spare, pltpu.roll(third, variables - spare, 1), 0.0)
    lower = jnp.where(lane < variables, second, tail)
    owners = partial.shape[0]
    own = chan // owners
    for owner in range(owners):
        mine = slice(owner * own, (owner + 1) * own)
        partial[owner] = jnp.concatenate([upper[mine], lower[mine]], axis=0).astype(BF)


def band_sum(factor, variables, padded, parts, w_bwd, spread):
    owners, height, lon = parts.shape
    total = parts[0].astype(F32)
    for owner in range(1, owners):
        total = total + parts[owner].astype(F32)
    total = total * factor
    own = height // 2
    spare = lon - variables
    lane = lax.broadcasted_iota(jnp.int32, (own, lon), 1)
    front = pltpu.roll(total[:own], lon - variables, 1)
    rest = pltpu.roll(total[own:], lon + spare - variables, 1)
    third = jnp.where(lane < spare, front, jnp.where(lane < variables, rest, 0.0))
    wide = lax.broadcasted_iota(jnp.int32, total.shape, 1)
    total = jnp.where(wide < variables, total, 0.0)
    total = jnp.concatenate([total, third, jnp.zeros((lon - height - own, lon), F32)], axis=0)
    upper = total.astype(BF)
    lower = (total - upper.astype(F32)).astype(BF)
    dec = w_bwd[:, :padded]
    result = dot_nt(dec, upper[:, :padded]) + dot_nt(dec, lower[:, :padded])
    per = spread.shape[1]
    for member in range(spread.shape[0]):
        spread[member] = result[member * per : (member + 1) * per].astype(BF)


def member_sum(parts, owned):
    kernels, own, width = owned.shape
    total = parts[0].astype(F32)
    for member in range(1, parts.shape[0]):
        total = total + parts[member].astype(F32)
    turned = total.T
    for k in range(kernels):
        owned[k] = turned[k * own : (k + 1) * own, :width]


def adjoint_own(rows, kernels, pred_grad, ahead, turned):
    lon = pred_grad.shape[2]
    for k in range(kernels):
        sums = [None] * rows
        for at in range(rows):
            least = HALO - at
            taps = ahead[at, least * lon : (least + rows) * lon, k * lon : (k + 1) * lon]
            found = dot_nt(pred_grad[at], taps)
            for row in range(rows):
                piece = found[:, row * lon : (row + 1) * lon]
                sums[row] = piece if sums[row] is None else sums[row] + piece
        for row in range(rows):
            turned[row, :, k * lon : (k + 1) * lon] = sums[row]


def adjoint_rest(rows, kernels, pred_grad, cross, chip, turned, edge, w_bwd, result, buffer, sems):
    lon = pred_grad.shape[2]
    low, high = sides(odd_band(), cross, chip)
    outer = dict(enumerate(low, -HALO)) | dict(enumerate(high, rows))
    moves = []
    for row in range(rows):
        sources = jnp.concatenate([outer[at] for at, _ in edge_taps(rows, row)], axis=1)
        taps = (turned[row] + dot_nt(sources, edge[row])).astype(BF)
        stack = [pred_grad[row]] + [taps[:, k * lon : (k + 1) * lon] for k in range(kernels)]
        buffer[row] = dot_nn(w_bwd[...], jnp.concatenate(stack, axis=0)).astype(BF)
        moves.append(pltpu.make_async_copy(buffer.at[row], result.at[row], sems.at[row]))
        moves[-1].start()
    for move in moves:
        move.wait()


def cut(field, cross, chip, sems):
    rows = field.shape[0]
    odd = lax.axis_index("lat") & 1
    far = (rows - HALO) * odd
    moves = [
        pltpu.make_async_copy(field.at[pl.ds(far, HALO)], cross, sems.at[0]),
        pltpu.make_async_copy(field.at[pl.ds(rows - HALO - far, HALO)], chip, sems.at[1]),
    ]
    for move in moves:
        move.start()
    for move in moves:
        move.wait()


def sides(odd, cross, chip):
    low = [jnp.where(odd, chip[n], cross[n]) for n in range(HALO)]
    high = [jnp.where(odd, cross[n], chip[n]) for n in range(HALO)]
    return low, high


def exchange(cross, chip, axis):
    count = lax.axis_size(axis)
    far = [(i, i + 1) for i in range(1, count - 1, 2)]
    near = [(i, i + 1) for i in range(0, count - 1, 2)]
    cross = lax.ppermute(cross, axis, far + [(b, a) for a, b in far])
    chip = lax.ppermute(chip, axis, near + [(b, a) for a, b in near])
    return cross, chip


def body(latent_fields, target_fields, filters, decoder, cycle_basis, cycle_offsets):
    field = latent_fields[0]
    rows, chan, lon = field.shape
    lat_count, kernels, taps = cycle_basis.shape
    variables = decoder.shape[1]
    members, bands = lax.axis_size("ens"), lax.axis_size("lat")
    per = 16
    padded = -(-variables // per) * per
    area = np.cos(np.pi * (np.arange(lat_count) + 0.5) / lat_count - np.pi / 2)
    area = jnp.asarray(np.broadcast_to(area[:, None], (lat_count, lon)), F32)
    dec_t = decoder.T
    basis = cycle_basis.transpose(2, 1, 0)
    offsets = cycle_offsets.T

    stay = functools.partial(pltpu.with_memory_space_constraint, memory_space=pltpu.HBM)
    hbm = pl.BlockSpec(memory_space=pltpu.HBM)
    edge = jax.ShapeDtypeStruct((HALO, chan, lon), BF)
    pair = pltpu.SemaphoreType.DMA((2,))
    cross, chip = call(cut, (edge, edge), [hbm], 0, 500_000, [pair])(stay(field))
    cross, chip = exchange(cross, chip, "lat")
    ahead, tap_edge, w_fwd, w_bwd, near = call(
        functools.partial(prepare, rows, lat_count),
        (
            jax.ShapeDtypeStruct((rows, REACH * lon, kernels * lon), BF),
            jax.ShapeDtypeStruct((rows, kernels * lon, (REACH - rows) * lon), BF),
            jax.ShapeDtypeStruct((padded, (kernels + 1) * chan), BF),
            jax.ShapeDtypeStruct((chan, (kernels + 1) * padded), BF),
            jax.ShapeDtypeStruct(field.shape, BF),
        ),
        [hbm] * 5,
        30_000_000,
        2_000_000,
        [
            pltpu.VMEM(filters.shape, BF),
            pltpu.VMEM(dec_t.shape, BF),
            pltpu.SMEM(basis.shape, F32),
            pltpu.SMEM(offsets.shape, jnp.int32),
            pltpu.SemaphoreType.DMA((5,)),
        ],
    )(stay(basis), stay(offsets), stay(filters), stay(dec_t), stay(field))
    packed, predicted, mixed = call(
        functools.partial(forward, rows, kernels),
        (
            jax.ShapeDtypeStruct((members, per, lon), BF),
            jax.ShapeDtypeStruct((rows, padded, lon), F32),
            jax.ShapeDtypeStruct((rows, kernels * chan, lon), BF),
        ),
        [VMEM] * 5,
        450_000_000,
        3_000_000,
    )(near, cross, chip, ahead, w_fwd)
    visitors = lax.all_to_all(packed, "ens", 0, 0, tiled=True)
    sums = call(pairs, jax.ShapeDtypeStruct((members, per, lon), BF), [VMEM], 2_000_000, 200_000)(visitors)
    sums = lax.all_to_all(sums, "ens", 0, 0, tiled=True)
    own = chan // bands
    edge = jax.ShapeDtypeStruct((HALO, padded, lon), BF)
    pred_grad, cross, chip, partial = call(
        functools.partial(gradient, rows, kernels, members),
        (
            jax.ShapeDtypeStruct((rows, padded, lon), BF),
            edge,
            edge,
            jax.ShapeDtypeStruct((bands, 2 * own, lon), BF),
        ),
        [VMEM] * 5,
        80_000_000,
        1_200_000,
    )(area, sums, predicted, target_fields, mixed)
    parts = lax.all_to_all(partial, "lat", 0, 0, tiled=True)
    cross, chip = exchange(cross, chip, "lat")
    turned = call(
        functools.partial(adjoint_own, rows, kernels),
        jax.ShapeDtypeStruct((rows, padded, kernels * lon), F32),
        [VMEM] * 2,
        80_000_000,
        1_500_000,
    )(pred_grad, ahead)
    latent_grad = call(
        functools.partial(adjoint_rest, rows, kernels),
        jax.ShapeDtypeStruct((rows, chan, lon), BF),
        [VMEM] * 6,
        150_000_000,
        1_500_000,
        [pltpu.VMEM((rows, chan, lon), BF), pltpu.SemaphoreType.DMA((rows,))],
        hbm,
    )(pred_grad, cross, chip, turned, tap_edge, w_bwd)
    parts, latent_grad = lax.optimization_barrier((parts, latent_grad))
    factor = 1.0 / math.sqrt(members * lat_count * lon)
    width = chan // members
    spread = call(
        functools.partial(band_sum, factor, variables, padded),
        jax.ShapeDtypeStruct((members, width, lon), BF),
        [VMEM] * 2,
        20_000_000,
        400_000,
    )(parts, w_bwd)
    spread = lax.all_to_all(spread, "ens", 0, 0, tiled=True)
    owned = call(
        member_sum, jax.ShapeDtypeStruct((kernels, own, width), F32), [VMEM], 100_000, 150_000
    )(spread)
    return latent_grad[None], owned.transpose(1, 0, 2)


def solution(mesh):
    placed = (P("ens", "lat", None, None), P("lat", None, None), P(), P(), P(), P())
    return jax.shard_map(
        body,
        mesh=mesh,
        in_specs=placed,
        out_specs=(P("ens", "lat", None, None), P("lat", None, "ens")),
        check_vma=False,
    )
```

```python
import functools
import math

import jax
import jax.numpy as jnp
import numpy as np
from jax import lax
from jax.experimental import pallas as pl
from jax.experimental.pallas import tpu as pltpu
from jax.sharding import PartitionSpec as P

HALO = 2
SIDE = 2
REACH = 2 * HALO + 1
DELTA = 0.25
BF = jnp.bfloat16
F32 = jnp.float32
VMEM = pl.BlockSpec(memory_space=pltpu.VMEM)


def smooth_slope(differ):
    return differ * lax.rsqrt(differ * differ + DELTA * DELTA)


def dot_nn(a, b):
    return lax.dot_general(a, b, (((1,), (0,)), ((), ())), preferred_element_type=F32)


def dot_nt(a, b):
    return lax.dot_general(a, b, (((1,), (1,)), ((), ())), preferred_element_type=F32)


def call(kernel, out, specs, flops, moved, scratch=(), home=VMEM):
    many = isinstance(out, (tuple, list))
    return pl.pallas_call(
        kernel,
        out_shape=out,
        in_specs=specs,
        out_specs=tuple([home] * len(out)) if many else home,
        scratch_shapes=list(scratch),
        compiler_params=pltpu.CompilerParams(vmem_limit_bytes=32 * 2**20),
        cost_estimate=pl.CostEstimate(flops=flops, bytes_accessed=moved, transcendentals=0),
    )


def odd_band():
    return (lax.axis_index("lat") & 1) == 1


def tap_block(lat_count, lag, band, rows, basis, offsets, source, step, put):
    kernels, lon = basis.shape[1], lag.shape[0]
    cycle = band * rows + source
    inside = jnp.logical_and(cycle >= 0, cycle < lat_count)
    cycle = jnp.clip(cycle, 0, lat_count - 1)
    one, two = SIDE * step, SIDE * step + 1
    off_one, off_two = offsets[one, cycle], offsets[two, cycle]
    mask_one = lag == (off_one & (lon - 1))
    mask_two = lag == (off_two & (lon - 1))
    for k in range(kernels):
        weight_one = jnp.where(inside, basis[one, k, cycle], 0.0)
        weight_two = jnp.where(inside, basis[two, k, cycle], 0.0)
        weight_two = weight_two + jnp.where(off_one == off_two, weight_one, 0.0)
        value = jnp.where(mask_two, weight_two, jnp.where(mask_one, weight_one, 0.0))
        put(k, value.astype(BF))


def edge_taps(rows, row):
    outside = list(range(-HALO, 0)) + list(range(rows, rows + HALO))
    return [(at, row - at + HALO) for at in outside if 0 <= row - at + HALO < REACH]


def lags(lon):
    return (lax.broadcasted_iota(jnp.int32, (lon, lon), 0) - lax.broadcasted_iota(jnp.int32, (lon, lon), 1)) & (lon - 1)


def padded_rows(dec_t, padded):
    rows, chan = dec_t.shape
    return jnp.concatenate([dec_t[...].astype(F32), jnp.zeros((padded - rows, chan), F32)], axis=0).astype(BF)


def prepare(
    rows, lat_count, basis_in, offsets_in, filters, dec_in, field,
    ahead, edge, w_fwd, w_bwd, near, held, dec_t, basis, offsets, sems,
):
    moves = ((offsets_in, offsets), (basis_in, basis), (dec_in, dec_t), (filters, held), (field, near))
    moves = [pltpu.make_async_copy(source, target, sems.at[n]) for n, (source, target) in enumerate(moves)]
    for move in moves:
        move.start()
    lon = ahead.shape[1] // REACH
    lag = lags(lon)
    band = lax.axis_index("lat")

    def block(source, step, put):
        tap_block(lat_count, lag, band, rows, basis, offsets, source, step, put)

    def ahead_put(row, step):
        def put(k, value):
            ahead[row, step * lon : (step + 1) * lon, k * lon : (k + 1) * lon] = value

        return put

    def edge_put(row, slot):
        def put(k, value):
            edge[row, k * lon : (k + 1) * lon, slot * lon : (slot + 1) * lon] = value

        return put

    for move in moves[:2]:
        move.wait()
    for row in range(rows):
        for step in range(REACH):
            block(row, step, ahead_put(row, step))
        for slot, (at, step) in enumerate(edge_taps(rows, row)):
            block(at, step, edge_put(row, slot))
    kernels, chan = held.shape[:2]
    padded = w_fwd.shape[0]
    for move in moves[2:]:
        move.wait()
    dec = padded_rows(dec_t, padded)

    square = (chan, chan)
    unit = lax.broadcasted_iota(jnp.int32, square, 0) == lax.broadcasted_iota(jnp.int32, square, 1)
    columns = [dot_nt(jnp.where(unit, 1.0, 0.0).astype(BF), dec)]
    w_fwd[:, :chan] = dec
    for k in range(kernels):
        w_fwd[:, (k + 1) * chan : (k + 2) * chan] = dot_nt(dec, held[k]).astype(BF)
        columns.append(dot_nt(held[k], dec))
    w_bwd[...] = jnp.concatenate(columns, axis=1).astype(BF)


def forward(rows, kernels, field, cross, chip, ahead, w_fwd, packed, predicted, mixed):
    lon = field.shape[2]
    chan = field.shape[1]
    low, high = sides(odd_band(), cross, chip)
    wide = low + [field[i] for i in range(rows)] + high
    per = packed.shape[1]
    padded = predicted.shape[1]
    pieces = padded // per
    for i in range(rows):
        source = jnp.concatenate(wide[i : i + REACH], axis=1)
        taps = dot_nn(source, ahead[i]).astype(BF)
        for k in range(kernels):
            mixed[i, k * chan : (k + 1) * chan, :] = taps[:, k * lon : (k + 1) * lon]
        stack = jnp.concatenate([wide[i + HALO]] + [taps[:, k * lon : (k + 1) * lon] for k in range(kernels)], axis=0)
        pred = dot_nn(w_fwd[...], stack)
        predicted[i] = pred
        rounded = pred.astype(BF)
        for q in range(pieces):
            packed[i * pieces + q] = rounded[q * per : (q + 1) * per]
    for q in range(rows * pieces, packed.shape[0]):
        packed[q] = jnp.zeros(packed.shape[1:], BF)


def pairs(visitors, sums):
    members, height, _ = visitors.shape
    pieces = []
    for start in range(0, height, 8):
        values = [visitors[m].astype(F32)[start : start + 8] for m in range(members)]
        totals = [None] * members
        for m in range(members):
            for n in range(m + 1, members):
                slope = smooth_slope(values[m] - values[n])
                totals[m] = slope if totals[m] is None else totals[m] + slope
                totals[n] = -slope if totals[n] is None else totals[n] - slope
        pieces.append(totals)
    for m in range(members):
        sums[m] = jnp.concatenate([totals[m] for totals in pieces], axis=0).astype(BF)


def gradient(rows, kernels, members, area, sums, predicted, target, mixed, pred_grad, cross, chip, partial):
    variables = target.shape[1]
    padded = predicted.shape[1]
    per = sums.shape[1]
    pieces = padded // per
    lon = predicted.shape[2]
    chan = mixed.shape[1] // kernels
    grads, edges = [], []
    odd = odd_band()
    band = lax.axis_index("lat")
    for i in range(rows):
        pair_sum = jnp.concatenate([sums[i * pieces + q].astype(F32) for q in range(pieces)], axis=0)
        aim = jnp.concatenate([target[i].astype(F32), jnp.zeros((padded - variables, lon), F32)], axis=0)
        grad = area[pl.ds(band * rows + i, 1), :] * (smooth_slope(predicted[i] - aim) - pair_sum * (1.0 / (members - 1)))
        grad = grad.astype(BF)
        pred_grad[i] = grad
        edges.append(grad)
        grads.append(jnp.concatenate([grad, jnp.zeros((lon - padded, lon), BF)], axis=0))
    for n in range(HALO):
        top, bottom = edges[rows - HALO + n], edges[n]
        cross[n] = jnp.where(odd, top, bottom)
        chip[n] = jnp.where(odd, bottom, top)
    total = dot_nt(
        jnp.concatenate([mixed[i] for i in range(rows)], axis=1), jnp.concatenate(grads, axis=1)
    )
    first, second, third = [total[k * chan : (k + 1) * chan] for k in range(kernels)]
    lane = lax.broadcasted_iota(jnp.int32, first.shape, 1)
    spare = lon - variables
    upper = jnp.where(lane < variables, first, pltpu.roll(third, variables, 1))
    tail = jnp.where(lane < 2 * variables - spare, pltpu.roll(third, variables - spare, 1), 0.0)
    lower = jnp.where(lane < variables, second, tail)
    owners = partial.shape[0]
    own = chan // owners
    for owner in range(owners):
        mine = slice(owner * own, (owner + 1) * own)
        partial[owner] = jnp.concatenate([upper[mine], lower[mine]], axis=0).astype(BF)


def band_sum(factor, variables, padded, parts, w_bwd, spread):
    owners, height, lon = parts.shape
    total = parts[0].astype(F32)
    for owner in range(1, owners):
        total = total + parts[owner].astype(F32)
    total = total * factor
    own = height // 2
    spare = lon - variables
    lane = lax.broadcasted_iota(jnp.int32, (own, lon), 1)
    front = pltpu.roll(total[:own], lon - variables, 1)
    rest = pltpu.roll(total[own:], lon + spare - variables, 1)
    third = jnp.where(lane < spare, front, jnp.where(lane < variables, rest, 0.0))
    wide = lax.broadcasted_iota(jnp.int32, total.shape, 1)
    total = jnp.where(wide < variables, total, 0.0)
    total = jnp.concatenate([total, third, jnp.zeros((lon - height - own, lon), F32)], axis=0)
    upper = total.astype(BF)
    lower = (total - upper.astype(F32)).astype(BF)
    dec = w_bwd[:, :padded]
    result = dot_nt(dec, upper[:, :padded]) + dot_nt(dec, lower[:, :padded])
    per = spread.shape[1]
    for member in range(spread.shape[0]):
        spread[member] = result[member * per : (member + 1) * per].astype(BF)


def adjoint_own(rows, kernels, pred_grad, ahead, turned):
    lon = pred_grad.shape[2]
    for k in range(kernels):
        sums = [None] * rows
        for at in range(rows):
            least = HALO - at
            taps = ahead[at, least * lon : (least + rows) * lon, k * lon : (k + 1) * lon]
            found = dot_nt(pred_grad[at], taps)
            for row in range(rows):
                piece = found[:, row * lon : (row + 1) * lon]
                sums[row] = piece if sums[row] is None else sums[row] + piece
        for row in range(rows):
            turned[row, :, k * lon : (k + 1) * lon] = sums[row]


def finish(rows, kernels, pred_grad, cross, chip, turned, edge, w_bwd, parts, result, owned, buffer, small, sems):
    own, width = owned.shape[1:]
    total = parts[0].astype(F32)
    for member in range(1, parts.shape[0]):
        total = total + parts[member].astype(F32)
    turned_sum = total.T
    for k in range(kernels):
        small[k] = turned_sum[k * own : (k + 1) * own, :width]
    moves = [pltpu.make_async_copy(small, owned, sems.at[rows])]
    moves[0].start()
    lon = pred_grad.shape[2]
    low, high = sides(odd_band(), cross, chip)
    outer = dict(enumerate(low, -HALO)) | dict(enumerate(high, rows))
    for row in range(rows):
        sources = jnp.concatenate([outer[at] for at, _ in edge_taps(rows, row)], axis=1)
        taps = (turned[row] + dot_nt(sources, edge[row])).astype(BF)
        stack = [pred_grad[row]] + [taps[:, k * lon : (k + 1) * lon] for k in range(kernels)]
        buffer[row] = dot_nn(w_bwd[...], jnp.concatenate(stack, axis=0)).astype(BF)
        moves.append(pltpu.make_async_copy(buffer.at[row], result.at[row], sems.at[row]))
        moves[-1].start()
    for move in moves:
        move.wait()


def cut(field, cross, chip, sems):
    rows = field.shape[0]
    odd = lax.axis_index("lat") & 1
    far = (rows - HALO) * odd
    moves = [
        pltpu.make_async_copy(field.at[pl.ds(far, HALO)], cross, sems.at[0]),
        pltpu.make_async_copy(field.at[pl.ds(rows - HALO - far, HALO)], chip, sems.at[1]),
    ]
    for move in moves:
        move.start()
    for move in moves:
        move.wait()


def sides(odd, cross, chip):
    low = [jnp.where(odd, chip[n], cross[n]) for n in range(HALO)]
    high = [jnp.where(odd, cross[n], chip[n]) for n in range(HALO)]
    return low, high


def exchange(cross, chip, axis):
    count = lax.axis_size(axis)
    far = [(i, i + 1) for i in range(1, count - 1, 2)]
    near = [(i, i + 1) for i in range(0, count - 1, 2)]
    cross = lax.ppermute(cross, axis, far + [(b, a) for a, b in far])
    chip = lax.ppermute(chip, axis, near + [(b, a) for a, b in near])
    return cross, chip


def body(latent_fields, target_fields, filters, decoder, cycle_basis, cycle_offsets):
    field = latent_fields[0]
    rows, chan, lon = field.shape
    lat_count, kernels, taps = cycle_basis.shape
    variables = decoder.shape[1]
    members, bands = lax.axis_size("ens"), lax.axis_size("lat")
    per = 16
    padded = -(-variables // per) * per
    area = np.cos(np.pi * (np.arange(lat_count) + 0.5) / lat_count - np.pi / 2)
    area = jnp.asarray(np.broadcast_to(area[:, None], (lat_count, lon)), F32)
    dec_t = decoder.T
    basis = cycle_basis.transpose(2, 1, 0)
    offsets = cycle_offsets.T

    stay = functools.partial(pltpu.with_memory_space_constraint, memory_space=pltpu.HBM)
    hbm = pl.BlockSpec(memory_space=pltpu.HBM)
    edge = jax.ShapeDtypeStruct((HALO, chan, lon), BF)
    pair = pltpu.SemaphoreType.DMA((2,))
    cross, chip = call(cut, (edge, edge), [hbm], 0, 500_000, [pair])(stay(field))
    cross, chip = exchange(cross, chip, "lat")
    ahead, tap_edge, w_fwd, w_bwd, near = call(
        functools.partial(prepare, rows, lat_count),
        (
            jax.ShapeDtypeStruct((rows, REACH * lon, kernels * lon), BF),
            jax.ShapeDtypeStruct((rows, kernels * lon, (REACH - rows) * lon), BF),
            jax.ShapeDtypeStruct((padded, (kernels + 1) * chan), BF),
            jax.ShapeDtypeStruct((chan, (kernels + 1) * padded), BF),
            jax.ShapeDtypeStruct(field.shape, BF),
        ),
        [hbm] * 5,
        30_000_000,
        2_000_000,
        [
            pltpu.VMEM(filters.shape, BF),
            pltpu.VMEM(dec_t.shape, BF),
            pltpu.SMEM(basis.shape, F32),
            pltpu.SMEM(offsets.shape, jnp.int32),
            pltpu.SemaphoreType.DMA((5,)),
        ],
    )(stay(basis), stay(offsets), stay(filters), stay(dec_t), stay(field))
    packed, predicted, mixed = call(
        functools.partial(forward, rows, kernels),
        (
            jax.ShapeDtypeStruct((members, per, lon), BF),
            jax.ShapeDtypeStruct((rows, padded, lon), F32),
            jax.ShapeDtypeStruct((rows, kernels * chan, lon), BF),
        ),
        [VMEM] * 5,
        450_000_000,
        3_000_000,
    )(near, cross, chip, ahead, w_fwd)
    visitors = lax.all_to_all(packed, "ens", 0, 0, tiled=True)
    sums = call(pairs, jax.ShapeDtypeStruct((members, per, lon), BF), [VMEM], 2_000_000, 200_000)(visitors)
    sums = lax.all_to_all(sums, "ens", 0, 0, tiled=True)
    own = chan // bands
    edge = jax.ShapeDtypeStruct((HALO, padded, lon), BF)
    pred_grad, cross, chip, partial = call(
        functools.partial(gradient, rows, kernels, members),
        (
            jax.ShapeDtypeStruct((rows, padded, lon), BF),
            edge,
            edge,
            jax.ShapeDtypeStruct((bands, 2 * own, lon), BF),
        ),
        [VMEM] * 5,
        80_000_000,
        1_200_000,
    )(area, sums, predicted, target_fields, mixed)
    parts = lax.all_to_all(partial, "lat", 0, 0, tiled=True)
    cross, chip = exchange(cross, chip, "lat")
    turned = call(
        functools.partial(adjoint_own, rows, kernels),
        jax.ShapeDtypeStruct((rows, padded, kernels * lon), F32),
        [VMEM] * 2,
        80_000_000,
        1_500_000,
    )(pred_grad, ahead)
    parts, turned, cross, chip = lax.optimization_barrier((parts, turned, cross, chip))
    factor = 1.0 / math.sqrt(members * lat_count * lon)
    width = chan // members
    spread = call(
        functools.partial(band_sum, factor, variables, padded),
        jax.ShapeDtypeStruct((members, width, lon), BF),
        [VMEM] * 2,
        20_000_000,
        400_000,
    )(parts, w_bwd)
    spread = lax.all_to_all(spread, "ens", 0, 0, tiled=True)
    latent_grad, owned = call(
        functools.partial(finish, rows, kernels),
        (jax.ShapeDtypeStruct((rows, chan, lon), BF), jax.ShapeDtypeStruct((kernels, own, width), F32)),
        [VMEM] * 7,
        150_000_000,
        1_500_000,
        [
            pltpu.VMEM((rows, chan, lon), BF),
            pltpu.VMEM((kernels, own, width), F32),
            pltpu.SemaphoreType.DMA((rows + 1,)),
        ],
        hbm,
    )(pred_grad, cross, chip, turned, tap_edge, w_bwd, spread)
    return latent_grad[None], owned.transpose(1, 0, 2)


def solution(mesh):
    placed = (P("ens", "lat", None, None), P("lat", None, None), P(), P(), P(), P())
    return jax.shard_map(
        body,
        mesh=mesh,
        in_specs=placed,
        out_specs=(P("ens", "lat", None, None), P("lat", None, "ens")),
        check_vma=False,
    )
```

```python
import functools
import math

import jax
import jax.numpy as jnp
import numpy as np
from jax import lax
from jax.experimental import pallas as pl
from jax.experimental.pallas import tpu as pltpu
from jax.sharding import PartitionSpec as P

HALO = 2
SIDE = 2
REACH = 2 * HALO + 1
DELTA = 0.25
BF = jnp.bfloat16
F32 = jnp.float32
VMEM = pl.BlockSpec(memory_space=pltpu.VMEM)


def smooth_slope(differ):
    return differ * lax.rsqrt(differ * differ + DELTA * DELTA)


def dot_nn(a, b):
    return lax.dot_general(a, b, (((1,), (0,)), ((), ())), preferred_element_type=F32)


def dot_nt(a, b):
    return lax.dot_general(a, b, (((1,), (1,)), ((), ())), preferred_element_type=F32)


def call(kernel, out, specs, flops, moved, scratch=(), home=VMEM):
    many = isinstance(out, (tuple, list))
    return pl.pallas_call(
        kernel,
        out_shape=out,
        in_specs=specs,
        out_specs=tuple([home] * len(out)) if many else home,
        scratch_shapes=list(scratch),
        compiler_params=pltpu.CompilerParams(vmem_limit_bytes=32 * 2**20),
        cost_estimate=pl.CostEstimate(flops=flops, bytes_accessed=moved, transcendentals=0),
    )


def odd_band():
    return (lax.axis_index("lat") & 1) == 1


def tap_block(lat_count, lag, band, rows, basis, offsets, source, step, put):
    kernels, lon = basis.shape[1], lag.shape[0]
    cycle = band * rows + source
    inside = jnp.logical_and(cycle >= 0, cycle < lat_count)
    cycle = jnp.clip(cycle, 0, lat_count - 1)
    one, two = SIDE * step, SIDE * step + 1
    off_one, off_two = offsets[one, cycle], offsets[two, cycle]
    mask_one = lag == (off_one & (lon - 1))
    mask_two = lag == (off_two & (lon - 1))
    for k in range(kernels):
        weight_one = jnp.where(inside, basis[one, k, cycle], 0.0)
        weight_two = jnp.where(inside, basis[two, k, cycle], 0.0)
        weight_two = weight_two + jnp.where(off_one == off_two, weight_one, 0.0)
        value = jnp.where(mask_two, weight_two, jnp.where(mask_one, weight_one, 0.0))
        put(k, value.astype(BF))


def edge_taps(rows, row):
    outside = list(range(-HALO, 0)) + list(range(rows, rows + HALO))
    return [(at, row - at + HALO) for at in outside if 0 <= row - at + HALO < REACH]


def lags(lon):
    return (lax.broadcasted_iota(jnp.int32, (lon, lon), 0) - lax.broadcasted_iota(jnp.int32, (lon, lon), 1)) & (lon - 1)


def padded_rows(dec_t, padded):
    rows, chan = dec_t.shape
    return jnp.concatenate([dec_t[...].astype(F32), jnp.zeros((padded - rows, chan), F32)], axis=0).astype(BF)


def prepare(
    rows, lat_count, basis_in, offsets_in, filters, dec_in, field,
    ahead, edge, w_fwd, w_bwd, near, held, dec_t, basis, offsets, sems,
):
    moves = ((offsets_in, offsets), (basis_in, basis), (dec_in, dec_t), (filters, held), (field, near))
    moves = [pltpu.make_async_copy(source, target, sems.at[n]) for n, (source, target) in enumerate(moves)]
    for move in moves:
        move.start()
    lon = ahead.shape[1] // REACH
    lag = lags(lon)
    band = lax.axis_index("lat")

    def block(source, step, put):
        tap_block(lat_count, lag, band, rows, basis, offsets, source, step, put)

    def ahead_put(row, step):
        def put(k, value):
            ahead[row, step * lon : (step + 1) * lon, k * lon : (k + 1) * lon] = value

        return put

    def edge_put(row, slot):
        def put(k, value):
            edge[row, k * lon : (k + 1) * lon, slot * lon : (slot + 1) * lon] = value

        return put

    for move in moves[:2]:
        move.wait()
    for row in range(rows):
        for step in range(REACH):
            block(row, step, ahead_put(row, step))
        for slot, (at, step) in enumerate(edge_taps(rows, row)):
            block(at, step, edge_put(row, slot))
    kernels, chan = held.shape[:2]
    padded = w_fwd.shape[0]
    for move in moves[2:]:
        move.wait()
    dec = padded_rows(dec_t, padded)

    square = (chan, chan)
    unit = lax.broadcasted_iota(jnp.int32, square, 0) == lax.broadcasted_iota(jnp.int32, square, 1)
    columns = [dot_nt(jnp.where(unit, 1.0, 0.0).astype(BF), dec)]
    w_fwd[:, :chan] = dec
    for k in range(kernels):
        w_fwd[:, (k + 1) * chan : (k + 2) * chan] = dot_nt(dec, held[k]).astype(BF)
        columns.append(dot_nt(held[k], dec))
    w_bwd[...] = jnp.concatenate(columns, axis=1).astype(BF)


def forward_own(rows, kernels, field, ahead, w_fwd, mixed, predicted):
    chan, lon = field.shape[1:]
    source = jnp.concatenate([field[i] for i in range(rows)], axis=1)
    for i in range(rows):
        mixed[i] = dot_nn(source, ahead[i, (HALO - i) * lon : (HALO - i + rows) * lon, :])
        predicted[i] = dot_nn(w_fwd[:, :chan], field[i])


def forward_rest(rows, kernels, cross, chip, begun, based, ahead, w_fwd, packed, predicted, mixed):
    chan, lon = cross.shape[1:]
    low, high = sides(odd_band(), cross, chip)
    outer = dict(enumerate(low, -HALO)) | dict(enumerate(high, rows))
    per = packed.shape[1]
    padded = predicted.shape[1]
    pieces = padded // per
    for i in range(rows):
        reach = [at for at in outer if 0 <= at - i + HALO < REACH]
        source = jnp.concatenate([outer[at] for at in reach], axis=1)
        steps = [at - i + HALO for at in reach]
        table = jnp.concatenate([ahead[i, step * lon : (step + 1) * lon, :] for step in steps], axis=0)
        taps = (begun[i] + dot_nn(source, table)).astype(BF)
        stack = [taps[:, k * lon : (k + 1) * lon] for k in range(kernels)]
        for k in range(kernels):
            mixed[i, k * chan : (k + 1) * chan, :] = stack[k]
        pred = based[i] + dot_nn(w_fwd[:, chan:], jnp.concatenate(stack, axis=0))
        predicted[i] = pred
        rounded = pred.astype(BF)
        for q in range(pieces):
            packed[i * pieces + q] = rounded[q * per : (q + 1) * per]
    for q in range(rows * pieces, packed.shape[0]):
        packed[q] = jnp.zeros(packed.shape[1:], BF)


def pairs(visitors, sums):
    members, height, _ = visitors.shape
    pieces = []
    for start in range(0, height, 8):
        values = [visitors[m].astype(F32)[start : start + 8] for m in range(members)]
        totals = [None] * members
        for m in range(members):
            for n in range(m + 1, members):
                slope = smooth_slope(values[m] - values[n])
                totals[m] = slope if totals[m] is None else totals[m] + slope
                totals[n] = -slope if totals[n] is None else totals[n] - slope
        pieces.append(totals)
    for m in range(members):
        sums[m] = jnp.concatenate([totals[m] for totals in pieces], axis=0).astype(BF)


def gradient(rows, kernels, members, area, sums, predicted, target, mixed, pred_grad, cross, chip, partial):
    variables = target.shape[1]
    padded = predicted.shape[1]
    per = sums.shape[1]
    pieces = padded // per
    lon = predicted.shape[2]
    chan = mixed.shape[1] // kernels
    grads, edges = [], []
    odd = odd_band()
    band = lax.axis_index("lat")
    for i in range(rows):
        pair_sum = jnp.concatenate([sums[i * pieces + q].astype(F32) for q in range(pieces)], axis=0)
        aim = jnp.concatenate([target[i].astype(F32), jnp.zeros((padded - variables, lon), F32)], axis=0)
        grad = area[pl.ds(band * rows + i, 1), :] * (smooth_slope(predicted[i] - aim) - pair_sum * (1.0 / (members - 1)))
        grad = grad.astype(BF)
        pred_grad[i] = grad
        edges.append(grad)
        grads.append(jnp.concatenate([grad, jnp.zeros((lon - padded, lon), BF)], axis=0))
    for n in range(HALO):
        top, bottom = edges[rows - HALO + n], edges[n]
        cross[n] = jnp.where(odd, top, bottom)
        chip[n] = jnp.where(odd, bottom, top)
    total = dot_nt(
        jnp.concatenate([mixed[i] for i in range(rows)], axis=1), jnp.concatenate(grads, axis=1)
    )
    first, second, third = [total[k * chan : (k + 1) * chan] for k in range(kernels)]
    lane = lax.broadcasted_iota(jnp.int32, first.shape, 1)
    spare = lon - variables
    upper = jnp.where(lane < variables, first, pltpu.roll(third, variables, 1))
    tail = jnp.where(lane < 2 * variables - spare, pltpu.roll(third, variables - spare, 1), 0.0)
    lower = jnp.where(lane < variables, second, tail)
    owners = partial.shape[0]
    own = chan // owners
    for owner in range(owners):
        mine = slice(owner * own, (owner + 1) * own)
        partial[owner] = jnp.concatenate([upper[mine], lower[mine]], axis=0).astype(BF)


def band_sum(factor, variables, padded, parts, w_bwd, spread):
    owners, height, lon = parts.shape
    total = parts[0].astype(F32)
    for owner in range(1, owners):
        total = total + parts[owner].astype(F32)
    total = total * factor
    own = height // 2
    spare = lon - variables
    lane = lax.broadcasted_iota(jnp.int32, (own, lon), 1)
    front = pltpu.roll(total[:own], lon - variables, 1)
    rest = pltpu.roll(total[own:], lon + spare - variables, 1)
    third = jnp.where(lane < spare, front, jnp.where(lane < variables, rest, 0.0))
    wide = lax.broadcasted_iota(jnp.int32, total.shape, 1)
    total = jnp.where(wide < variables, total, 0.0)
    total = jnp.concatenate([total, third, jnp.zeros((lon - height - own, lon), F32)], axis=0)
    upper = total.astype(BF)
    lower = (total - upper.astype(F32)).astype(BF)
    dec = w_bwd[:, :padded]
    result = dot_nt(dec, upper[:, :padded]) + dot_nt(dec, lower[:, :padded])
    per = spread.shape[1]
    for member in range(spread.shape[0]):
        spread[member] = result[member * per : (member + 1) * per].astype(BF)


def member_sum(parts, owned):
    kernels, own, width = owned.shape
    total = parts[0].astype(F32)
    for member in range(1, parts.shape[0]):
        total = total + parts[member].astype(F32)
    turned = total.T
    for k in range(kernels):
        owned[k] = turned[k * own : (k + 1) * own, :width]


def adjoint_own(rows, kernels, pred_grad, ahead, turned):
    lon = pred_grad.shape[2]
    for k in range(kernels):
        sums = [None] * rows
        for at in range(rows):
            least = HALO - at
            taps = ahead[at, least * lon : (least + rows) * lon, k * lon : (k + 1) * lon]
            found = dot_nt(pred_grad[at], taps)
            for row in range(rows):
                piece = found[:, row * lon : (row + 1) * lon]
                sums[row] = piece if sums[row] is None else sums[row] + piece
        for row in range(rows):
            turned[row, :, k * lon : (k + 1) * lon] = sums[row]


def adjoint_rest(rows, kernels, pred_grad, cross, chip, turned, edge, w_bwd, result, buffer, sems):
    lon = pred_grad.shape[2]
    low, high = sides(odd_band(), cross, chip)
    outer = dict(enumerate(low, -HALO)) | dict(enumerate(high, rows))
    moves = []
    for row in range(rows):
        sources = jnp.concatenate([outer[at] for at, _ in edge_taps(rows, row)], axis=1)
        taps = (turned[row] + dot_nt(sources, edge[row])).astype(BF)
        stack = [pred_grad[row]] + [taps[:, k * lon : (k + 1) * lon] for k in range(kernels)]
        buffer[row] = dot_nn(w_bwd[...], jnp.concatenate(stack, axis=0)).astype(BF)
        moves.append(pltpu.make_async_copy(buffer.at[row], result.at[row], sems.at[row]))
        moves[-1].start()
    for move in moves:
        move.wait()


def cut(field, cross, chip, sems):
    rows = field.shape[0]
    odd = lax.axis_index("lat") & 1
    far = (rows - HALO) * odd
    moves = [
        pltpu.make_async_copy(field.at[pl.ds(far, HALO)], cross, sems.at[0]),
        pltpu.make_async_copy(field.at[pl.ds(rows - HALO - far, HALO)], chip, sems.at[1]),
    ]
    for move in moves:
        move.start()
    for move in moves:
        move.wait()


def sides(odd, cross, chip):
    low = [jnp.where(odd, chip[n], cross[n]) for n in range(HALO)]
    high = [jnp.where(odd, cross[n], chip[n]) for n in range(HALO)]
    return low, high


def across(block, axis, start):
    count = lax.axis_size(axis)
    up = [(i, i + 1) for i in range(start, count - 1, 2)]
    return lax.ppermute(block, axis, up + [(b, a) for a, b in up])


def body(latent_fields, target_fields, filters, decoder, cycle_basis, cycle_offsets):
    field = latent_fields[0]
    rows, chan, lon = field.shape
    lat_count, kernels, taps = cycle_basis.shape
    variables = decoder.shape[1]
    members, bands = lax.axis_size("ens"), lax.axis_size("lat")
    per = 16
    padded = -(-variables // per) * per
    area = np.cos(np.pi * (np.arange(lat_count) + 0.5) / lat_count - np.pi / 2)
    area = jnp.asarray(np.broadcast_to(area[:, None], (lat_count, lon)), F32)
    dec_t = decoder.T
    basis = cycle_basis.transpose(2, 1, 0)
    offsets = cycle_offsets.T

    stay = functools.partial(pltpu.with_memory_space_constraint, memory_space=pltpu.HBM)
    hbm = pl.BlockSpec(memory_space=pltpu.HBM)
    edge = jax.ShapeDtypeStruct((HALO, chan, lon), BF)
    pair = pltpu.SemaphoreType.DMA((2,))
    cross, chip = call(cut, (edge, edge), [hbm], 0, 500_000, [pair])(stay(field))
    cross = across(cross, "lat", 1)
    ahead, tap_edge, w_fwd, w_bwd, near = call(
        functools.partial(prepare, rows, lat_count),
        (
            jax.ShapeDtypeStruct((rows, REACH * lon, kernels * lon), BF),
            jax.ShapeDtypeStruct((rows, kernels * lon, (REACH - rows) * lon), BF),
            jax.ShapeDtypeStruct((padded, (kernels + 1) * chan), BF),
            jax.ShapeDtypeStruct((chan, (kernels + 1) * padded), BF),
            jax.ShapeDtypeStruct(field.shape, BF),
        ),
        [hbm] * 5,
        30_000_000,
        2_000_000,
        [
            pltpu.VMEM(filters.shape, BF),
            pltpu.VMEM(dec_t.shape, BF),
            pltpu.SMEM(basis.shape, F32),
            pltpu.SMEM(offsets.shape, jnp.int32),
            pltpu.SemaphoreType.DMA((5,)),
        ],
    )(stay(basis), stay(offsets), stay(filters), stay(dec_t), stay(field))
    chip, ahead = lax.optimization_barrier((chip, ahead))
    chip = across(chip, "lat", 0)
    begun, based = call(
        functools.partial(forward_own, rows, kernels),
        (jax.ShapeDtypeStruct((rows, chan, kernels * lon), F32), jax.ShapeDtypeStruct((rows, padded, lon), F32)),
        [VMEM] * 3,
        250_000_000,
        3_000_000,
    )(near, ahead, w_fwd)
    packed, predicted, mixed = call(
        functools.partial(forward_rest, rows, kernels),
        (
            jax.ShapeDtypeStruct((members, per, lon), BF),
            jax.ShapeDtypeStruct((rows, padded, lon), F32),
            jax.ShapeDtypeStruct((rows, kernels * chan, lon), BF),
        ),
        [VMEM] * 6,
        200_000_000,
        3_000_000,
    )(cross, chip, begun, based, ahead, w_fwd)
    visitors = lax.all_to_all(packed, "ens", 0, 0, tiled=True)
    sums = call(pairs, jax.ShapeDtypeStruct((members, per, lon), BF), [VMEM], 2_000_000, 200_000)(visitors)
    sums = lax.all_to_all(sums, "ens", 0, 0, tiled=True)
    own = chan // bands
    edge = jax.ShapeDtypeStruct((HALO, padded, lon), BF)
    pred_grad, cross, chip, partial = call(
        functools.partial(gradient, rows, kernels, members),
        (
            jax.ShapeDtypeStruct((rows, padded, lon), BF),
            edge,
            edge,
            jax.ShapeDtypeStruct((bands, 2 * own, lon), BF),
        ),
        [VMEM] * 5,
        80_000_000,
        1_200_000,
    )(area, sums, predicted, target_fields, mixed)
    parts = lax.all_to_all(partial, "lat", 0, 0, tiled=True)
    cross, chip = across(cross, "lat", 1), across(chip, "lat", 0)
    turned = call(
        functools.partial(adjoint_own, rows, kernels),
        jax.ShapeDtypeStruct((rows, padded, kernels * lon), F32),
        [VMEM] * 2,
        80_000_000,
        1_500_000,
    )(pred_grad, ahead)
    latent_grad = call(
        functools.partial(adjoint_rest, rows, kernels),
        jax.ShapeDtypeStruct((rows, chan, lon), BF),
        [VMEM] * 6,
        150_000_000,
        1_500_000,
        [pltpu.VMEM((rows, chan, lon), BF), pltpu.SemaphoreType.DMA((rows,))],
        hbm,
    )(pred_grad, cross, chip, turned, tap_edge, w_bwd)
    parts, latent_grad = lax.optimization_barrier((parts, latent_grad))
    factor = 1.0 / math.sqrt(members * lat_count * lon)
    width = chan // members
    spread = call(
        functools.partial(band_sum, factor, variables, padded),
        jax.ShapeDtypeStruct((members, width, lon), BF),
        [VMEM] * 2,
        20_000_000,
        400_000,
    )(parts, w_bwd)
    spread = lax.all_to_all(spread, "ens", 0, 0, tiled=True)
    owned = call(
        member_sum, jax.ShapeDtypeStruct((kernels, own, width), F32), [VMEM], 100_000, 150_000
    )(spread)
    return latent_grad[None], owned.transpose(1, 0, 2)


def solution(mesh):
    placed = (P("ens", "lat", None, None), P("lat", None, None), P(), P(), P(), P())
    return jax.shard_map(
        body,
        mesh=mesh,
        in_specs=placed,
        out_specs=(P("ens", "lat", None, None), P("lat", None, "ens")),
        check_vma=False,
    )
```

```python
import functools
import math

import jax
import jax.numpy as jnp
import numpy as np
from jax import lax
from jax.experimental import pallas as pl
from jax.experimental.pallas import tpu as pltpu
from jax.sharding import PartitionSpec as P

HALO = 2
SIDE = 2
REACH = 2 * HALO + 1
DELTA = 0.25
BF = jnp.bfloat16
F32 = jnp.float32
VMEM = pl.BlockSpec(memory_space=pltpu.VMEM)


def smooth_slope(differ):
    return differ * lax.rsqrt(differ * differ + DELTA * DELTA)


def dot_nn(a, b):
    return lax.dot_general(a, b, (((1,), (0,)), ((), ())), preferred_element_type=F32)


def dot_nt(a, b):
    return lax.dot_general(a, b, (((1,), (1,)), ((), ())), preferred_element_type=F32)


def call(kernel, out, specs, flops, moved, scratch=(), home=VMEM):
    many = isinstance(out, (tuple, list))
    return pl.pallas_call(
        kernel,
        out_shape=out,
        in_specs=specs,
        out_specs=tuple([home] * len(out)) if many else home,
        scratch_shapes=list(scratch),
        compiler_params=pltpu.CompilerParams(vmem_limit_bytes=32 * 2**20),
        cost_estimate=pl.CostEstimate(flops=flops, bytes_accessed=moved, transcendentals=0),
    )


def odd_band():
    return (lax.axis_index("lat") & 1) == 1


def tap_block(lat_count, lag, band, rows, basis, offsets, source, step, put):
    kernels, lon = basis.shape[1], lag.shape[0]
    cycle = band * rows + source
    inside = jnp.logical_and(cycle >= 0, cycle < lat_count)
    cycle = jnp.clip(cycle, 0, lat_count - 1)
    one, two = SIDE * step, SIDE * step + 1
    off_one, off_two = offsets[one, cycle], offsets[two, cycle]
    mask_one = lag == (off_one & (lon - 1))
    mask_two = lag == (off_two & (lon - 1))
    for k in range(kernels):
        weight_one = jnp.where(inside, basis[one, k, cycle], 0.0)
        weight_two = jnp.where(inside, basis[two, k, cycle], 0.0)
        weight_two = weight_two + jnp.where(off_one == off_two, weight_one, 0.0)
        value = jnp.where(mask_two, weight_two, jnp.where(mask_one, weight_one, 0.0))
        put(k, value.astype(BF))


def edge_taps(rows, row):
    outside = list(range(-HALO, 0)) + list(range(rows, rows + HALO))
    return [(at, row - at + HALO) for at in outside if 0 <= row - at + HALO < REACH]


def lags(lon):
    return (lax.broadcasted_iota(jnp.int32, (lon, lon), 0) - lax.broadcasted_iota(jnp.int32, (lon, lon), 1)) & (lon - 1)


def padded_rows(dec_t, padded):
    rows, chan = dec_t.shape
    return jnp.concatenate([dec_t[...].astype(F32), jnp.zeros((padded - rows, chan), F32)], axis=0).astype(BF)


def prepare(
    rows, lat_count, basis_in, offsets_in, filters, dec_in, field,
    ahead, edge, w_fwd, w_bwd, near, held, dec_t, basis, offsets, sems,
):
    moves = ((offsets_in, offsets), (basis_in, basis), (dec_in, dec_t), (filters, held), (field, near))
    moves = [pltpu.make_async_copy(source, target, sems.at[n]) for n, (source, target) in enumerate(moves)]
    for move in moves:
        move.start()
    lon = ahead.shape[1] // REACH
    lag = lags(lon)
    band = lax.axis_index("lat")

    def block(source, step, put):
        tap_block(lat_count, lag, band, rows, basis, offsets, source, step, put)

    def ahead_put(row, step):
        def put(k, value):
            ahead[row, step * lon : (step + 1) * lon, k * lon : (k + 1) * lon] = value

        return put

    def edge_put(row, slot):
        def put(k, value):
            edge[row, k * lon : (k + 1) * lon, slot * lon : (slot + 1) * lon] = value

        return put

    for move in moves[:2]:
        move.wait()
    for row in range(rows):
        for step in range(REACH):
            block(row, step, ahead_put(row, step))
        for slot, (at, step) in enumerate(edge_taps(rows, row)):
            block(at, step, edge_put(row, slot))
    kernels, chan = held.shape[:2]
    padded = w_fwd.shape[0]
    for move in moves[2:]:
        move.wait()
    dec = padded_rows(dec_t, padded)

    square = (chan, chan)
    unit = lax.broadcasted_iota(jnp.int32, square, 0) == lax.broadcasted_iota(jnp.int32, square, 1)
    columns = [dot_nt(jnp.where(unit, 1.0, 0.0).astype(BF), dec)]
    w_fwd[:, :chan] = dec
    for k in range(kernels):
        w_fwd[:, (k + 1) * chan : (k + 2) * chan] = dot_nt(dec, held[k]).astype(BF)
        columns.append(dot_nt(held[k], dec))
    w_bwd[...] = jnp.concatenate(columns, axis=1).astype(BF)


def forward_own(rows, kernels, field, ahead, w_fwd, mixed, predicted):
    chan, lon = field.shape[1:]
    source = jnp.concatenate([field[i] for i in range(rows)], axis=1)
    for i in range(rows):
        mixed[i] = dot_nn(source, ahead[i, (HALO - i) * lon : (HALO - i + rows) * lon, :])
        predicted[i] = dot_nn(w_fwd[:, :chan], field[i])


def forward_rest(rows, kernels, cross, chip, begun, based, ahead, w_fwd, packed, predicted, mixed):
    chan, lon = cross.shape[1:]
    low, high = sides(odd_band(), cross, chip)
    outer = dict(enumerate(low, -HALO)) | dict(enumerate(high, rows))
    per = packed.shape[1]
    padded = predicted.shape[1]
    pieces = padded // per
    for i in range(rows):
        reach = [at for at in outer if 0 <= at - i + HALO < REACH]
        source = jnp.concatenate([outer[at] for at in reach], axis=1)
        steps = [at - i + HALO for at in reach]
        table = jnp.concatenate([ahead[i, step * lon : (step + 1) * lon, :] for step in steps], axis=0)
        taps = (begun[i] + dot_nn(source, table)).astype(BF)
        stack = [taps[:, k * lon : (k + 1) * lon] for k in range(kernels)]
        for k in range(kernels):
            mixed[i, k * chan : (k + 1) * chan, :] = stack[k]
        pred = based[i] + dot_nn(w_fwd[:, chan:], jnp.concatenate(stack, axis=0))
        predicted[i] = pred
        rounded = pred.astype(BF)
        for q in range(pieces):
            packed[i * pieces + q] = rounded[q * per : (q + 1) * per]
    for q in range(rows * pieces, packed.shape[0]):
        packed[q] = jnp.zeros(packed.shape[1:], BF)


def pairs(visitors, sums):
    members, height, _ = visitors.shape
    pieces = []
    for start in range(0, height, 8):
        values = [visitors[m].astype(F32)[start : start + 8] for m in range(members)]
        totals = [None] * members
        for m in range(members):
            for n in range(m + 1, members):
                slope = smooth_slope(values[m] - values[n])
                totals[m] = slope if totals[m] is None else totals[m] + slope
                totals[n] = -slope if totals[n] is None else totals[n] - slope
        pieces.append(totals)
    for m in range(members):
        sums[m] = jnp.concatenate([totals[m] for totals in pieces], axis=0).astype(BF)


def gradient(rows, kernels, members, area, sums, predicted, target, mixed, pred_grad, cross, chip, partial):
    variables = target.shape[1]
    padded = predicted.shape[1]
    per = sums.shape[1]
    pieces = padded // per
    lon = predicted.shape[2]
    chan = mixed.shape[1] // kernels
    grads, edges = [], []
    odd = odd_band()
    band = lax.axis_index("lat")
    for i in range(rows):
        pair_sum = jnp.concatenate([sums[i * pieces + q].astype(F32) for q in range(pieces)], axis=0)
        aim = jnp.concatenate([target[i].astype(F32), jnp.zeros((padded - variables, lon), F32)], axis=0)
        grad = area[pl.ds(band * rows + i, 1), :] * (smooth_slope(predicted[i] - aim) - pair_sum * (1.0 / (members - 1)))
        grad = grad.astype(BF)
        pred_grad[i] = grad
        edges.append(grad)
        grads.append(jnp.concatenate([grad, jnp.zeros((lon - padded, lon), BF)], axis=0))
    for n in range(HALO):
        top, bottom = edges[rows - HALO + n], edges[n]
        cross[n] = jnp.where(odd, top, bottom)
        chip[n] = jnp.where(odd, bottom, top)
    total = dot_nt(
        jnp.concatenate([mixed[i] for i in range(rows)], axis=1), jnp.concatenate(grads, axis=1)
    )
    first, second, third = [total[k * chan : (k + 1) * chan] for k in range(kernels)]
    lane = lax.broadcasted_iota(jnp.int32, first.shape, 1)
    spare = lon - variables
    upper = jnp.where(lane < variables, first, pltpu.roll(third, variables, 1))
    tail = jnp.where(lane < 2 * variables - spare, pltpu.roll(third, variables - spare, 1), 0.0)
    lower = jnp.where(lane < variables, second, tail)
    owners = partial.shape[0]
    own = chan // owners
    for owner in range(owners):
        mine = slice(owner * own, (owner + 1) * own)
        partial[owner] = jnp.concatenate([upper[mine], lower[mine]], axis=0).astype(BF)


def band_sum(factor, variables, padded, parts, w_bwd, spread):
    owners, height, lon = parts.shape
    total = parts[0].astype(F32)
    for owner in range(1, owners):
        total = total + parts[owner].astype(F32)
    total = total * factor
    own = height // 2
    spare = lon - variables
    lane = lax.broadcasted_iota(jnp.int32, (own, lon), 1)
    front = pltpu.roll(total[:own], lon - variables, 1)
    rest = pltpu.roll(total[own:], lon + spare - variables, 1)
    third = jnp.where(lane < spare, front, jnp.where(lane < variables, rest, 0.0))
    wide = lax.broadcasted_iota(jnp.int32, total.shape, 1)
    total = jnp.where(wide < variables, total, 0.0)
    total = jnp.concatenate([total, third, jnp.zeros((lon - height - own, lon), F32)], axis=0)
    upper = total.astype(BF)
    lower = (total - upper.astype(F32)).astype(BF)
    dec = w_bwd[:, :padded]
    result = dot_nt(dec, upper[:, :padded]) + dot_nt(dec, lower[:, :padded])
    per = spread.shape[1]
    for member in range(spread.shape[0]):
        spread[member] = result[member * per : (member + 1) * per].astype(BF)


def member_sum(parts, owned):
    kernels, own, width = owned.shape
    total = parts[0].astype(F32)
    for member in range(1, parts.shape[0]):
        total = total + parts[member].astype(F32)
    turned = total.T
    for k in range(kernels):
        owned[k] = turned[k * own : (k + 1) * own, :width]


def adjoint_own(rows, kernels, pred_grad, ahead, turned):
    lon = pred_grad.shape[2]
    for k in range(kernels):
        sums = [None] * rows
        for at in range(rows):
            least = HALO - at
            taps = ahead[at, least * lon : (least + rows) * lon, k * lon : (k + 1) * lon]
            found = dot_nt(pred_grad[at], taps)
            for row in range(rows):
                piece = found[:, row * lon : (row + 1) * lon]
                sums[row] = piece if sums[row] is None else sums[row] + piece
        for row in range(rows):
            turned[row, :, k * lon : (k + 1) * lon] = sums[row]


def adjoint_rest(rows, kernels, pred_grad, cross, chip, turned, edge, w_bwd, result, buffer, sems):
    lon = pred_grad.shape[2]
    low, high = sides(odd_band(), cross, chip)
    outer = dict(enumerate(low, -HALO)) | dict(enumerate(high, rows))
    moves = []
    for row in range(rows):
        sources = jnp.concatenate([outer[at] for at, _ in edge_taps(rows, row)], axis=1)
        taps = (turned[row] + dot_nt(sources, edge[row])).astype(BF)
        stack = [pred_grad[row]] + [taps[:, k * lon : (k + 1) * lon] for k in range(kernels)]
        buffer[row] = dot_nn(w_bwd[...], jnp.concatenate(stack, axis=0)).astype(BF)
        moves.append(pltpu.make_async_copy(buffer.at[row], result.at[row], sems.at[row]))
        moves[-1].start()
    for move in moves:
        move.wait()


def cut(field, cross, chip, sems):
    rows = field.shape[0]
    odd = lax.axis_index("lat") & 1
    far = (rows - HALO) * odd
    moves = [
        pltpu.make_async_copy(field.at[pl.ds(far, HALO)], cross, sems.at[0]),
        pltpu.make_async_copy(field.at[pl.ds(rows - HALO - far, HALO)], chip, sems.at[1]),
    ]
    for move in moves:
        move.start()
    for move in moves:
        move.wait()


def sides(odd, cross, chip):
    low = [jnp.where(odd, chip[n], cross[n]) for n in range(HALO)]
    high = [jnp.where(odd, cross[n], chip[n]) for n in range(HALO)]
    return low, high


def across(block, axis, start):
    count = lax.axis_size(axis)
    up = [(i, i + 1) for i in range(start, count - 1, 2)]
    return lax.ppermute(block, axis, up + [(b, a) for a, b in up])


def body(latent_fields, target_fields, filters, decoder, cycle_basis, cycle_offsets):
    field = latent_fields[0]
    rows, chan, lon = field.shape
    lat_count, kernels, taps = cycle_basis.shape
    variables = decoder.shape[1]
    members, bands = lax.axis_size("ens"), lax.axis_size("lat")
    per = 16
    padded = -(-variables // per) * per
    area = np.cos(np.pi * (np.arange(lat_count) + 0.5) / lat_count - np.pi / 2)
    area = jnp.asarray(np.broadcast_to(area[:, None], (lat_count, lon)), F32)
    dec_t = decoder.T
    basis = cycle_basis.transpose(2, 1, 0)
    offsets = cycle_offsets.T

    stay = functools.partial(pltpu.with_memory_space_constraint, memory_space=pltpu.HBM)
    hbm = pl.BlockSpec(memory_space=pltpu.HBM)
    edge = jax.ShapeDtypeStruct((HALO, chan, lon), BF)
    pair = pltpu.SemaphoreType.DMA((2,))
    cross, chip = call(cut, (edge, edge), [hbm], 0, 500_000, [pair])(stay(field))
    cross, chip = across(cross, "lat", 1), across(chip, "lat", 0)
    ahead, tap_edge, w_fwd, w_bwd, near = call(
        functools.partial(prepare, rows, lat_count),
        (
            jax.ShapeDtypeStruct((rows, REACH * lon, kernels * lon), BF),
            jax.ShapeDtypeStruct((rows, kernels * lon, (REACH - rows) * lon), BF),
            jax.ShapeDtypeStruct((padded, (kernels + 1) * chan), BF),
            jax.ShapeDtypeStruct((chan, (kernels + 1) * padded), BF),
            jax.ShapeDtypeStruct(field.shape, BF),
        ),
        [hbm] * 5,
        30_000_000,
        2_000_000,
        [
            pltpu.VMEM(filters.shape, BF),
            pltpu.VMEM(dec_t.shape, BF),
            pltpu.SMEM(basis.shape, F32),
            pltpu.SMEM(offsets.shape, jnp.int32),
            pltpu.SemaphoreType.DMA((5,)),
        ],
    )(stay(basis), stay(offsets), stay(filters), stay(dec_t), stay(field))
    begun, based = call(
        functools.partial(forward_own, rows, kernels),
        (jax.ShapeDtypeStruct((rows, chan, kernels * lon), F32), jax.ShapeDtypeStruct((rows, padded, lon), F32)),
        [VMEM] * 3,
        250_000_000,
        3_000_000,
    )(near, ahead, w_fwd)
    packed, predicted, mixed = call(
        functools.partial(forward_rest, rows, kernels),
        (
            jax.ShapeDtypeStruct((members, per, lon), BF),
            jax.ShapeDtypeStruct((rows, padded, lon), F32),
            jax.ShapeDtypeStruct((rows, kernels * chan, lon), BF),
        ),
        [VMEM] * 6,
        200_000_000,
        3_000_000,
    )(cross, chip, begun, based, ahead, w_fwd)
    visitors = lax.all_to_all(packed, "ens", 0, 0, tiled=True)
    sums = call(pairs, jax.ShapeDtypeStruct((members, per, lon), BF), [VMEM], 2_000_000, 200_000)(visitors)
    sums = lax.all_to_all(sums, "ens", 0, 0, tiled=True)
    own = chan // bands
    edge = jax.ShapeDtypeStruct((HALO, padded, lon), BF)
    pred_grad, cross, chip, partial = call(
        functools.partial(gradient, rows, kernels, members),
        (
            jax.ShapeDtypeStruct((rows, padded, lon), BF),
            edge,
            edge,
            jax.ShapeDtypeStruct((bands, 2 * own, lon), BF),
        ),
        [VMEM] * 5,
        80_000_000,
        1_200_000,
    )(area, sums, predicted, target_fields, mixed)
    parts = lax.all_to_all(partial, "lat", 0, 0, tiled=True)
    cross, chip = across(cross, "lat", 1), across(chip, "lat", 0)
    turned = call(
        functools.partial(adjoint_own, rows, kernels),
        jax.ShapeDtypeStruct((rows, padded, kernels * lon), F32),
        [VMEM] * 2,
        80_000_000,
        1_500_000,
    )(pred_grad, ahead)
    latent_grad = call(
        functools.partial(adjoint_rest, rows, kernels),
        jax.ShapeDtypeStruct((rows, chan, lon), BF),
        [VMEM] * 6,
        150_000_000,
        1_500_000,
        [pltpu.VMEM((rows, chan, lon), BF), pltpu.SemaphoreType.DMA((rows,))],
        hbm,
    )(pred_grad, cross, chip, turned, tap_edge, w_bwd)
    parts, latent_grad = lax.optimization_barrier((parts, latent_grad))
    factor = 1.0 / math.sqrt(members * lat_count * lon)
    width = chan // members
    spread = call(
        functools.partial(band_sum, factor, variables, padded),
        jax.ShapeDtypeStruct((members, width, lon), BF),
        [VMEM] * 2,
        20_000_000,
        400_000,
    )(parts, w_bwd)
    spread = lax.all_to_all(spread, "ens", 0, 0, tiled=True)
    owned = call(
        member_sum, jax.ShapeDtypeStruct((kernels, own, width), F32), [VMEM], 100_000, 150_000
    )(spread)
    return latent_grad[None], owned.transpose(1, 0, 2)


def solution(mesh):
    placed = (P("ens", "lat", None, None), P("lat", None, None), P(), P(), P(), P())
    return jax.shard_map(
        body,
        mesh=mesh,
        in_specs=placed,
        out_specs=(P("ens", "lat", None, None), P("lat", None, "ens")),
        check_vma=False,
    )
```

```python
import functools
import math

import jax
import jax.numpy as jnp
import numpy as np
from jax import lax
from jax.experimental import pallas as pl
from jax.experimental.pallas import tpu as pltpu
from jax.sharding import PartitionSpec as P

HALO = 2
SIDE = 2
REACH = 2 * HALO + 1
DELTA = 0.25
BF = jnp.bfloat16
F32 = jnp.float32
VMEM = pl.BlockSpec(memory_space=pltpu.VMEM)


def smooth_slope(differ):
    return differ * lax.rsqrt(differ * differ + DELTA * DELTA)


def dot_nn(a, b):
    return lax.dot_general(a, b, (((1,), (0,)), ((), ())), preferred_element_type=F32)


def dot_nt(a, b):
    return lax.dot_general(a, b, (((1,), (1,)), ((), ())), preferred_element_type=F32)


def call(kernel, out, specs, flops, moved, scratch=(), home=VMEM):
    many = isinstance(out, (tuple, list))
    return pl.pallas_call(
        kernel,
        out_shape=out,
        in_specs=specs,
        out_specs=tuple([home] * len(out)) if many else home,
        scratch_shapes=list(scratch),
        compiler_params=pltpu.CompilerParams(vmem_limit_bytes=32 * 2**20),
        cost_estimate=pl.CostEstimate(flops=flops, bytes_accessed=moved, transcendentals=0),
    )


def odd_band():
    return (lax.axis_index("lat") & 1) == 1


def tap_block(lat_count, lag, band, rows, basis, offsets, source, step, put):
    kernels, lon = basis.shape[1], lag.shape[0]
    cycle = band * rows + source
    inside = jnp.logical_and(cycle >= 0, cycle < lat_count)
    cycle = jnp.clip(cycle, 0, lat_count - 1)
    one, two = SIDE * step, SIDE * step + 1
    off_one, off_two = offsets[one, cycle], offsets[two, cycle]
    mask_one = lag == (off_one & (lon - 1))
    mask_two = lag == (off_two & (lon - 1))
    for k in range(kernels):
        weight_one = jnp.where(inside, basis[one, k, cycle], 0.0)
        weight_two = jnp.where(inside, basis[two, k, cycle], 0.0)
        weight_two = weight_two + jnp.where(off_one == off_two, weight_one, 0.0)
        value = jnp.where(mask_two, weight_two, jnp.where(mask_one, weight_one, 0.0))
        put(k, value.astype(BF))


def edge_taps(rows, row):
    outside = list(range(-HALO, 0)) + list(range(rows, rows + HALO))
    return [(at, row - at + HALO) for at in outside if 0 <= row - at + HALO < REACH]


def lags(lon):
    return (lax.broadcasted_iota(jnp.int32, (lon, lon), 0) - lax.broadcasted_iota(jnp.int32, (lon, lon), 1)) & (lon - 1)


def padded_rows(dec_t, padded):
    rows, chan = dec_t.shape
    return jnp.concatenate([dec_t[...].astype(F32), jnp.zeros((padded - rows, chan), F32)], axis=0).astype(BF)


def prepare(
    rows, lat_count, basis_in, offsets_in, filters, dec_in, field,
    ahead, edge, w_fwd, near, held, dec_t, basis, offsets, sems,
):
    moves = ((offsets_in, offsets), (basis_in, basis), (dec_in, dec_t), (filters, held), (field, near))
    moves = [pltpu.make_async_copy(source, target, sems.at[n]) for n, (source, target) in enumerate(moves)]
    for move in moves:
        move.start()
    lon = ahead.shape[1] // REACH
    lag = lags(lon)
    band = lax.axis_index("lat")

    def block(source, step, put):
        tap_block(lat_count, lag, band, rows, basis, offsets, source, step, put)

    def ahead_put(row, step):
        def put(k, value):
            ahead[row, step * lon : (step + 1) * lon, k * lon : (k + 1) * lon] = value

        return put

    def edge_put(row, slot):
        def put(k, value):
            edge[row, k * lon : (k + 1) * lon, slot * lon : (slot + 1) * lon] = value

        return put

    for move in moves[:2]:
        move.wait()
    for row in range(rows):
        for step in range(REACH):
            block(row, step, ahead_put(row, step))
        for slot, (at, step) in enumerate(edge_taps(rows, row)):
            block(at, step, edge_put(row, slot))
    kernels, chan = held.shape[:2]
    padded = w_fwd.shape[0]
    for move in moves[2:]:
        move.wait()
    dec = padded_rows(dec_t, padded)

    w_fwd[:, :chan] = dec
    for k in range(kernels):
        w_fwd[:, (k + 1) * chan : (k + 2) * chan] = dot_nt(dec, held[k]).astype(BF)


def forward_own(rows, kernels, field, ahead, w_fwd, mixed, predicted):
    chan, lon = field.shape[1:]
    source = jnp.concatenate([field[i] for i in range(rows)], axis=1)
    for i in range(rows):
        mixed[i] = dot_nn(source, ahead[i, (HALO - i) * lon : (HALO - i + rows) * lon, :])
        predicted[i] = dot_nn(w_fwd[:, :chan], field[i])


def forward_rest(rows, kernels, cross, chip, begun, based, ahead, w_fwd, packed, predicted, mixed):
    chan, lon = cross.shape[1:]
    low, high = sides(odd_band(), cross, chip)
    outer = dict(enumerate(low, -HALO)) | dict(enumerate(high, rows))
    per = packed.shape[1]
    padded = predicted.shape[1]
    pieces = padded // per
    for i in range(rows):
        reach = [at for at in outer if 0 <= at - i + HALO < REACH]
        source = jnp.concatenate([outer[at] for at in reach], axis=1)
        steps = [at - i + HALO for at in reach]
        table = jnp.concatenate([ahead[i, step * lon : (step + 1) * lon, :] for step in steps], axis=0)
        taps = (begun[i] + dot_nn(source, table)).astype(BF)
        stack = [taps[:, k * lon : (k + 1) * lon] for k in range(kernels)]
        for k in range(kernels):
            mixed[i, k * chan : (k + 1) * chan, :] = stack[k]
        pred = based[i] + dot_nn(w_fwd[:, chan:], jnp.concatenate(stack, axis=0))
        predicted[i] = pred
        rounded = pred.astype(BF)
        for q in range(pieces):
            packed[i * pieces + q] = rounded[q * per : (q + 1) * per]
    for q in range(rows * pieces, packed.shape[0]):
        packed[q] = jnp.zeros(packed.shape[1:], BF)


def pairs(visitors, sums):
    members, height, _ = visitors.shape
    pieces = []
    for start in range(0, height, 8):
        values = [visitors[m].astype(F32)[start : start + 8] for m in range(members)]
        totals = [None] * members
        for m in range(members):
            for n in range(m + 1, members):
                slope = smooth_slope(values[m] - values[n])
                totals[m] = slope if totals[m] is None else totals[m] + slope
                totals[n] = -slope if totals[n] is None else totals[n] - slope
        pieces.append(totals)
    for m in range(members):
        sums[m] = jnp.concatenate([totals[m] for totals in pieces], axis=0).astype(BF)


def gradient(rows, kernels, members, area, sums, predicted, target, mixed, pred_grad, cross, chip, partial):
    variables = target.shape[1]
    padded = predicted.shape[1]
    per = sums.shape[1]
    pieces = padded // per
    lon = predicted.shape[2]
    chan = mixed.shape[1] // kernels
    grads, edges = [], []
    odd = odd_band()
    band = lax.axis_index("lat")
    for i in range(rows):
        pair_sum = jnp.concatenate([sums[i * pieces + q].astype(F32) for q in range(pieces)], axis=0)
        aim = jnp.concatenate([target[i].astype(F32), jnp.zeros((padded - variables, lon), F32)], axis=0)
        grad = area[pl.ds(band * rows + i, 1), :] * (smooth_slope(predicted[i] - aim) - pair_sum * (1.0 / (members - 1)))
        grad = grad.astype(BF)
        pred_grad[i] = grad
        edges.append(grad)
        grads.append(jnp.concatenate([grad, jnp.zeros((lon - padded, lon), BF)], axis=0))
    for n in range(HALO):
        top, bottom = edges[rows - HALO + n], edges[n]
        cross[n] = jnp.where(odd, top, bottom)
        chip[n] = jnp.where(odd, bottom, top)
    total = dot_nt(
        jnp.concatenate([mixed[i] for i in range(rows)], axis=1), jnp.concatenate(grads, axis=1)
    )
    first, second, third = [total[k * chan : (k + 1) * chan] for k in range(kernels)]
    lane = lax.broadcasted_iota(jnp.int32, first.shape, 1)
    spare = lon - variables
    upper = jnp.where(lane < variables, first, pltpu.roll(third, variables, 1))
    tail = jnp.where(lane < 2 * variables - spare, pltpu.roll(third, variables - spare, 1), 0.0)
    lower = jnp.where(lane < variables, second, tail)
    owners = partial.shape[0]
    own = chan // owners
    for owner in range(owners):
        mine = slice(owner * own, (owner + 1) * own)
        partial[owner] = jnp.concatenate([upper[mine], lower[mine]], axis=0).astype(BF)


def band_sum(factor, variables, padded, parts, w_bwd, spread):
    owners, height, lon = parts.shape
    total = parts[0].astype(F32)
    for owner in range(1, owners):
        total = total + parts[owner].astype(F32)
    total = total * factor
    own = height // 2
    spare = lon - variables
    lane = lax.broadcasted_iota(jnp.int32, (own, lon), 1)
    front = pltpu.roll(total[:own], lon - variables, 1)
    rest = pltpu.roll(total[own:], lon + spare - variables, 1)
    third = jnp.where(lane < spare, front, jnp.where(lane < variables, rest, 0.0))
    wide = lax.broadcasted_iota(jnp.int32, total.shape, 1)
    total = jnp.where(wide < variables, total, 0.0)
    total = jnp.concatenate([total, third, jnp.zeros((lon - height - own, lon), F32)], axis=0)
    upper = total.astype(BF)
    lower = (total - upper.astype(F32)).astype(BF)
    dec = w_bwd[:, :padded]
    result = dot_nt(dec, upper[:, :padded]) + dot_nt(dec, lower[:, :padded])
    per = spread.shape[1]
    for member in range(spread.shape[0]):
        spread[member] = result[member * per : (member + 1) * per].astype(BF)


def member_sum(parts, owned):
    kernels, own, width = owned.shape
    total = parts[0].astype(F32)
    for member in range(1, parts.shape[0]):
        total = total + parts[member].astype(F32)
    turned = total.T
    for k in range(kernels):
        owned[k] = turned[k * own : (k + 1) * own, :width]


def adjoint_own(rows, kernels, pred_grad, ahead, held, w_fwd, turned, w_bwd):
    chan = held.shape[1]
    dec = w_fwd[:, :chan]
    square = (chan, chan)
    unit = lax.broadcasted_iota(jnp.int32, square, 0) == lax.broadcasted_iota(jnp.int32, square, 1)
    columns = [dot_nt(jnp.where(unit, 1.0, 0.0).astype(BF), dec)]
    columns = columns + [dot_nt(held[k], dec) for k in range(kernels)]
    w_bwd[...] = jnp.concatenate(columns, axis=1).astype(BF)
    lon = pred_grad.shape[2]
    for k in range(kernels):
        sums = [None] * rows
        for at in range(rows):
            least = HALO - at
            taps = ahead[at, least * lon : (least + rows) * lon, k * lon : (k + 1) * lon]
            found = dot_nt(pred_grad[at], taps)
            for row in range(rows):
                piece = found[:, row * lon : (row + 1) * lon]
                sums[row] = piece if sums[row] is None else sums[row] + piece
        for row in range(rows):
            turned[row, :, k * lon : (k + 1) * lon] = sums[row]


def adjoint_rest(rows, kernels, pred_grad, cross, chip, turned, edge, w_bwd, result, buffer, sems):
    lon = pred_grad.shape[2]
    low, high = sides(odd_band(), cross, chip)
    outer = dict(enumerate(low, -HALO)) | dict(enumerate(high, rows))
    moves = []
    for row in range(rows):
        sources = jnp.concatenate([outer[at] for at, _ in edge_taps(rows, row)], axis=1)
        taps = (turned[row] + dot_nt(sources, edge[row])).astype(BF)
        stack = [pred_grad[row]] + [taps[:, k * lon : (k + 1) * lon] for k in range(kernels)]
        buffer[row] = dot_nn(w_bwd[...], jnp.concatenate(stack, axis=0)).astype(BF)
        moves.append(pltpu.make_async_copy(buffer.at[row], result.at[row], sems.at[row]))
        moves[-1].start()
    for move in moves:
        move.wait()


def cut(field, cross, chip, sems):
    rows = field.shape[0]
    odd = lax.axis_index("lat") & 1
    far = (rows - HALO) * odd
    moves = [
        pltpu.make_async_copy(field.at[pl.ds(far, HALO)], cross, sems.at[0]),
        pltpu.make_async_copy(field.at[pl.ds(rows - HALO - far, HALO)], chip, sems.at[1]),
    ]
    for move in moves:
        move.start()
    for move in moves:
        move.wait()


def sides(odd, cross, chip):
    low = [jnp.where(odd, chip[n], cross[n]) for n in range(HALO)]
    high = [jnp.where(odd, cross[n], chip[n]) for n in range(HALO)]
    return low, high


def across(block, axis, start):
    count = lax.axis_size(axis)
    up = [(i, i + 1) for i in range(start, count - 1, 2)]
    return lax.ppermute(block, axis, up + [(b, a) for a, b in up])


def body(latent_fields, target_fields, filters, decoder, cycle_basis, cycle_offsets):
    field = latent_fields[0]
    rows, chan, lon = field.shape
    lat_count, kernels, taps = cycle_basis.shape
    variables = decoder.shape[1]
    members, bands = lax.axis_size("ens"), lax.axis_size("lat")
    per = 16
    padded = -(-variables // per) * per
    area = np.cos(np.pi * (np.arange(lat_count) + 0.5) / lat_count - np.pi / 2)
    area = jnp.asarray(np.broadcast_to(area[:, None], (lat_count, lon)), F32)
    dec_t = decoder.T
    basis = cycle_basis.transpose(2, 1, 0)
    offsets = cycle_offsets.T

    stay = functools.partial(pltpu.with_memory_space_constraint, memory_space=pltpu.HBM)
    hbm = pl.BlockSpec(memory_space=pltpu.HBM)
    edge = jax.ShapeDtypeStruct((HALO, chan, lon), BF)
    pair = pltpu.SemaphoreType.DMA((2,))
    cross, chip = call(cut, (edge, edge), [hbm], 0, 500_000, [pair])(stay(field))
    cross, chip = across(cross, "lat", 1), across(chip, "lat", 0)
    ahead, tap_edge, w_fwd, near, held = call(
        functools.partial(prepare, rows, lat_count),
        (
            jax.ShapeDtypeStruct((rows, REACH * lon, kernels * lon), BF),
            jax.ShapeDtypeStruct((rows, kernels * lon, (REACH - rows) * lon), BF),
            jax.ShapeDtypeStruct((padded, (kernels + 1) * chan), BF),
            jax.ShapeDtypeStruct(field.shape, BF),
            jax.ShapeDtypeStruct(filters.shape, BF),
        ),
        [hbm] * 5,
        30_000_000,
        2_000_000,
        [
            pltpu.VMEM(dec_t.shape, BF),
            pltpu.SMEM(basis.shape, F32),
            pltpu.SMEM(offsets.shape, jnp.int32),
            pltpu.SemaphoreType.DMA((5,)),
        ],
    )(stay(basis), stay(offsets), stay(filters), stay(dec_t), stay(field))
    begun, based = call(
        functools.partial(forward_own, rows, kernels),
        (jax.ShapeDtypeStruct((rows, chan, kernels * lon), F32), jax.ShapeDtypeStruct((rows, padded, lon), F32)),
        [VMEM] * 3,
        250_000_000,
        3_000_000,
    )(near, ahead, w_fwd)
    packed, predicted, mixed = call(
        functools.partial(forward_rest, rows, kernels),
        (
            jax.ShapeDtypeStruct((members, per, lon), BF),
            jax.ShapeDtypeStruct((rows, padded, lon), F32),
            jax.ShapeDtypeStruct((rows, kernels * chan, lon), BF),
        ),
        [VMEM] * 6,
        200_000_000,
        3_000_000,
    )(cross, chip, begun, based, ahead, w_fwd)
    visitors = lax.all_to_all(packed, "ens", 0, 0, tiled=True)
    sums = call(pairs, jax.ShapeDtypeStruct((members, per, lon), BF), [VMEM], 2_000_000, 200_000)(visitors)
    sums = lax.all_to_all(sums, "ens", 0, 0, tiled=True)
    own = chan // bands
    edge = jax.ShapeDtypeStruct((HALO, padded, lon), BF)
    pred_grad, cross, chip, partial = call(
        functools.partial(gradient, rows, kernels, members),
        (
            jax.ShapeDtypeStruct((rows, padded, lon), BF),
            edge,
            edge,
            jax.ShapeDtypeStruct((bands, 2 * own, lon), BF),
        ),
        [VMEM] * 5,
        80_000_000,
        1_200_000,
    )(area, sums, predicted, target_fields, mixed)
    parts = lax.all_to_all(partial, "lat", 0, 0, tiled=True)
    cross, chip = across(cross, "lat", 1), across(chip, "lat", 0)
    turned, w_bwd = call(
        functools.partial(adjoint_own, rows, kernels),
        (
            jax.ShapeDtypeStruct((rows, padded, kernels * lon), F32),
            jax.ShapeDtypeStruct((chan, (kernels + 1) * padded), BF),
        ),
        [VMEM] * 4,
        120_000_000,
        2_000_000,
    )(pred_grad, ahead, held, w_fwd)
    latent_grad = call(
        functools.partial(adjoint_rest, rows, kernels),
        jax.ShapeDtypeStruct((rows, chan, lon), BF),
        [VMEM] * 6,
        150_000_000,
        1_500_000,
        [pltpu.VMEM((rows, chan, lon), BF), pltpu.SemaphoreType.DMA((rows,))],
        hbm,
    )(pred_grad, cross, chip, turned, tap_edge, w_bwd)
    parts, latent_grad = lax.optimization_barrier((parts, latent_grad))
    factor = 1.0 / math.sqrt(members * lat_count * lon)
    width = chan // members
    spread = call(
        functools.partial(band_sum, factor, variables, padded),
        jax.ShapeDtypeStruct((members, width, lon), BF),
        [VMEM] * 2,
        20_000_000,
        400_000,
    )(parts, w_bwd)
    spread = lax.all_to_all(spread, "ens", 0, 0, tiled=True)
    owned = call(
        member_sum, jax.ShapeDtypeStruct((kernels, own, width), F32), [VMEM], 100_000, 150_000
    )(spread)
    return latent_grad[None], owned.transpose(1, 0, 2)


def solution(mesh):
    placed = (P("ens", "lat", None, None), P("lat", None, None), P(), P(), P(), P())
    return jax.shard_map(
        body,
        mesh=mesh,
        in_specs=placed,
        out_specs=(P("ens", "lat", None, None), P("lat", None, "ens")),
        check_vma=False,
    )
```

```python
import functools
import math

import jax
import jax.numpy as jnp
import numpy as np
from jax import lax
from jax.experimental import pallas as pl
from jax.experimental.pallas import tpu as pltpu
from jax.sharding import PartitionSpec as P

HALO = 2
SIDE = 2
REACH = 2 * HALO + 1
DELTA = 0.25
BF = jnp.bfloat16
F32 = jnp.float32
VMEM = pl.BlockSpec(memory_space=pltpu.VMEM)


def smooth_slope(differ):
    return differ * lax.rsqrt(differ * differ + DELTA * DELTA)


def dot_nn(a, b):
    return lax.dot_general(a, b, (((1,), (0,)), ((), ())), preferred_element_type=F32)


def dot_nt(a, b):
    return lax.dot_general(a, b, (((1,), (1,)), ((), ())), preferred_element_type=F32)


def call(kernel, out, specs, flops, moved, scratch=(), home=VMEM):
    many = isinstance(out, (tuple, list))
    return pl.pallas_call(
        kernel,
        out_shape=out,
        in_specs=specs,
        out_specs=tuple(home if isinstance(home, list) else [home] * len(out)) if many else home,
        scratch_shapes=list(scratch),
        compiler_params=pltpu.CompilerParams(vmem_limit_bytes=32 * 2**20),
        cost_estimate=pl.CostEstimate(flops=flops, bytes_accessed=moved, transcendentals=0),
    )


def odd_band():
    return (lax.axis_index("lat") & 1) == 1


def tap_block(lat_count, lag, band, rows, basis, offsets, source, step, put):
    kernels, lon = basis.shape[1], lag.shape[0]
    cycle = band * rows + source
    inside = jnp.logical_and(cycle >= 0, cycle < lat_count)
    cycle = jnp.clip(cycle, 0, lat_count - 1)
    one, two = SIDE * step, SIDE * step + 1
    off_one, off_two = offsets[one, cycle], offsets[two, cycle]
    mask_one = lag == (off_one & (lon - 1))
    mask_two = lag == (off_two & (lon - 1))
    for k in range(kernels):
        weight_one = jnp.where(inside, basis[one, k, cycle], 0.0)
        weight_two = jnp.where(inside, basis[two, k, cycle], 0.0)
        weight_two = weight_two + jnp.where(off_one == off_two, weight_one, 0.0)
        value = jnp.where(mask_two, weight_two, jnp.where(mask_one, weight_one, 0.0))
        put(k, value.astype(BF))


def edge_taps(rows, row):
    outside = list(range(-HALO, 0)) + list(range(rows, rows + HALO))
    return [(at, row - at + HALO) for at in outside if 0 <= row - at + HALO < REACH]


def lags(lon):
    return (lax.broadcasted_iota(jnp.int32, (lon, lon), 0) - lax.broadcasted_iota(jnp.int32, (lon, lon), 1)) & (lon - 1)


def padded_rows(dec_t, padded):
    rows, chan = dec_t.shape
    return jnp.concatenate([dec_t[...].astype(F32), jnp.zeros((padded - rows, chan), F32)], axis=0).astype(BF)


def prepare(
    rows, lat_count, basis_in, offsets_in, filters, dec_in, field,
    ahead, edge, w_fwd, w_bwd, near, held, dec_t, basis, offsets, sems,
):
    moves = ((offsets_in, offsets), (basis_in, basis), (dec_in, dec_t), (filters, held), (field, near))
    moves = [pltpu.make_async_copy(source, target, sems.at[n]) for n, (source, target) in enumerate(moves)]
    for move in moves:
        move.start()
    lon = ahead.shape[1] // REACH
    lag = lags(lon)
    band = lax.axis_index("lat")

    def block(source, step, put):
        tap_block(lat_count, lag, band, rows, basis, offsets, source, step, put)

    def ahead_put(row, step):
        def put(k, value):
            ahead[row, step * lon : (step + 1) * lon, k * lon : (k + 1) * lon] = value

        return put

    def edge_put(row, slot):
        def put(k, value):
            edge[row, k * lon : (k + 1) * lon, slot * lon : (slot + 1) * lon] = value

        return put

    for move in moves[:2]:
        move.wait()
    for row in range(rows):
        for step in range(REACH):
            block(row, step, ahead_put(row, step))
        for slot, (at, step) in enumerate(edge_taps(rows, row)):
            block(at, step, edge_put(row, slot))
    kernels, chan = held.shape[:2]
    padded = w_fwd.shape[0]
    for move in moves[2:]:
        move.wait()
    dec = padded_rows(dec_t, padded)

    square = (chan, chan)
    unit = lax.broadcasted_iota(jnp.int32, square, 0) == lax.broadcasted_iota(jnp.int32, square, 1)
    columns = [dot_nt(jnp.where(unit, 1.0, 0.0).astype(BF), dec)]
    w_fwd[:, :chan] = dec
    for k in range(kernels):
        w_fwd[:, (k + 1) * chan : (k + 2) * chan] = dot_nt(dec, held[k]).astype(BF)
        columns.append(dot_nt(held[k], dec))
    w_bwd[...] = jnp.concatenate(columns, axis=1).astype(BF)


def forward_own(rows, kernels, field, ahead, w_fwd, mixed, predicted):
    chan, lon = field.shape[1:]
    source = jnp.concatenate([field[i] for i in range(rows)], axis=1)
    for i in range(rows):
        mixed[i] = dot_nn(source, ahead[i, (HALO - i) * lon : (HALO - i + rows) * lon, :])
        predicted[i] = dot_nn(w_fwd[:, :chan], field[i])


def forward_rest(rows, kernels, cross, chip, begun, based, ahead, w_fwd, packed, predicted, mixed):
    chan, lon = cross.shape[1:]
    low, high = sides(odd_band(), cross, chip)
    outer = dict(enumerate(low, -HALO)) | dict(enumerate(high, rows))
    per = packed.shape[1]
    padded = predicted.shape[1]
    pieces = padded // per
    for i in range(rows):
        reach = [at for at in outer if 0 <= at - i + HALO < REACH]
        source = jnp.concatenate([outer[at] for at in reach], axis=1)
        steps = [at - i + HALO for at in reach]
        table = jnp.concatenate([ahead[i, step * lon : (step + 1) * lon, :] for step in steps], axis=0)
        taps = (begun[i] + dot_nn(source, table)).astype(BF)
        stack = [taps[:, k * lon : (k + 1) * lon] for k in range(kernels)]
        for k in range(kernels):
            mixed[i, k * chan : (k + 1) * chan, :] = stack[k]
        pred = based[i] + dot_nn(w_fwd[:, chan:], jnp.concatenate(stack, axis=0))
        predicted[i] = pred
        rounded = pred.astype(BF)
        for q in range(pieces):
            packed[i * pieces + q] = rounded[q * per : (q + 1) * per]
    for q in range(rows * pieces, packed.shape[0]):
        packed[q] = jnp.zeros(packed.shape[1:], BF)


def pairs(visitors, sums):
    members, height, _ = visitors.shape
    pieces = []
    for start in range(0, height, 8):
        values = [visitors[m].astype(F32)[start : start + 8] for m in range(members)]
        totals = [None] * members
        for m in range(members):
            for n in range(m + 1, members):
                slope = smooth_slope(values[m] - values[n])
                totals[m] = slope if totals[m] is None else totals[m] + slope
                totals[n] = -slope if totals[n] is None else totals[n] - slope
        pieces.append(totals)
    for m in range(members):
        sums[m] = jnp.concatenate([totals[m] for totals in pieces], axis=0).astype(BF)


def gradient(rows, kernels, members, area, sums, predicted, target, mixed, pred_grad, cross, chip, partial, buffer, sems):
    variables = target.shape[1]
    padded = predicted.shape[1]
    per = sums.shape[1]
    pieces = padded // per
    lon = predicted.shape[2]
    chan = mixed.shape[1] // kernels
    grads, edges = [], []
    odd = odd_band()
    band = lax.axis_index("lat")
    for i in range(rows):
        pair_sum = jnp.concatenate([sums[i * pieces + q].astype(F32) for q in range(pieces)], axis=0)
        aim = jnp.concatenate([target[i].astype(F32), jnp.zeros((padded - variables, lon), F32)], axis=0)
        grad = area[pl.ds(band * rows + i, 1), :] * (smooth_slope(predicted[i] - aim) - pair_sum * (1.0 / (members - 1)))
        grad = grad.astype(BF)
        pred_grad[i] = grad
        edges.append(grad)
        grads.append(jnp.concatenate([grad, jnp.zeros((lon - padded, lon), BF)], axis=0))
    for n in range(HALO):
        top, bottom = edges[rows - HALO + n], edges[n]
        cross[n] = jnp.where(odd, top, bottom)
        chip[n] = jnp.where(odd, bottom, top)
    total = dot_nt(
        jnp.concatenate([mixed[i] for i in range(rows)], axis=1), jnp.concatenate(grads, axis=1)
    )
    first, second, third = [total[k * chan : (k + 1) * chan] for k in range(kernels)]
    lane = lax.broadcasted_iota(jnp.int32, first.shape, 1)
    spare = lon - variables
    upper = jnp.where(lane < variables, first, pltpu.roll(third, variables, 1))
    tail = jnp.where(lane < 2 * variables - spare, pltpu.roll(third, variables - spare, 1), 0.0)
    lower = jnp.where(lane < variables, second, tail)
    owners = partial.shape[0]
    own = chan // owners
    groups = sems.shape[0]
    size = owners // groups
    moves = []
    for group in range(groups):
        for owner in range(group * size, (group + 1) * size):
            mine = slice(owner * own, (owner + 1) * own)
            buffer[owner] = jnp.concatenate([upper[mine], lower[mine]], axis=0).astype(BF)
        part = pl.ds(group * size, size)
        moves.append(pltpu.make_async_copy(buffer.at[part], partial.at[part], sems.at[group]))
        moves[-1].start()
    for move in moves:
        move.wait()


def band_sum(factor, variables, padded, parts, w_bwd, spread):
    owners, height, lon = parts.shape
    total = parts[0].astype(F32)
    for owner in range(1, owners):
        total = total + parts[owner].astype(F32)
    total = total * factor
    own = height // 2
    spare = lon - variables
    lane = lax.broadcasted_iota(jnp.int32, (own, lon), 1)
    front = pltpu.roll(total[:own], lon - variables, 1)
    rest = pltpu.roll(total[own:], lon + spare - variables, 1)
    third = jnp.where(lane < spare, front, jnp.where(lane < variables, rest, 0.0))
    wide = lax.broadcasted_iota(jnp.int32, total.shape, 1)
    total = jnp.where(wide < variables, total, 0.0)
    total = jnp.concatenate([total, third, jnp.zeros((lon - height - own, lon), F32)], axis=0)
    upper = total.astype(BF)
    lower = (total - upper.astype(F32)).astype(BF)
    dec = w_bwd[:, :padded]
    result = dot_nt(dec, upper[:, :padded]) + dot_nt(dec, lower[:, :padded])
    per = spread.shape[1]
    for member in range(spread.shape[0]):
        spread[member] = result[member * per : (member + 1) * per].astype(BF)


def member_sum(parts, owned):
    kernels, own, width = owned.shape
    total = parts[0].astype(F32)
    for member in range(1, parts.shape[0]):
        total = total + parts[member].astype(F32)
    turned = total.T
    for k in range(kernels):
        owned[k] = turned[k * own : (k + 1) * own, :width]


def adjoint_own(rows, kernels, pred_grad, ahead, turned):
    lon = pred_grad.shape[2]
    for k in range(kernels):
        sums = [None] * rows
        for at in range(rows):
            least = HALO - at
            taps = ahead[at, least * lon : (least + rows) * lon, k * lon : (k + 1) * lon]
            found = dot_nt(pred_grad[at], taps)
            for row in range(rows):
                piece = found[:, row * lon : (row + 1) * lon]
                sums[row] = piece if sums[row] is None else sums[row] + piece
        for row in range(rows):
            turned[row, :, k * lon : (k + 1) * lon] = sums[row]


def adjoint_rest(rows, kernels, pred_grad, cross, chip, turned, edge, w_bwd, result, buffer, sems):
    lon = pred_grad.shape[2]
    low, high = sides(odd_band(), cross, chip)
    outer = dict(enumerate(low, -HALO)) | dict(enumerate(high, rows))
    moves = []
    for row in range(rows):
        sources = jnp.concatenate([outer[at] for at, _ in edge_taps(rows, row)], axis=1)
        taps = (turned[row] + dot_nt(sources, edge[row])).astype(BF)
        stack = [pred_grad[row]] + [taps[:, k * lon : (k + 1) * lon] for k in range(kernels)]
        buffer[row] = dot_nn(w_bwd[...], jnp.concatenate(stack, axis=0)).astype(BF)
        moves.append(pltpu.make_async_copy(buffer.at[row], result.at[row], sems.at[row]))
        moves[-1].start()
    for move in moves:
        move.wait()


def cut(field, cross, chip, sems):
    rows = field.shape[0]
    odd = lax.axis_index("lat") & 1
    far = (rows - HALO) * odd
    moves = [
        pltpu.make_async_copy(field.at[pl.ds(far, HALO)], cross, sems.at[0]),
        pltpu.make_async_copy(field.at[pl.ds(rows - HALO - far, HALO)], chip, sems.at[1]),
    ]
    for move in moves:
        move.start()
    for move in moves:
        move.wait()


def sides(odd, cross, chip):
    low = [jnp.where(odd, chip[n], cross[n]) for n in range(HALO)]
    high = [jnp.where(odd, cross[n], chip[n]) for n in range(HALO)]
    return low, high


def across(block, axis, start):
    count = lax.axis_size(axis)
    up = [(i, i + 1) for i in range(start, count - 1, 2)]
    return lax.ppermute(block, axis, up + [(b, a) for a, b in up])


def body(latent_fields, target_fields, filters, decoder, cycle_basis, cycle_offsets):
    field = latent_fields[0]
    rows, chan, lon = field.shape
    lat_count, kernels, taps = cycle_basis.shape
    variables = decoder.shape[1]
    members, bands = lax.axis_size("ens"), lax.axis_size("lat")
    per = 16
    padded = -(-variables // per) * per
    area = np.cos(np.pi * (np.arange(lat_count) + 0.5) / lat_count - np.pi / 2)
    area = jnp.asarray(np.broadcast_to(area[:, None], (lat_count, lon)), F32)
    dec_t = decoder.T
    basis = cycle_basis.transpose(2, 1, 0)
    offsets = cycle_offsets.T

    stay = functools.partial(pltpu.with_memory_space_constraint, memory_space=pltpu.HBM)
    hbm = pl.BlockSpec(memory_space=pltpu.HBM)
    edge = jax.ShapeDtypeStruct((HALO, chan, lon), BF)
    pair = pltpu.SemaphoreType.DMA((2,))
    cross, chip = call(cut, (edge, edge), [hbm], 0, 500_000, [pair])(stay(field))
    cross, chip = across(cross, "lat", 1), across(chip, "lat", 0)
    ahead, tap_edge, w_fwd, w_bwd, near = call(
        functools.partial(prepare, rows, lat_count),
        (
            jax.ShapeDtypeStruct((rows, REACH * lon, kernels * lon), BF),
            jax.ShapeDtypeStruct((rows, kernels * lon, (REACH - rows) * lon), BF),
            jax.ShapeDtypeStruct((padded, (kernels + 1) * chan), BF),
            jax.ShapeDtypeStruct((chan, (kernels + 1) * padded), BF),
            jax.ShapeDtypeStruct(field.shape, BF),
        ),
        [hbm] * 5,
        30_000_000,
        2_000_000,
        [
            pltpu.VMEM(filters.shape, BF),
            pltpu.VMEM(dec_t.shape, BF),
            pltpu.SMEM(basis.shape, F32),
            pltpu.SMEM(offsets.shape, jnp.int32),
            pltpu.SemaphoreType.DMA((5,)),
        ],
    )(stay(basis), stay(offsets), stay(filters), stay(dec_t), stay(field))
    begun, based = call(
        functools.partial(forward_own, rows, kernels),
        (jax.ShapeDtypeStruct((rows, chan, kernels * lon), F32), jax.ShapeDtypeStruct((rows, padded, lon), F32)),
        [VMEM] * 3,
        250_000_000,
        3_000_000,
    )(near, ahead, w_fwd)
    packed, predicted, mixed = call(
        functools.partial(forward_rest, rows, kernels),
        (
            jax.ShapeDtypeStruct((members, per, lon), BF),
            jax.ShapeDtypeStruct((rows, padded, lon), F32),
            jax.ShapeDtypeStruct((rows, kernels * chan, lon), BF),
        ),
        [VMEM] * 6,
        200_000_000,
        3_000_000,
    )(cross, chip, begun, based, ahead, w_fwd)
    visitors = lax.all_to_all(packed, "ens", 0, 0, tiled=True)
    sums = call(pairs, jax.ShapeDtypeStruct((members, per, lon), BF), [VMEM], 2_000_000, 200_000)(visitors)
    sums = lax.all_to_all(sums, "ens", 0, 0, tiled=True)
    own = chan // bands
    edge = jax.ShapeDtypeStruct((HALO, padded, lon), BF)
    pred_grad, cross, chip, partial = call(
        functools.partial(gradient, rows, kernels, members),
        (
            jax.ShapeDtypeStruct((rows, padded, lon), BF),
            edge,
            edge,
            jax.ShapeDtypeStruct((bands, 2 * own, lon), BF),
        ),
        [VMEM] * 5,
        80_000_000,
        1_200_000,
        [pltpu.VMEM((bands, 2 * own, lon), BF), pltpu.SemaphoreType.DMA((4,))],
        [VMEM, VMEM, VMEM, hbm],
    )(area, sums, predicted, target_fields, mixed)
    parts = lax.all_to_all(partial, "lat", 0, 0, tiled=True)
    cross, chip = across(cross, "lat", 1), across(chip, "lat", 0)
    turned = call(
        functools.partial(adjoint_own, rows, kernels),
        jax.ShapeDtypeStruct((rows, padded, kernels * lon), F32),
        [VMEM] * 2,
        80_000_000,
        1_500_000,
    )(pred_grad, ahead)
    latent_grad = call(
        functools.partial(adjoint_rest, rows, kernels),
        jax.ShapeDtypeStruct((rows, chan, lon), BF),
        [VMEM] * 6,
        150_000_000,
        1_500_000,
        [pltpu.VMEM((rows, chan, lon), BF), pltpu.SemaphoreType.DMA((rows,))],
        hbm,
    )(pred_grad, cross, chip, turned, tap_edge, w_bwd)
    parts, latent_grad = lax.optimization_barrier((parts, latent_grad))
    factor = 1.0 / math.sqrt(members * lat_count * lon)
    width = chan // members
    spread = call(
        functools.partial(band_sum, factor, variables, padded),
        jax.ShapeDtypeStruct((members, width, lon), BF),
        [VMEM] * 2,
        20_000_000,
        400_000,
    )(parts, w_bwd)
    spread = lax.all_to_all(spread, "ens", 0, 0, tiled=True)
    owned = call(
        member_sum, jax.ShapeDtypeStruct((kernels, own, width), F32), [VMEM], 100_000, 150_000
    )(spread)
    return latent_grad[None], owned.transpose(1, 0, 2)


def solution(mesh):
    placed = (P("ens", "lat", None, None), P("lat", None, None), P(), P(), P(), P())
    return jax.shard_map(
        body,
        mesh=mesh,
        in_specs=placed,
        out_specs=(P("ens", "lat", None, None), P("lat", None, "ens")),
        check_vma=False,
    )
```

```python
import functools
import math

import jax
import jax.numpy as jnp
import numpy as np
from jax import lax
from jax.experimental import pallas as pl
from jax.experimental.pallas import tpu as pltpu
from jax.sharding import PartitionSpec as P

HALO = 2
SIDE = 2
REACH = 2 * HALO + 1
DELTA = 0.25
BF = jnp.bfloat16
F32 = jnp.float32
VMEM = pl.BlockSpec(memory_space=pltpu.VMEM)


def smooth_slope(differ):
    return differ * lax.rsqrt(differ * differ + DELTA * DELTA)


def dot_nn(a, b):
    return lax.dot_general(a, b, (((1,), (0,)), ((), ())), preferred_element_type=F32)


def dot_nt(a, b):
    return lax.dot_general(a, b, (((1,), (1,)), ((), ())), preferred_element_type=F32)


def call(kernel, out, specs, flops, moved, scratch=(), home=VMEM):
    many = isinstance(out, (tuple, list))
    return pl.pallas_call(
        kernel,
        out_shape=out,
        in_specs=specs,
        out_specs=tuple(home if isinstance(home, list) else [home] * len(out)) if many else home,
        scratch_shapes=list(scratch),
        compiler_params=pltpu.CompilerParams(vmem_limit_bytes=32 * 2**20),
        cost_estimate=pl.CostEstimate(flops=flops, bytes_accessed=moved, transcendentals=0),
    )


def odd_band():
    return (lax.axis_index("lat") & 1) == 1


def tap_block(lat_count, lag, band, rows, basis, offsets, source, step, put):
    kernels, lon = basis.shape[1], lag.shape[0]
    cycle = band * rows + source
    inside = jnp.logical_and(cycle >= 0, cycle < lat_count)
    cycle = jnp.clip(cycle, 0, lat_count - 1)
    one, two = SIDE * step, SIDE * step + 1
    off_one, off_two = offsets[one, cycle], offsets[two, cycle]
    mask_one = lag == (off_one & (lon - 1))
    mask_two = lag == (off_two & (lon - 1))
    for k in range(kernels):
        weight_one = jnp.where(inside, basis[one, k, cycle], 0.0)
        weight_two = jnp.where(inside, basis[two, k, cycle], 0.0)
        weight_two = weight_two + jnp.where(off_one == off_two, weight_one, 0.0)
        value = jnp.where(mask_two, weight_two, jnp.where(mask_one, weight_one, 0.0))
        put(k, value.astype(BF))


def edge_taps(rows, row):
    outside = list(range(-HALO, 0)) + list(range(rows, rows + HALO))
    return [(at, row - at + HALO) for at in outside if 0 <= row - at + HALO < REACH]


def lags(lon):
    return (lax.broadcasted_iota(jnp.int32, (lon, lon), 0) - lax.broadcasted_iota(jnp.int32, (lon, lon), 1)) & (lon - 1)


def padded_rows(dec_t, padded):
    rows, chan = dec_t.shape
    return jnp.concatenate([dec_t[...].astype(F32), jnp.zeros((padded - rows, chan), F32)], axis=0).astype(BF)


def prepare(
    rows, lat_count, basis_in, offsets_in, filters, dec_in, field,
    ahead, edge, w_fwd, near, held, dec_t, basis, offsets, sems,
):
    moves = ((offsets_in, offsets), (basis_in, basis), (dec_in, dec_t), (filters, held), (field, near))
    moves = [pltpu.make_async_copy(source, target, sems.at[n]) for n, (source, target) in enumerate(moves)]
    for move in moves:
        move.start()
    lon = ahead.shape[1] // REACH
    lag = lags(lon)
    band = lax.axis_index("lat")

    def block(source, step, put):
        tap_block(lat_count, lag, band, rows, basis, offsets, source, step, put)

    def ahead_put(row, step):
        def put(k, value):
            ahead[row, step * lon : (step + 1) * lon, k * lon : (k + 1) * lon] = value

        return put

    def edge_put(row, slot):
        def put(k, value):
            edge[row, k * lon : (k + 1) * lon, slot * lon : (slot + 1) * lon] = value

        return put

    for move in moves[:2]:
        move.wait()
    for row in range(rows):
        for step in range(REACH):
            block(row, step, ahead_put(row, step))
        for slot, (at, step) in enumerate(edge_taps(rows, row)):
            block(at, step, edge_put(row, slot))
    kernels, chan = held.shape[:2]
    padded = w_fwd.shape[0]
    for move in moves[2:]:
        move.wait()
    dec = padded_rows(dec_t, padded)

    w_fwd[:, :chan] = dec
    for k in range(kernels):
        w_fwd[:, (k + 1) * chan : (k + 2) * chan] = dot_nt(dec, held[k]).astype(BF)


def forward_own(rows, kernels, field, ahead, w_fwd, mixed, predicted):
    chan, lon = field.shape[1:]
    source = jnp.concatenate([field[i] for i in range(rows)], axis=1)
    for i in range(rows):
        mixed[i] = dot_nn(source, ahead[i, (HALO - i) * lon : (HALO - i + rows) * lon, :])
        predicted[i] = dot_nn(w_fwd[:, :chan], field[i])


def forward_rest(rows, kernels, cross, chip, begun, based, ahead, w_fwd, packed, predicted, mixed):
    chan, lon = cross.shape[1:]
    low, high = sides(odd_band(), cross, chip)
    outer = dict(enumerate(low, -HALO)) | dict(enumerate(high, rows))
    per = packed.shape[1]
    padded = predicted.shape[1]
    pieces = padded // per
    for i in range(rows):
        reach = [at for at in outer if 0 <= at - i + HALO < REACH]
        source = jnp.concatenate([outer[at] for at in reach], axis=1)
        steps = [at - i + HALO for at in reach]
        table = jnp.concatenate([ahead[i, step * lon : (step + 1) * lon, :] for step in steps], axis=0)
        taps = (begun[i] + dot_nn(source, table)).astype(BF)
        stack = [taps[:, k * lon : (k + 1) * lon] for k in range(kernels)]
        for k in range(kernels):
            mixed[i, k * chan : (k + 1) * chan, :] = stack[k]
        pred = based[i] + dot_nn(w_fwd[:, chan:], jnp.concatenate(stack, axis=0))
        predicted[i] = pred
        rounded = pred.astype(BF)
        for q in range(pieces):
            packed[i * pieces + q] = rounded[q * per : (q + 1) * per]
    for q in range(rows * pieces, packed.shape[0]):
        packed[q] = jnp.zeros(packed.shape[1:], BF)


def pairs(visitors, sums):
    members, height, _ = visitors.shape
    pieces = []
    for start in range(0, height, 8):
        values = [visitors[m].astype(F32)[start : start + 8] for m in range(members)]
        totals = [None] * members
        for m in range(members):
            for n in range(m + 1, members):
                slope = smooth_slope(values[m] - values[n])
                totals[m] = slope if totals[m] is None else totals[m] + slope
                totals[n] = -slope if totals[n] is None else totals[n] - slope
        pieces.append(totals)
    for m in range(members):
        sums[m] = jnp.concatenate([totals[m] for totals in pieces], axis=0).astype(BF)


def gradient(rows, kernels, members, area, sums, predicted, target, mixed, pred_grad, cross, chip, partial, buffer, sems):
    variables = target.shape[1]
    padded = predicted.shape[1]
    per = sums.shape[1]
    pieces = padded // per
    lon = predicted.shape[2]
    chan = mixed.shape[1] // kernels
    grads, edges = [], []
    odd = odd_band()
    band = lax.axis_index("lat")
    for i in range(rows):
        pair_sum = jnp.concatenate([sums[i * pieces + q].astype(F32) for q in range(pieces)], axis=0)
        aim = jnp.concatenate([target[i].astype(F32), jnp.zeros((padded - variables, lon), F32)], axis=0)
        grad = area[pl.ds(band * rows + i, 1), :] * (smooth_slope(predicted[i] - aim) - pair_sum * (1.0 / (members - 1)))
        grad = grad.astype(BF)
        pred_grad[i] = grad
        edges.append(grad)
        grads.append(jnp.concatenate([grad, jnp.zeros((lon - padded, lon), BF)], axis=0))
    for n in range(HALO):
        top, bottom = edges[rows - HALO + n], edges[n]
        cross[n] = jnp.where(odd, top, bottom)
        chip[n] = jnp.where(odd, bottom, top)
    total = dot_nt(
        jnp.concatenate([mixed[i] for i in range(rows)], axis=1), jnp.concatenate(grads, axis=1)
    )
    first, second, third = [total[k * chan : (k + 1) * chan] for k in range(kernels)]
    lane = lax.broadcasted_iota(jnp.int32, first.shape, 1)
    spare = lon - variables
    upper = jnp.where(lane < variables, first, pltpu.roll(third, variables, 1))
    tail = jnp.where(lane < 2 * variables - spare, pltpu.roll(third, variables - spare, 1), 0.0)
    lower = jnp.where(lane < variables, second, tail)
    owners = partial.shape[0]
    own = chan // owners
    groups = sems.shape[0]
    size = owners // groups
    moves = []
    for group in range(groups):
        for owner in range(group * size, (group + 1) * size):
            mine = slice(owner * own, (owner + 1) * own)
            buffer[owner] = jnp.concatenate([upper[mine], lower[mine]], axis=0).astype(BF)
        part = pl.ds(group * size, size)
        moves.append(pltpu.make_async_copy(buffer.at[part], partial.at[part], sems.at[group]))
        moves[-1].start()
    for move in moves:
        move.wait()


def band_sum(factor, variables, padded, parts, w_bwd, spread):
    owners, height, lon = parts.shape
    total = parts[0].astype(F32)
    for owner in range(1, owners):
        total = total + parts[owner].astype(F32)
    total = total * factor
    own = height // 2
    spare = lon - variables
    lane = lax.broadcasted_iota(jnp.int32, (own, lon), 1)
    front = pltpu.roll(total[:own], lon - variables, 1)
    rest = pltpu.roll(total[own:], lon + spare - variables, 1)
    third = jnp.where(lane < spare, front, jnp.where(lane < variables, rest, 0.0))
    wide = lax.broadcasted_iota(jnp.int32, total.shape, 1)
    total = jnp.where(wide < variables, total, 0.0)
    total = jnp.concatenate([total, third, jnp.zeros((lon - height - own, lon), F32)], axis=0)
    upper = total.astype(BF)
    lower = (total - upper.astype(F32)).astype(BF)
    dec = w_bwd[:, :padded]
    result = dot_nt(dec, upper[:, :padded]) + dot_nt(dec, lower[:, :padded])
    per = spread.shape[1]
    for member in range(spread.shape[0]):
        spread[member] = result[member * per : (member + 1) * per].astype(BF)


def member_sum(parts, owned):
    kernels, own, width = owned.shape
    total = parts[0].astype(F32)
    for member in range(1, parts.shape[0]):
        total = total + parts[member].astype(F32)
    turned = total.T
    for k in range(kernels):
        owned[k] = turned[k * own : (k + 1) * own, :width]


def adjoint_own(rows, kernels, pred_grad, ahead, held, w_fwd, turned, w_bwd):
    chan = held.shape[1]
    dec = w_fwd[:, :chan]
    square = (chan, chan)
    unit = lax.broadcasted_iota(jnp.int32, square, 0) == lax.broadcasted_iota(jnp.int32, square, 1)
    columns = [dot_nt(jnp.where(unit, 1.0, 0.0).astype(BF), dec)]
    columns = columns + [dot_nt(held[k], dec) for k in range(kernels)]
    w_bwd[...] = jnp.concatenate(columns, axis=1).astype(BF)
    lon = pred_grad.shape[2]
    for k in range(kernels):
        sums = [None] * rows
        for at in range(rows):
            least = HALO - at
            taps = ahead[at, least * lon : (least + rows) * lon, k * lon : (k + 1) * lon]
            found = dot_nt(pred_grad[at], taps)
            for row in range(rows):
                piece = found[:, row * lon : (row + 1) * lon]
                sums[row] = piece if sums[row] is None else sums[row] + piece
        for row in range(rows):
            turned[row, :, k * lon : (k + 1) * lon] = sums[row]


def adjoint_rest(rows, kernels, pred_grad, cross, chip, turned, edge, w_bwd, result, buffer, sems):
    lon = pred_grad.shape[2]
    low, high = sides(odd_band(), cross, chip)
    outer = dict(enumerate(low, -HALO)) | dict(enumerate(high, rows))
    moves = []
    for row in range(rows):
        sources = jnp.concatenate([outer[at] for at, _ in edge_taps(rows, row)], axis=1)
        taps = (turned[row] + dot_nt(sources, edge[row])).astype(BF)
        stack = [pred_grad[row]] + [taps[:, k * lon : (k + 1) * lon] for k in range(kernels)]
        buffer[row] = dot_nn(w_bwd[...], jnp.concatenate(stack, axis=0)).astype(BF)
        moves.append(pltpu.make_async_copy(buffer.at[row], result.at[row], sems.at[row]))
        moves[-1].start()
    for move in moves:
        move.wait()


def cut(field, cross, chip, sems):
    rows = field.shape[0]
    odd = lax.axis_index("lat") & 1
    far = (rows - HALO) * odd
    moves = [
        pltpu.make_async_copy(field.at[pl.ds(far, HALO)], cross, sems.at[0]),
        pltpu.make_async_copy(field.at[pl.ds(rows - HALO - far, HALO)], chip, sems.at[1]),
    ]
    for move in moves:
        move.start()
    for move in moves:
        move.wait()


def sides(odd, cross, chip):
    low = [jnp.where(odd, chip[n], cross[n]) for n in range(HALO)]
    high = [jnp.where(odd, cross[n], chip[n]) for n in range(HALO)]
    return low, high


def across(block, axis, start):
    count = lax.axis_size(axis)
    up = [(i, i + 1) for i in range(start, count - 1, 2)]
    return lax.ppermute(block, axis, up + [(b, a) for a, b in up])


def body(latent_fields, target_fields, filters, decoder, cycle_basis, cycle_offsets):
    field = latent_fields[0]
    rows, chan, lon = field.shape
    lat_count, kernels, taps = cycle_basis.shape
    variables = decoder.shape[1]
    members, bands = lax.axis_size("ens"), lax.axis_size("lat")
    per = 16
    padded = -(-variables // per) * per
    area = np.cos(np.pi * (np.arange(lat_count) + 0.5) / lat_count - np.pi / 2)
    area = jnp.asarray(np.broadcast_to(area[:, None], (lat_count, lon)), F32)
    dec_t = decoder.T
    basis = cycle_basis.transpose(2, 1, 0)
    offsets = cycle_offsets.T

    stay = functools.partial(pltpu.with_memory_space_constraint, memory_space=pltpu.HBM)
    hbm = pl.BlockSpec(memory_space=pltpu.HBM)
    edge = jax.ShapeDtypeStruct((HALO, chan, lon), BF)
    pair = pltpu.SemaphoreType.DMA((2,))
    cross, chip = call(cut, (edge, edge), [hbm], 0, 500_000, [pair])(stay(field))
    cross, chip = across(cross, "lat", 1), across(chip, "lat", 0)
    ahead, tap_edge, w_fwd, near, held = call(
        functools.partial(prepare, rows, lat_count),
        (
            jax.ShapeDtypeStruct((rows, REACH * lon, kernels * lon), BF),
            jax.ShapeDtypeStruct((rows, kernels * lon, (REACH - rows) * lon), BF),
            jax.ShapeDtypeStruct((padded, (kernels + 1) * chan), BF),
            jax.ShapeDtypeStruct(field.shape, BF),
            jax.ShapeDtypeStruct(filters.shape, BF),
        ),
        [hbm] * 5,
        30_000_000,
        2_000_000,
        [
            pltpu.VMEM(dec_t.shape, BF),
            pltpu.SMEM(basis.shape, F32),
            pltpu.SMEM(offsets.shape, jnp.int32),
            pltpu.SemaphoreType.DMA((5,)),
        ],
    )(stay(basis), stay(offsets), stay(filters), stay(dec_t), stay(field))
    begun, based = call(
        functools.partial(forward_own, rows, kernels),
        (jax.ShapeDtypeStruct((rows, chan, kernels * lon), F32), jax.ShapeDtypeStruct((rows, padded, lon), F32)),
        [VMEM] * 3,
        250_000_000,
        3_000_000,
    )(near, ahead, w_fwd)
    packed, predicted, mixed = call(
        functools.partial(forward_rest, rows, kernels),
        (
            jax.ShapeDtypeStruct((members, per, lon), BF),
            jax.ShapeDtypeStruct((rows, padded, lon), F32),
            jax.ShapeDtypeStruct((rows, kernels * chan, lon), BF),
        ),
        [VMEM] * 6,
        200_000_000,
        3_000_000,
    )(cross, chip, begun, based, ahead, w_fwd)
    visitors = lax.all_to_all(packed, "ens", 0, 0, tiled=True)
    sums = call(pairs, jax.ShapeDtypeStruct((members, per, lon), BF), [VMEM], 2_000_000, 200_000)(visitors)
    sums = lax.all_to_all(sums, "ens", 0, 0, tiled=True)
    own = chan // bands
    edge = jax.ShapeDtypeStruct((HALO, padded, lon), BF)
    pred_grad, cross, chip, partial = call(
        functools.partial(gradient, rows, kernels, members),
        (
            jax.ShapeDtypeStruct((rows, padded, lon), BF),
            edge,
            edge,
            jax.ShapeDtypeStruct((bands, 2 * own, lon), BF),
        ),
        [VMEM] * 5,
        80_000_000,
        1_200_000,
        [pltpu.VMEM((bands, 2 * own, lon), BF), pltpu.SemaphoreType.DMA((4,))],
        [VMEM, VMEM, VMEM, hbm],
    )(area, sums, predicted, target_fields, mixed)
    parts = lax.all_to_all(partial, "lat", 0, 0, tiled=True)
    cross, chip = across(cross, "lat", 1), across(chip, "lat", 0)
    turned, w_bwd = call(
        functools.partial(adjoint_own, rows, kernels),
        (
            jax.ShapeDtypeStruct((rows, padded, kernels * lon), F32),
            jax.ShapeDtypeStruct((chan, (kernels + 1) * padded), BF),
        ),
        [VMEM] * 4,
        120_000_000,
        2_000_000,
    )(pred_grad, ahead, held, w_fwd)
    latent_grad = call(
        functools.partial(adjoint_rest, rows, kernels),
        jax.ShapeDtypeStruct((rows, chan, lon), BF),
        [VMEM] * 6,
        150_000_000,
        1_500_000,
        [pltpu.VMEM((rows, chan, lon), BF), pltpu.SemaphoreType.DMA((rows,))],
        hbm,
    )(pred_grad, cross, chip, turned, tap_edge, w_bwd)
    parts, latent_grad = lax.optimization_barrier((parts, latent_grad))
    factor = 1.0 / math.sqrt(members * lat_count * lon)
    width = chan // members
    spread = call(
        functools.partial(band_sum, factor, variables, padded),
        jax.ShapeDtypeStruct((members, width, lon), BF),
        [VMEM] * 2,
        20_000_000,
        400_000,
    )(parts, w_bwd)
    spread = lax.all_to_all(spread, "ens", 0, 0, tiled=True)
    owned = call(
        member_sum, jax.ShapeDtypeStruct((kernels, own, width), F32), [VMEM], 100_000, 150_000
    )(spread)
    return latent_grad[None], owned.transpose(1, 0, 2)


def solution(mesh):
    placed = (P("ens", "lat", None, None), P("lat", None, None), P(), P(), P(), P())
    return jax.shard_map(
        body,
        mesh=mesh,
        in_specs=placed,
        out_specs=(P("ens", "lat", None, None), P("lat", None, "ens")),
        check_vma=False,
    )
```
